32 devices in a mesh: dp: 16 (over z, y, x), tensor: 2 (over core).
Axes of the slice: x: 2, y: 2, z: 4, core: 2. Of those that a mesh axis runs over, the one named last changes fastest.
Arguments:
- tokens: bfloat16 [16384, 768], P('dp'), may hold values from -6 to 6
- cotangent: bfloat16 [16384, 768], P('dp'), may hold values from -6 to 6
- lengths: int32 [32], P('dp'), may hold values from 113 to 512, as said below
- proj_weight: float32 [2, 768, 3, 768], P(None, 'dp', None, 'tensor'), may hold values from -0.21875 to 0.21875
- out_weight: float32 [2, 768, 768], P(None, 'dp', 'tensor'), may hold values from -0.875 to 0.875
- up_weight: float32 [2, 768, 3072], P(None, 'dp', 'tensor'), may hold values from -0.21875 to 0.21875
- down_weight: float32 [2, 768, 3072], P(None, 'dp', 'tensor'), may hold values from -0.109375 to 0.109375
- small_params: float32 [2, 8448], replicated, may hold values from -0.8 to 1.4
- proj_first: float32 [2, 768, 3, 768], P(None, 'dp', None, 'tensor'), may hold values from -0.00018310547 to 0.00018310547
- proj_second: float32 [2, 768, 3, 768], P(None, 'dp', None, 'tensor'), may hold values from 3.527916e-11 to 3.52791626e-09
- out_first: float32 [2, 768, 768], P(None, 'dp', 'tensor'), may hold values from -0.00018310547 to 0.00018310547
- out_second: float32 [2, 768, 768], P(None, 'dp', 'tensor'), may hold values from 7.0558325e-12 to 7.0558325e-10
- up_first: float32 [2, 768, 3072], P(None, 'dp', 'tensor'), may hold values from -0.00018310547 to 0.00018310547
- up_second: float32 [2, 768, 3072], P(None, 'dp', 'tensor'), may hold values from 3.527916e-11 to 3.52791626e-09
- down_first: float32 [2, 768, 3072], P(None, 'dp', 'tensor'), may hold values from -0.00018310547 to 0.00018310547
- down_second: float32 [2, 768, 3072], P(None, 'dp', 'tensor'), may hold values from 3.527916e-11 to 3.52791626e-09
- small_first: float32 [2, 8448], replicated, may hold values from -0.00018310547 to 0.00018310547
- small_second: float32 [2, 8448], replicated, may hold values from 3.527916e-11 to 5.644666e-10
Outputs:
- activations: float32 [16384, 768], P('dp')
- input_grad: float32 [16384, 768], P('dp')
- grad_norm: float32 [], replicated
- proj_first_new: float32 [2, 768, 3, 768], P(None, 'dp', None, 'tensor')
- proj_second_new: float32 [2, 768, 3, 768], P(None, 'dp', None, 'tensor')
- proj_weight_new: float32 [2, 768, 3, 768], P(None, 'dp', None, 'tensor')
- out_first_new: float32 [2, 768, 768], P(None, 'dp', 'tensor')
- out_second_new: float32 [2, 768, 768], P(None, 'dp', 'tensor')
- out_weight_new: float32 [2, 768, 768], P(None, 'dp', 'tensor')
- up_first_new: float32 [2, 768, 3072], P(None, 'dp', 'tensor')
- up_second_new: float32 [2, 768, 3072], P(None, 'dp', 'tensor')
- up_weight_new: float32 [2, 768, 3072], P(None, 'dp', 'tensor')
- down_first_new: float32 [2, 768, 3072], P(None, 'dp', 'tensor')
- down_second_new: float32 [2, 768, 3072], P(None, 'dp', 'tensor')
- down_weight_new: float32 [2, 768, 3072], P(None, 'dp', 'tensor')
- small_first_new: float32 [2, 8448], replicated
- small_second_new: float32 [2, 8448], replicated
- small_params_new: float32 [2, 8448], replicated
The draws below stay inside these ranges and needn't reach their ends.
Inputs may be any that keep to these rules, and one draw needn't show every extreme that they name: `lengths`: each length is 512, 256 or 128, reduced by less than max(1, 16); the first sequence has length 512.
All inputs are finite; a program needn't handle non-finite values.
Results may differ from the reference program's by a relative error of at most 0.03.
The reference program's roundings to bfloat16 on the way count: a program that leaves them out, or rounds other values in their place, can miss the bound.
Values may be sent and summed in bfloat16 or wider, within the bound.
No kernel may reach another device: no remote copies, remote signals or barrier semaphores. Data moves between devices by JAX's collectives and lax.ppermute only.
A program may use at most 192 MiB of HBM per device.

```python
import math
from functools import partial
import jax
import jax.numpy as jnp
from jax import lax

D = 768
HEADS = 12
FF = 3072
LAYERS = 2
LEN = 512
SEQS = 32
TOKENS = 16384
PARAMS = 14172672


def draw_lengths(key, part):
    bucket_key, trim_key = jax.random.split(jax.random.fold_in(key, 11))
    bucket = jax.random.randint(bucket_key, (SEQS,), 0, 3)
    trim_amount = jax.random.randint(trim_key, (SEQS,), 0, max(1, LEN // 32))
    seq_lengths = jnp.right_shift(jnp.full((SEQS,), LEN, jnp.int32), bucket.astype(jnp.int32)) - trim_amount.astype(jnp.int32)
    return seq_lengths.at[0].set(LEN).astype(jnp.int32)


def draw_small_params(key, part):
    width = 7 * D + FF
    base = jnp.clip(jax.random.normal(jax.random.fold_in(key, 23), (LAYERS, width), jnp.float32), -4.0, 4.0)
    column = jnp.arange(width)
    gains = (column >= 3 * D + FF) & (column < 4 * D + FF) | (column >= 5 * D + FF) & (column < 6 * D + FF)
    return jnp.where(gains[None, :], 1.0 + 0.1 * base, 0.2 * base).astype(jnp.float32)


def second_rows(key, salt, shape, level):
    lo_value = 0.0005 / PARAMS
    hi_value = 0.002 / PARAMS
    spread = jax.random.uniform(jax.random.fold_in(key, salt), shape, jnp.float32, jnp.log(lo_value), jnp.log(hi_value))
    rise_top = 9.0
    row_place = jnp.arange(D, dtype=jnp.float32) / max(1, D - 1)
    rise = jnp.exp(jnp.log(rise_top) * row_place).reshape((1, D) + (1,) * (len(shape) - 2))
    return (level * jnp.exp(spread) * rise).astype(jnp.float32)


def draw_proj_second(key, part):
    return second_rows(key, 31, (LAYERS, D, 3, D), 1.0)


def draw_out_second(key, part):
    return second_rows(key, 37, (LAYERS, D, D), 0.2)


def draw_up_second(key, part):
    return second_rows(key, 41, (LAYERS, D, FF), 1.0)


def draw_down_second(key, part):
    return second_rows(key, 43, (LAYERS, D, FF), 1.0)


def with_spikes(array, own_key, source, target, blocks, factor):
    owner, partner = [(jnp.arange(array.shape[position]) // (array.shape[position] // blocks)).reshape([-1 if axis == position else 1 for axis in range(array.ndim)]) for position in (source, target)]
    chosen = jax.random.permutation(own_key, blocks)[partner]
    strong = (owner == chosen) | (owner == (partner + blocks // 2) % blocks)
    return jnp.where(strong, factor * array, array)


def block_levels(rng, shape, shards, smallest, top_value):
    def one(dim, parts):
        heights = jax.random.uniform(jax.random.fold_in(jax.random.fold_in(rng, 6), dim), (parts,), jnp.float32, smallest / len(shards), top_value / len(shards))
        return jnp.repeat(jnp.exp(heights), shape[dim] // parts).reshape((-1,) + (1,) * (len(shape) - dim - 1))

    gain = one(*shards[0])
    for cut in shards[1:]:
        gain = gain * one(*cut)
    return gain


def noise(stream_key, extent, deviation, reach, shards=(), kind=jnp.bfloat16):
    values = deviation * jax.random.normal(stream_key, extent, jnp.float32)
    if shards:
        values = values * block_levels(stream_key, extent, shards, -0.22, 0.18)
    return jnp.clip(values, -reach, reach).astype(kind)


def bell_draw_with(rng, extent, scale, reach, pieces, heavy, kind=jnp.bfloat16):
    drawn = scale * jax.random.normal(rng, extent, jnp.float32)
    if pieces:
        drawn = drawn * block_levels(rng, extent, pieces, -0.22, 0.18)
    return jnp.clip(with_spikes(drawn, jax.random.fold_in(rng, 3), *heavy), -reach, reach).astype(kind)


def setup_inputs(seed: int = 0) -> dict:
    streams_of = jax.random.split(jax.random.key(seed), 19)
    tokens = bell_draw_with(streams_of[0], (TOKENS, D), 1.0, 6.0, ((0, 16),), (0, 1, 16, 2.0))
    cotangent = bell_draw_with(streams_of[1], (TOKENS, D), 1.0, 6.0, ((0, 16),), (0, 1, 16, 2.0))
    lengths = draw_lengths(jax.random.fold_in(streams_of[18], 71), 0)
    proj_weight = noise(streams_of[3], (LAYERS, D, 3, D), D ** -0.5, 0.21875, ((1, 16), (3, 2)), jnp.float32)
    out_weight = noise(streams_of[4], (LAYERS, D, D), (D // 16) ** -0.5, 0.875, ((1, 16), (2, 2)), jnp.float32)
    up_weight = noise(streams_of[5], (LAYERS, D, FF), D ** -0.5, 0.21875, ((1, 16), (2, 2)), jnp.float32)
    down_weight = noise(streams_of[6], (LAYERS, D, FF), FF ** -0.5, 0.109375, ((1, 16), (2, 2)), jnp.float32)
    small_params = draw_small_params(jax.random.fold_in(streams_of[18], 71), 0)
    proj_first = noise(streams_of[8], (LAYERS, D, 3, D), (0.11 * PARAMS ** -0.5), 0.00018310547, ((1, 16), (3, 2)), jnp.float32)
    proj_second = draw_proj_second(jax.random.fold_in(streams_of[18], 71), 0)
    out_first = noise(streams_of[10], (LAYERS, D, D), (0.11 * PARAMS ** -0.5), 0.00018310547, ((1, 16), (2, 2)), jnp.float32)
    out_second = draw_out_second(jax.random.fold_in(streams_of[18], 71), 0)
    up_first = noise(streams_of[12], (LAYERS, D, FF), (0.11 * PARAMS ** -0.5), 0.00018310547, ((1, 16), (2, 2)), jnp.float32)
    up_second = draw_up_second(jax.random.fold_in(streams_of[18], 71), 0)
    down_first = noise(streams_of[14], (LAYERS, D, FF), (0.11 * PARAMS ** -0.5), 0.00018310547, ((1, 16), (2, 2)), jnp.float32)
    down_second = draw_down_second(jax.random.fold_in(streams_of[18], 71), 0)
    small_first = noise(streams_of[16], (LAYERS, 7 * D + FF), (0.11 * PARAMS ** -0.5), 0.00018310547, (), jnp.float32)
    small_second = jnp.clip(jnp.exp(jax.random.uniform(streams_of[17], (LAYERS, 7 * D + FF), jnp.float32, math.log(3.5279161536561077e-11), math.log(5.644665845849772e-10))), 3.5279161536561077e-11, 5.644665845849772e-10)
    return {"tokens": tokens, "cotangent": cotangent, "lengths": lengths, "proj_weight": proj_weight, "out_weight": out_weight, "up_weight": up_weight, "down_weight": down_weight, "small_params": small_params, "proj_first": proj_first, "proj_second": proj_second, "out_first": out_first, "out_second": out_second, "up_first": up_first, "up_second": up_second, "down_first": down_first, "down_second": down_second, "small_first": small_first, "small_second": small_second}


@jax.custom_vjp
def low(v):
    return lax.optimization_barrier(v.astype(jnp.bfloat16)).astype(jnp.float32)

@jax.custom_vjp
def low_back(v):
    return v

def low_keep(v):
    return (low(v), None)

def low_pass(kept, grad):
    return (grad,)

def back_keep(v):
    return (v, None)

def back_low(kept, grad):
    return (low(grad),)
low.defvjp(low_keep, low_pass)
low_back.defvjp(back_keep, back_low)
highest = lax.Precision.HIGHEST
beta_one = 0.9
beta_two = 0.999
adam_eps = 1e-06
decay_rate = 0.01
matrix_rate = 1.0
vector_rate = 0.3
clip_norm = 1.0
step_count = 10.0
norm_eps = 1e-06
masked_score = -1e+30

def layer_norm(values, norm_gain, norm_shift):
    average = lax.optimization_barrier(jnp.mean(values, axis=-1, keepdims=True))
    centered = values - average
    variance = lax.optimization_barrier(jnp.mean(centered * centered, axis=-1, keepdims=True))
    return centered * lax.rsqrt(variance + norm_eps) * norm_gain + norm_shift

def split_vector(packed):
    bounds = [0, D, 2 * D, 2 * D + FF, 3 * D + FF, 4 * D + FF, 5 * D + FF, 6 * D + FF, 7 * D + FF]
    return [packed[bounds[place]:bounds[place + 1]] for place in range(8)]

def group_forward(weights, inputs, seq_lengths):
    proj_low, out_low, up_low, down_low, small = weights
    count = inputs.shape[0]
    head_dim = D // HEADS
    score_scale = 1.0 / math.sqrt(head_dim)
    key_valid = jnp.arange(LEN)[None, :] < seq_lengths[:, None]
    hidden = inputs
    earlier = None
    for layer_at in range(LAYERS):
        bias_v, bias_o, bias_up, bias_down, gain_one, shift_one, gain_two, shift_two = split_vector(small[layer_at])
        projected = jnp.einsum('gtd,dcf->gtcf', low(hidden), proj_low[layer_at], precision=highest)
        query = low(low_back(projected[:, :, 0])).reshape(count, LEN, HEADS, head_dim)
        keys = low(low_back(projected[:, :, 1])).reshape(count, LEN, HEADS, head_dim)
        value_rows = low(low_back(projected[:, :, 2]) + bias_v).reshape(count, LEN, HEADS, head_dim)
        raw = low_back(jnp.einsum('gqhe,gkhe->ghqk', query, keys, precision=highest) * score_scale)
        score_total = raw if earlier is None else raw + earlier
        earlier = score_total
        masked = jnp.where(key_valid[:, None, None, :], score_total, masked_score)
        soft = jax.nn.softmax(masked, axis=-1)
        context = jnp.einsum('ghqk,gkhe->gqhe', low(soft), value_rows, precision=highest).reshape(count, LEN, D)
        context = low(low_back(context))
        attended = low_back(jnp.einsum('gtf,df->gtd', context, out_low[layer_at], precision=highest))
        first_out = layer_norm(hidden + attended + bias_o, gain_one, shift_one)
        before_act = low_back(jnp.einsum('gtd,df->gtf', low(first_out), up_low[layer_at], precision=highest)) + bias_up
        activated = low(jax.nn.gelu(before_act, approximate=False))
        returned = low_back(jnp.einsum('gtf,df->gtd', activated, down_low[layer_at], precision=highest))
        hidden = layer_norm(first_out + returned + bias_down, gain_two, shift_two)
    return hidden

def adam_parts(gradient, first, second, factor):
    clipped = gradient * factor
    first_new = beta_one * first + (1.0 - beta_one) * clipped
    second_new = beta_two * second + (1.0 - beta_two) * clipped * clipped
    first_hat = first_new / (1.0 - beta_one ** step_count)
    second_hat = second_new / (1.0 - beta_two ** step_count)
    return (first_new, second_new, first_hat / (jnp.sqrt(second_hat) + adam_eps))

def matrix_update(weight, gradient, first, second, factor):
    first_new, second_new, direction = adam_parts(gradient, first, second, factor)
    update = direction + decay_rate * weight
    axes_rest = tuple(range(1, weight.ndim))
    weight_norm = jnp.sqrt(lax.optimization_barrier(jnp.sum(weight * weight, axis=axes_rest, keepdims=True)))
    update_norm = jnp.sqrt(lax.optimization_barrier(jnp.sum(update * update, axis=axes_rest, keepdims=True)))
    return (first_new, second_new, weight - matrix_rate * (weight_norm / update_norm) * update)

def reference(tokens, cotangent, lengths, proj_weight, out_weight, up_weight, down_weight, small_params, proj_first, proj_second, out_first, out_second, up_first, up_second, down_first, down_second, small_first, small_second):
    seqs_all = lengths.shape[0]
    group = math.gcd(seqs_all, max(1, 4096 // LEN))
    inputs = tokens.astype(jnp.float32).reshape(seqs_all // group, group, LEN, D)
    grouped_lengths = lengths.reshape(seqs_all // group, group)
    row_valid = (jnp.arange(LEN)[None, :] < lengths[:, None]).reshape(seqs_all // group, group, LEN, 1)
    seed_grad = jnp.where(row_valid, cotangent.astype(jnp.float32).reshape(inputs.shape), 0.0)

    def whole(inputs_all, proj_master, out_master, up_master, down_master, small):
        weights = (low(proj_master), low(out_master), low(up_master), low(down_master), small)
        step_fn = jax.checkpoint(partial(group_forward, weights))
        return lax.map(lambda block_item: step_fn(block_item[0], block_item[1]), (inputs_all, grouped_lengths))
    outputs, pullback = jax.vjp(whole, inputs, proj_weight, out_weight, up_weight, down_weight, small_params)
    input_grad, proj_grad, out_grad, up_grad, down_grad, small_grad = pullback(seed_grad)
    square_total = jnp.sum(small_grad * small_grad)
    for gradient in (proj_grad, out_grad, up_grad, down_grad):
        square_total = square_total + jnp.sum(gradient * gradient)
    grad_norm = jnp.sqrt(square_total)
    factor = clip_norm / jnp.maximum(grad_norm, clip_norm)
    proj_new = matrix_update(proj_weight, proj_grad, proj_first, proj_second, factor)
    out_new = matrix_update(out_weight, out_grad, out_first, out_second, factor)
    up_new = matrix_update(up_weight, up_grad, up_first, up_second, factor)
    down_new = matrix_update(down_weight, down_grad, down_first, down_second, factor)
    small_first_new, small_second_new, small_direction = adam_parts(small_grad, small_first, small_second, factor)
    small_params_new = small_params - vector_rate * small_direction
    return (outputs.reshape(-1, D), input_grad.reshape(-1, D), grad_norm, proj_new[0], proj_new[1], proj_new[2], out_new[0], out_new[1], out_new[2], up_new[0], up_new[1], up_new[2], down_new[0], down_new[1], down_new[2], small_first_new, small_second_new, small_params_new)
```

```python
from functools import partial
import math

import jax
import jax.numpy as jnp
import numpy as np
from jax import lax
from jax.experimental import pallas as pl
from jax.experimental.pallas import tpu as pltpu
from jax.sharding import PartitionSpec as P

D = 768
HEADS = 12
FF = 3072


beta_one = 0.9
beta_two = 0.999
adam_eps = 1e-06
decay_rate = 0.01
matrix_rate = 1.0
vector_rate = 0.3
clip_norm = 1.0
step_count = 10.0
norm_eps = 1e-06
masked_score = -1e30

f32 = jnp.float32
bf16 = jnp.bfloat16


def layer_norm(values, norm_gain, norm_shift):
    average = jnp.mean(values, axis=-1, keepdims=True)
    centered = values - average
    variance = jnp.mean(centered * centered, axis=-1, keepdims=True)
    return centered * lax.rsqrt(variance + norm_eps) * norm_gain + norm_shift


def split_vector(packed):
    bounds = [0, D, 2 * D, 2 * D + FF, 3 * D + FF, 4 * D + FF, 5 * D + FF, 6 * D + FF, 7 * D + FF]
    return [packed[bounds[place] : bounds[place + 1]] for place in range(8)]


class Links:
    def __init__(self, parts):
        self.parts = parts
        count = parts.bit_length() - 1
        high = list(range(count - 1, -1, -1))
        other = high[:-2] + high[-2:][::-1]
        self.orders = (other, high)
        self.masks = np.zeros((2, parts), np.int32)
        self.inverse = np.zeros((2, parts), np.int32)
        for core in range(2):
            for place in range(parts):
                mask = 0
                for stage in range(count):
                    if (place >> stage) & 1:
                        mask |= 1 << self.orders[core][stage]
                self.masks[core, place] = mask
                self.inverse[core, mask] = place
        self.stages = count

    def swap(self, value, stage):
        pairs = []
        for core in range(2):
            flip = 1 << self.orders[core][stage]
            pairs += [(2 * at + core, 2 * (at ^ flip) + core) for at in range(self.parts)]
        return lax.ppermute(value, ("dp", "tensor"), pairs)

    def sibling(self, value):
        return lax.ppermute(value, "tensor", [(0, 1), (1, 0)])

    def gather(self, share):
        held = share[None]
        for stage in range(self.stages):
            held = jnp.concatenate([held, self.swap(held, stage)], axis=0)
        return held

    def scatter(self, own, other):
        pieces = [own, self.sibling(other)]
        size = self.parts
        for stage in reversed(range(self.stages)):
            half = size // 2
            total = sum(piece[half:size].astype(f32) for piece in pieces).astype(bf16)
            pieces = [piece[:half] for piece in pieces]
            pieces.append(self.swap(total, stage))
            size = half
        return sum(piece[0].astype(f32) for piece in pieces)

    def total(self, value):
        value = value + self.sibling(value)
        for stage in range(self.stages):
            value = value + self.swap(value, stage)
        return value


def assemble_kernel(own_at, other_at, own, other, *outs, widths):
    start = 0
    for out, parts in zip(outs, widths):
        place = 0
        for width in parts:
            out[0, :, place : place + width] = own[0, :, start : start + width]
            out[0, :, place + width : place + 2 * width] = other[0, :, start : start + width]
            place += 2 * width
            start += width


def assemble(own_at, other_at, own, other, widths):
    parts, rows, cols = own.shape
    return pl.pallas_call(
        partial(assemble_kernel, widths=widths),
        out_shape=[jax.ShapeDtypeStruct((parts, rows, 2 * sum(w)), own.dtype) for w in widths],
        grid_spec=pltpu.PrefetchScalarGridSpec(
            num_scalar_prefetch=2,
            grid=(parts,),
            in_specs=[
                pl.BlockSpec((1, rows, cols), lambda i, a, b: (a[i], 0, 0)),
                pl.BlockSpec((1, rows, cols), lambda i, a, b: (b[i], 0, 0)),
            ],
            out_specs=[pl.BlockSpec((1, rows, 2 * sum(w)), lambda i, a, b: (i, 0, 0)) for w in widths],
        ),
        compiler_params=pltpu.CompilerParams(dimension_semantics=("arbitrary",)),
        name="assemble",
    )(own_at, other_at, own, other)


def outer_kernel(own_at, other_at, *refs, counts, parts, rows):
    sources = len(counts)
    own, other, turned = refs[3 * sources :]
    step = pl.program_id(0)
    start = 0
    for source, count in enumerate(counts):
        left, right_own, right_other = refs[3 * source : 3 * source + 3]

        @pl.when(step == start)
        def _():
            turned[...] = left[...].T

        @pl.when((step >= start) & (step < start + count))
        def _():
            for right, place_of, out in ((right_own, own_at, own), (right_other, other_at, other)):
                product = jnp.dot(turned[...], right[...], preferred_element_type=f32).astype(bf16)
                for block in range(parts):
                    out[place_of[block]] = product[block * rows : (block + 1) * rows]

        start += count


def outer(own_at, other_at, sources, width):
    parts = own_at.shape[0]
    rows = D // parts
    counts = [sum(spans) // width for _, _, spans in sources]
    in_specs, args = [], []
    start = 0
    for (left, right, spans), count in zip(sources, counts):
        per_span = spans[0] // width

        def column(step, half, start=start, count=count, per_span=per_span):
            at = jnp.clip(step - start, 0, count - 1)
            return (at // per_span) * (2 * per_span) + half * per_span + at % per_span

        in_specs.append(pl.BlockSpec(left.shape, lambda i, a, b: (0, 0)))
        for half in range(2):
            in_specs.append(
                pl.BlockSpec(
                    (right.shape[0], width), lambda i, a, b, half=half, column=column: (0, column(i, half))
                )
            )
        args += [left, right, right]
        start += count
    out_spec = pl.BlockSpec((parts, rows, width), lambda i, a, b: (0, 0, i))
    out_shape = jax.ShapeDtypeStruct((parts, rows, start * width), bf16)
    return pl.pallas_call(
        partial(outer_kernel, counts=counts, parts=parts, rows=rows),
        out_shape=[out_shape, out_shape],
        grid_spec=pltpu.PrefetchScalarGridSpec(
            num_scalar_prefetch=2,
            grid=(start,),
            in_specs=in_specs,
            out_specs=[out_spec, out_spec],
            scratch_shapes=[pltpu.VMEM((D, sources[0][0].shape[0]), bf16)],
        ),
        compiler_params=pltpu.CompilerParams(
            dimension_semantics=("arbitrary",), vmem_limit_bytes=48 << 20
        ),
        name="outer",
    )(own_at, other_at, *args)


def head_scores(query, keys, score_scale):
    return jnp.einsum("qhe,khe->hqk", query, keys, preferred_element_type=jnp.float32) * score_scale


def total_scores(pairs, score_scale):
    score_total = head_scores(pairs[0], pairs[1], score_scale)
    for place in range(2, len(pairs), 2):
        score_total = score_total + head_scores(pairs[place], pairs[place + 1], score_scale)
    return score_total


def attend_forward(key_valid, value_rows, pairs, score_scale):
    score_total = total_scores(pairs, score_scale)
    masked = jnp.where(key_valid[None, None, :], score_total, masked_score)
    row_max = jnp.max(masked, axis=-1, keepdims=True)
    exp_terms = jnp.exp(masked - row_max)
    row_sum = jnp.sum(exp_terms, axis=-1, keepdims=True)
    soft_low = (exp_terms / row_sum).astype(jnp.bfloat16)
    context = jnp.einsum("hqk,khe->qhe", soft_low, value_rows, preferred_element_type=jnp.float32)
    return (context.astype(jnp.bfloat16), (row_max + jnp.log(row_sum))[..., 0])


def attend_backward(key_valid, value_rows, log_norm, context_grad, later, pairs, score_scale):
    score_total = total_scores(pairs, score_scale)
    soft = jnp.where(key_valid[None, None, :], jnp.exp(score_total - log_norm[..., None]), 0.0)
    soft_grad = jnp.einsum(
        "qhe,khe->hqk", context_grad, value_rows, preferred_element_type=jnp.float32
    )
    total_grad = soft * (soft_grad - jnp.sum(soft * soft_grad, axis=-1, keepdims=True))
    if later is not None:
        total_grad = total_grad + later
    total_low = total_grad.astype(jnp.bfloat16)
    query_grad = (
        jnp.einsum("hqk,khe->qhe", total_low, pairs[1], preferred_element_type=jnp.float32)
        * score_scale
    )
    key_grad = (
        jnp.einsum("hqk,qhe->khe", total_low, pairs[0], preferred_element_type=jnp.float32)
        * score_scale
    )
    value_grad = jnp.einsum(
        "hqk,qhe->khe", soft.astype(jnp.bfloat16), context_grad, preferred_element_type=jnp.float32
    )
    return (query_grad, key_grad, value_grad, total_grad)


def adam_parts(gradient, first, second, factor):
    clipped = gradient * factor
    first_new = beta_one * first + (1.0 - beta_one) * clipped
    second_new = beta_two * second + (1.0 - beta_two) * clipped * clipped
    first_hat = first_new / (1.0 - beta_one**step_count)
    second_hat = second_new / (1.0 - beta_two**step_count)
    return (first_new, second_new, first_hat / (jnp.sqrt(second_hat) + adam_eps))


def local(
    tokens,
    cotangent,
    lengths,
    proj_weight,
    out_weight,
    up_weight,
    down_weight,
    small_params,
    proj_first,
    proj_second,
    out_first,
    out_second,
    up_first,
    up_second,
    down_first,
    down_second,
    small_first,
    small_second,
):
    layers = proj_weight.shape[0]
    seq_here = lengths.shape[0] // 2
    seq_len = tokens.shape[0] // lengths.shape[0]
    rows_here = seq_here * seq_len
    head_dim = D // HEADS
    half_d = proj_weight.shape[3]
    half_ff = up_weight.shape[2]
    row_count = proj_weight.shape[1]
    score_scale = 1.0 / math.sqrt(head_dim)
    core = lax.axis_index("tensor")
    parts = lax.axis_size("dp")
    links = Links(parts)
    at = lax.axis_index("dp")
    inverse = jnp.asarray(links.inverse)
    order = jnp.arange(parts, dtype=jnp.int32) ^ at
    own_at = inverse[core][order]
    other_at = inverse[1 - core][order]

    def shares_of(layer_at, kinds):
        table = {"proj": proj_weight, "out": out_weight, "up": up_weight, "down": down_weight}
        return jnp.concatenate(
            [table[kind][layer_at].reshape(row_count, -1).astype(bf16) for kind in kinds], axis=1
        )

    spans = {"proj": (half_d,) * 3, "out": (half_d,), "up": (half_ff,), "down": (half_ff,)}
    full = [dict() for _ in range(layers)]
    for layer_at in range(layers):
        groups = [("proj",), ("out", "up", "down")]
        for kinds in groups:
            held = links.gather(shares_of(layer_at, kinds))
            swapped = links.sibling(held)
            ready = assemble(own_at, other_at, held, swapped, [spans[kind] for kind in kinds])
            for kind, weight in zip(kinds, ready):
                full[layer_at][kind] = weight.reshape(D, -1)

    def own_first(vector):
        half = vector.shape[0] // 2
        return jnp.where(core == 0, vector, jnp.concatenate([vector[half:], vector[:half]]))

    tokens = lax.dynamic_slice_in_dim(tokens, core * rows_here, rows_here)
    cotangent = lax.dynamic_slice_in_dim(cotangent, core * rows_here, rows_here)
    lengths = lax.dynamic_slice_in_dim(lengths, core * seq_here, seq_here)
    positions = jnp.arange(seq_len)
    key_valid = positions[None, :] < lengths[:, None]
    row_valid = key_valid.reshape(-1, 1)

    def heads_view(rows):
        return rows.reshape(seq_here, seq_len, HEADS, head_dim)

    hidden = tokens.astype(jnp.float32)
    saved = []
    for layer_at in range(layers):
        bias_v, bias_o, bias_up, bias_down, gain_one, shift_one, gain_two, shift_two = split_vector(
            small_params[layer_at]
        )
        weights = full[layer_at]
        input_low = hidden.astype(jnp.bfloat16)
        projected = jnp.einsum("td,df->tf", input_low, weights["proj"], preferred_element_type=f32)
        query_low = projected[:, :D].astype(jnp.bfloat16)
        key_low = projected[:, D : 2 * D].astype(jnp.bfloat16)
        value_low = (projected[:, 2 * D :] + own_first(bias_v)).astype(jnp.bfloat16)
        pairs = [heads_view(query_low), heads_view(key_low)]
        for earlier in reversed(saved):
            pairs += [heads_view(earlier["query"]), heads_view(earlier["keys"])]
        context_low, log_norm = jax.vmap(partial(attend_forward, score_scale=score_scale))(
            key_valid, heads_view(value_low), pairs
        )
        context_low = context_low.reshape(-1, D)
        attended = jnp.einsum("tf,df->td", context_low, weights["out"], preferred_element_type=f32)
        first_in = hidden + attended + bias_o
        first_out = layer_norm(first_in, gain_one, shift_one)
        first_low = first_out.astype(jnp.bfloat16)
        before_act = jnp.einsum(
            "td,df->tf", first_low, weights["up"], preferred_element_type=f32
        ) + own_first(bias_up)
        act_low = jax.nn.gelu(before_act, approximate=False).astype(jnp.bfloat16)
        returned = jnp.einsum("tf,df->td", act_low, weights["down"], preferred_element_type=f32)
        second_in = first_out + returned + bias_down
        saved.append(
            {
                "layer_input": input_low,
                "query": query_low,
                "keys": key_low,
                "value_rows": value_low,
                "log_norm": log_norm,
                "context": context_low,
                "first_in": first_in,
                "first_low": first_low,
                "before_act": before_act,
                "act_low": act_low,
                "second_in": second_in,
            }
        )
        hidden = layer_norm(second_in, gain_two, shift_two)

    grad_rows = jnp.where(row_valid, cotangent.astype(jnp.float32), 0.0)
    shares = [None] * layers
    small_grads = [None] * layers
    later_total = None
    for layer_at in reversed(range(layers)):
        kept = saved[layer_at]
        weights = full[layer_at]
        bias_v, bias_o, bias_up, bias_down, gain_one, shift_one, gain_two, shift_two = split_vector(
            small_params[layer_at]
        )
        second_in_grad, gain_two_grad, shift_two_grad = jax.vjp(
            layer_norm, kept["second_in"], gain_two, shift_two
        )[1](grad_rows)
        down_in_low = second_in_grad.astype(jnp.bfloat16)
        act_grad = jnp.einsum("td,df->tf", down_in_low, weights["down"], preferred_element_type=f32)
        before_grad = jax.vjp(partial(jax.nn.gelu, approximate=False), kept["before_act"])[1](
            act_grad
        )[0]
        before_low = before_grad.astype(jnp.bfloat16)
        ff_share = links.scatter(
            *outer(
                own_at,
                other_at,
                [
                    (down_in_low, kept["act_low"], spans["down"]),
                    (kept["first_low"], before_low, spans["up"]),
                ],
                half_d,
            )
        )
        first_back = jnp.einsum("tf,df->td", before_low, weights["up"], preferred_element_type=f32)
        first_out_grad = second_in_grad + first_back
        first_in_grad, gain_one_grad, shift_one_grad = jax.vjp(
            layer_norm, kept["first_in"], gain_one, shift_one
        )[1](first_out_grad)
        out_in_low = first_in_grad.astype(jnp.bfloat16)
        context_grad = jnp.einsum(
            "td,df->tf", out_in_low, weights["out"], preferred_element_type=f32
        ).astype(jnp.bfloat16)
        pairs = [heads_view(kept["query"]), heads_view(kept["keys"])]
        for earlier in reversed(saved[:layer_at]):
            pairs += [heads_view(earlier["query"]), heads_view(earlier["keys"])]
        query_grad, key_grad, value_grad, later_total = jax.vmap(
            partial(attend_backward, score_scale=score_scale)
        )(
            key_valid,
            heads_view(kept["value_rows"]),
            kept["log_norm"],
            heads_view(context_grad),
            later_total,
            pairs,
        )
        value_grad = value_grad.reshape(-1, D)
        proj_grad_low = jnp.concatenate(
            [query_grad.reshape(-1, D), key_grad.reshape(-1, D), value_grad], axis=1
        ).astype(jnp.bfloat16)
        attention_share = links.scatter(
            *outer(
                own_at,
                other_at,
                [
                    (out_in_low, kept["context"], spans["out"]),
                    (kept["layer_input"], proj_grad_low, spans["proj"]),
                ],
                half_d,
            )
        )
        input_back = jnp.einsum(
            "tf,df->td", proj_grad_low, weights["proj"], preferred_element_type=f32
        )
        grad_rows = first_in_grad + input_back
        shares[layer_at] = (
            attention_share[:, half_d:],
            attention_share[:, :half_d],
            ff_share[:, half_ff:],
            ff_share[:, :half_ff],
        )
        small_grads[layer_at] = jnp.concatenate(
            [
                own_first(jnp.sum(value_grad, axis=0)),
                jnp.sum(first_in_grad, axis=0),
                own_first(jnp.sum(before_grad, axis=0)),
                jnp.sum(second_in_grad, axis=0),
                gain_one_grad,
                shift_one_grad,
                gain_two_grad,
                shift_two_grad,
            ]
        )

    masters = (proj_weight, out_weight, up_weight, down_weight)
    firsts = (proj_first, out_first, up_first, down_first)
    seconds = (proj_second, out_second, up_second, down_second)
    grads = [
        jnp.stack([shares[layer_at][kind_at] for layer_at in range(layers)]).reshape(
            masters[kind_at].shape
        )
        for kind_at in range(4)
    ]
    weight_square = jnp.stack(
        [jnp.sum(master * master, axis=tuple(range(1, master.ndim))) for master in masters]
    )
    small_size = small_params.size
    first_pack = jnp.concatenate(
        [
            jnp.stack(small_grads).reshape(-1),
            jnp.pad(weight_square.reshape(-1), (0, 128 - 4 * layers)),
        ]
    ).reshape(-1, 128)
    first_pack = links.total(first_pack).reshape(-1)
    small_grad = first_pack[:small_size].reshape(small_params.shape)
    weight_square = first_pack[small_size : small_size + 4 * layers].reshape(4, layers)

    square_part = sum(jnp.sum(grad * grad) for grad in grads)
    square_big = links.total(jnp.broadcast_to(square_part, (8, 128)))[0, 0]
    grad_norm = jnp.sqrt(square_big + jnp.sum(small_grad * small_grad))
    factor = clip_norm / jnp.maximum(grad_norm, clip_norm)
    moments = []
    updates = []
    for kind_at in range(4):
        first_new, second_new, direction = adam_parts(
            grads[kind_at], firsts[kind_at], seconds[kind_at], factor
        )
        moments.append((first_new, second_new))
        updates.append(direction + decay_rate * masters[kind_at])
    update_square = jnp.stack(
        [jnp.sum(update * update, axis=tuple(range(1, update.ndim))) for update in updates]
    )
    update_square = links.total(jnp.pad(update_square.reshape(1, -1), ((0, 7), (0, 128 - 4 * layers))))
    update_square = update_square[0, : 4 * layers].reshape(4, layers)
    ratio = jnp.sqrt(weight_square) / jnp.sqrt(update_square)

    def whole_rows(rows):
        other = links.sibling(rows)
        return jnp.where(
            core == 0, jnp.concatenate([rows, other]), jnp.concatenate([other, rows])
        )

    outputs = [whole_rows(hidden), whole_rows(grad_rows), grad_norm]
    for kind_at in range(4):
        master = masters[kind_at]
        scaled = ratio[kind_at].reshape((-1,) + (1,) * (master.ndim - 1))
        outputs += [
            moments[kind_at][0],
            moments[kind_at][1],
            master - matrix_rate * scaled * updates[kind_at],
        ]
    small_first_new, small_second_new, small_direction = adam_parts(
        small_grad, small_first, small_second, factor
    )
    outputs += [small_first_new, small_second_new, small_params - vector_rate * small_direction]
    return tuple(outputs)


def solution(mesh):
    proj = P(None, "dp", None, "tensor")
    matrix = P(None, "dp", "tensor")
    rows = P("dp", None)
    return jax.shard_map(
        local,
        mesh=mesh,
        in_specs=(rows, rows, P("dp"), proj, matrix, matrix, matrix, P())
        + (proj, proj)
        + (matrix,) * 6
        + (P(), P()),
        out_specs=(rows, rows, P()) + (proj,) * 3 + (matrix,) * 9 + (P(),) * 3,
        check_vma=False,
    )
```

```python
from functools import partial
import math

import jax
import jax.numpy as jnp
import numpy as np
from jax import lax
from jax.experimental import pallas as pl
from jax.experimental.pallas import tpu as pltpu
from jax.sharding import PartitionSpec as P

D = 768
HEADS = 12
FF = 3072


beta_one = 0.9
beta_two = 0.999
adam_eps = 1e-06
decay_rate = 0.01
matrix_rate = 1.0
vector_rate = 0.3
clip_norm = 1.0
step_count = 10.0
norm_eps = 1e-06
masked_score = -1e30

f32 = jnp.float32
bf16 = jnp.bfloat16


def layer_norm(values, norm_gain, norm_shift):
    average = jnp.mean(values, axis=-1, keepdims=True)
    centered = values - average
    variance = jnp.mean(centered * centered, axis=-1, keepdims=True)
    return centered * lax.rsqrt(variance + norm_eps) * norm_gain + norm_shift


def split_vector(packed):
    bounds = [0, D, 2 * D, 2 * D + FF, 3 * D + FF, 4 * D + FF, 5 * D + FF, 6 * D + FF, 7 * D + FF]
    return [packed[bounds[place] : bounds[place + 1]] for place in range(8)]


class Links:
    def __init__(self, parts):
        self.parts = parts
        count = parts.bit_length() - 1
        high = list(range(count - 1, -1, -1))
        other = high[:-2] + high[-2:][::-1]
        self.orders = (other, high)
        self.masks = np.zeros((2, parts), np.int32)
        self.inverse = np.zeros((2, parts), np.int32)
        for core in range(2):
            for place in range(parts):
                mask = 0
                for stage in range(count):
                    if (place >> stage) & 1:
                        mask |= 1 << self.orders[core][stage]
                self.masks[core, place] = mask
                self.inverse[core, mask] = place
        self.stages = count
        self.last = ()

    def swap(self, value, stage):
        pairs = []
        for core in range(2):
            flip = 1 << self.orders[core][stage]
            pairs += [(2 * at + core, 2 * (at ^ flip) + core) for at in range(self.parts)]
        return lax.ppermute(value, ("dp", "tensor"), pairs)

    def sibling(self, value):
        return lax.ppermute(value, "tensor", [(0, 1), (1, 0)])

    def gather(self, share):
        return {"held": share[None], "stage": 0}

    def scatter(self, own, other):
        return {"pieces": [own], "other": other, "size": self.parts, "stage": self.stages}

    def advance(self, moves, rest=()):
        moves = [move for move in moves if self.running(move)]
        if not moves:
            return rest
        mine, rest, self.last = lax.optimization_barrier(
            ([move.get("held", move.get("pieces")) for move in moves], rest, self.last)
        )
        sending = []
        for move, value in zip(moves, mine):
            if "held" in move:
                come = move.pop("come", None)
                sending.append(value if come is None else jnp.concatenate([value, come], axis=0))
            elif "other" in move:
                sending.append(move["other"])
            else:
                half, size = move["size"] // 2, move["size"]
                move["pieces"] = value + move.pop("come")
                sending.append(sum(piece[half:size].astype(f32) for piece in move["pieces"]).astype(bf16))
        sending, rest, _ = lax.optimization_barrier((sending, rest, self.last))
        self.last = sending[0]
        for move, value in zip(moves, sending):
            if "held" in move:
                if move["stage"] < self.stages:
                    move["held"] = value
                    move["come"] = self.swap(value, move["stage"])
                else:
                    move["pair"] = (value, self.sibling(value), 0)
                    del move["held"]
                move["stage"] += 1
            elif "other" in move:
                move["come"] = [self.sibling(value)]
                del move["other"]
            else:
                move["size"] //= 2
                move["stage"] -= 1
                move["come"] = [self.swap(value, move["stage"])]
        return rest

    def running(self, move):
        return "held" in move or move.get("size", 1) > 1

    def finish(self, moves):
        for move in moves:
            while self.running(move):
                self.advance([move])
        return [sum(piece[0].astype(f32) for piece in move["pieces"] + move["come"]) for move in moves]

    def total(self, value):
        value = value + self.sibling(value)
        for stage in range(self.stages):
            value = value + self.swap(value, stage)
        return value


def dot_nt(left, right):
    return lax.dot_general(left, right, (((1,), (1,)), ((), ())), preferred_element_type=f32)


def dot_nn(left, right):
    return jnp.dot(left, right, preferred_element_type=f32)


def in_order(blocks, place_of):
    some = (0,) if len(blocks.shape) == 4 else ()
    return jnp.concatenate([blocks[(place_of[block], *some)] for block in range(blocks.shape[0])], axis=0)


def put_blocks(out, at, product, place_of):
    parts, _, rows, _ = out.shape
    for block in range(parts):
        out[place_of[block], at] = product[block * rows : (block + 1) * rows]


def norm_parts(values):
    centered = values - jnp.mean(values, axis=1, keepdims=True)
    variance = jnp.mean(centered * centered, axis=1, keepdims=True)
    scale = lax.rsqrt(variance + norm_eps)
    return centered * scale, scale


def norm_backward(values, gain, grad):
    unit, scale = norm_parts(values)
    scaled = grad * gain
    inner = scaled - jnp.mean(scaled, axis=1, keepdims=True)
    result = scale * (inner - unit * jnp.mean(scaled * unit, axis=1, keepdims=True))
    return result, jnp.sum(grad * unit, axis=0, keepdims=True), jnp.sum(grad, axis=0, keepdims=True)


def project_kernel(own_at, other_at, own_to, other_to, rows_in, own, other, bias, out):
    width = own.shape[-1]
    for half, (blocks, place_of) in enumerate(((own, own_at), (other, other_at))):
        weight = in_order(blocks, place_of)
        span = slice(half * width, (half + 1) * width)
        out[:, span] = (dot_nn(rows_in[...], weight) + bias[:, span]).astype(bf16)


def cost(microseconds):
    return pl.CostEstimate(flops=0, bytes_accessed=int(microseconds * 2.5e6), transcendentals=0)


def call(kernel, places, grid, ins, outs, scratch=(), name=None, time=1):
    spec = lambda block, index: pl.BlockSpec(block, lambda i, *at: index(i, at))
    return pl.pallas_call(
        kernel,
        out_shape=[jax.ShapeDtypeStruct(shape, kind) for shape, kind, _, _ in outs],
        grid_spec=pltpu.PrefetchScalarGridSpec(
            num_scalar_prefetch=4,
            grid=(grid,),
            in_specs=[spec(block, index) for _, block, index in ins],
            out_specs=[spec(block, index) for _, _, block, index in outs],
            scratch_shapes=list(scratch),
        ),
        compiler_params=pltpu.CompilerParams(
            dimension_semantics=("arbitrary",), vmem_limit_bytes=60 << 20
        ),
        cost_estimate=cost(time),
        name=name,
    )(*places, *[array for array, _, _ in ins])


def whole(array):
    return (array, array.shape, lambda i, at: (0,) * array.ndim)


def weight_tiles(pair, tile, count=1):
    own, other, first = pair
    tiles = []
    for half, array in enumerate((own, other)):
        parts, rows = array.shape[0], array.shape[-2]
        column = lambda i: first // tile + jnp.clip(i, 0, count - 1)
        if array.ndim == 3:
            tiles.append((array, (parts, rows, tile), lambda i, at: (0, 0, column(i))))
        else:
            index = lambda i, at, half=half, parts=parts: (0, at[half][parts], 0, column(i))
            tiles.append((array, (parts, 1, rows, tile), index))
    return tiles


def project(places, rows_in, pair, bias):
    rows = rows_in.shape[0]
    half = D // 2
    return call(
        project_kernel, places, 3,
        [whole(rows_in), *weight_tiles(pair, half, 3), (bias, (1, D), lambda i, at: (0, i))],
        [((rows, 3 * D), bf16, (rows, D), lambda i, at: (0, i))],
        name="project",
        time=7,
    )[0]


def feed_forward_kernel(
    own_at, other_at, own_to, other_to, hidden, context, out_own, out_other, up_own, up_other, down_own, down_other,
    bias_up, vectors, first_in, first_low, active, slope, second_in, hidden_new, hidden_low, first_out, total,
):
    step = pl.program_id(0)
    halves = ((own_at, up_own, down_own), (other_at, up_other, down_other))
    half_d = D // 2

    @pl.when(step == 0)
    def _():
        attended = dot_nt(context[:, :half_d], in_order(out_own, own_at))
        attended += dot_nt(context[:, half_d:], in_order(out_other, other_at))
        values = hidden[...].astype(f32) + attended + vectors[0:1]
        first_in[...] = values
        unit, _ = norm_parts(values)
        values = unit * vectors[1:2] + vectors[2:3]
        first_out[...] = values
        first_low[...] = values.astype(bf16)
        total[...] = values + vectors[3:4]

    for half, (place_of, up, down) in enumerate(halves):
        before = dot_nn(first_low[...], in_order(up, place_of)) + bias_up[half]
        shade = 0.5 * (1.0 + lax.erf(before * (1.0 / math.sqrt(2.0))))
        bell = jnp.exp(-0.5 * before * before) * (1.0 / math.sqrt(2.0 * math.pi))
        low = (before * shade).astype(bf16)
        active[half] = low
        slope[half] = shade + before * bell
        total[...] += dot_nt(low, in_order(down, place_of))

    @pl.when(step == pl.num_programs(0) - 1)
    def _():
        values = total[...]
        second_in[...] = values
        unit, _ = norm_parts(values)
        values = unit * vectors[4:5] + vectors[5:6]
        hidden_new[...] = values
        hidden_low[...] = values.astype(bf16)


def feed_forward(places, hidden, context, out_pair, up_pair, down_pair, bias_up, vectors, tile=384):
    rows = hidden.shape[0]
    half_ff = bias_up.shape[2]
    count = half_ff // tile
    flat = lambda kind: ((rows, D), kind, (rows, D), lambda i, at: (0, 0))
    tiled = lambda kind: ((2, rows, half_ff), kind, (2, rows, tile), lambda i, at: (0, 0, i))
    return call(
        feed_forward_kernel, places, count,
        [
            whole(hidden),
            whole(context),
            *weight_tiles(out_pair, D // 2),
            *weight_tiles(up_pair, tile, count),
            *weight_tiles(down_pair, tile, count),
            (bias_up, (2, 1, tile), lambda i, at: (0, 0, i)),
            whole(vectors),
        ],
        [flat(f32), flat(bf16), tiled(bf16), tiled(f32), flat(f32), flat(f32), flat(bf16)],
        [pltpu.VMEM((rows, D), f32), pltpu.VMEM((rows, D), f32)],
        name="feed_forward",
        time=18,
    )


def feed_backward_kernel(
    own_at, other_at, own_to, other_to, grad, second_in, first_low, active, slope,
    up_own, up_other, down_own, down_other, vectors, grads_own, grads_other, bias_grads, total,
    small, down_low, down_turned, first_turned,
):
    step = pl.program_id(0)
    halves = (
        (own_at, own_to, up_own, down_own, grads_own),
        (other_at, other_to, up_other, down_other, grads_other),
    )

    @pl.when(step == 0)
    def _():
        result, gain_grad, shift_grad = norm_backward(second_in[...], vectors[4:5], grad[...])
        small[...] = jnp.zeros_like(small)
        small[0:1] = jnp.sum(result, axis=0, keepdims=True)
        small[1:2] = gain_grad
        small[2:3] = shift_grad
        low = result.astype(bf16)
        down_low[...] = low
        down_turned[...] = low.T
        first_turned[...] = first_low[...].T
        total[...] = result

    for half, (place_of, place_to, up, down, grads) in enumerate(halves):
        act_grad = dot_nn(down_low[...], in_order(down, place_of))
        before_grad = act_grad * slope[half]
        bias_grads[half] = jnp.broadcast_to(jnp.sum(before_grad, axis=0, keepdims=True), bias_grads.shape[1:])
        low = before_grad.astype(bf16)
        put_blocks(grads, 0, dot_nn(down_turned[...], active[half]).astype(bf16), place_to)
        put_blocks(grads, 1, dot_nn(first_turned[...], low).astype(bf16), place_to)
        total[...] += dot_nt(low, in_order(up, place_of))


def context_backward_kernel(
    own_at, other_at, own_to, other_to, grad, first_in, out_own, out_other, vectors,
    first_in_grad, out_in_low, context_grad, small,
):
    half_d = D // 2
    result, gain_grad, shift_grad = norm_backward(first_in[...], vectors[1:2], grad[...])
    small[...] = jnp.zeros_like(small)
    small[0:1] = jnp.sum(result, axis=0, keepdims=True)
    small[1:2] = gain_grad
    small[2:3] = shift_grad
    first_in_grad[...] = result
    low = result.astype(bf16)
    out_in_low[...] = low
    context_grad[:, :half_d] = dot_nn(low, in_order(out_own, own_at)).astype(bf16)
    context_grad[:, half_d:] = dot_nn(low, in_order(out_other, other_at)).astype(bf16)


def context_backward(places, grad, first_in, out_pair, vectors):
    rows = grad.shape[0]
    flat = lambda kind: ((rows, D), kind, (rows, D), lambda i, at: (0, 0))
    return call(
        context_backward_kernel, places, 1,
        [
            whole(grad), whole(first_in),
            *weight_tiles(out_pair, D // 2),
            whole(vectors),
        ],
        [flat(f32), flat(bf16), flat(bf16), ((8, D), f32, (8, D), lambda i, at: (0, 0))],
        name="context_backward",
        time=6,
    )


def feed_backward(places, grad, kept, up_pair, down_pair, vectors, tile=384):
    second_in, first_low, active, slope = kept
    rows = grad.shape[0]
    half_ff = active.shape[2]
    count = half_ff // tile
    parts, block_rows = up_pair[0].shape[0], up_pair[0].shape[-2]
    tiled = lambda array: (array, (2, rows, tile), lambda i, at: (0, 0, i))
    grads = ((parts, 2, block_rows, half_ff), bf16, (parts, 2, block_rows, tile), lambda i, at: (0, 0, 0, i))
    return call(
        feed_backward_kernel, places, count,
        [
            whole(grad), whole(second_in), whole(first_low), tiled(active), tiled(slope),
            *weight_tiles(up_pair, tile, count),
            *weight_tiles(down_pair, tile, count),
            whole(vectors),
        ],
        [
            grads, grads,
            ((2, 8, half_ff), f32, (2, 8, tile), lambda i, at: (0, 0, i)),
            ((rows, D), f32, (rows, D), lambda i, at: (0, 0)),
            ((8, D), f32, (8, D), lambda i, at: (0, 0)),
        ],
        [pltpu.VMEM((rows, D), bf16), pltpu.VMEM((D, rows), bf16), pltpu.VMEM((D, rows), bf16)],
        name="feed_backward",
        time=22,
    )


def projection_grads_kernel(
    own_at, other_at, own_to, other_to, out_in_low, context, layer_input, head_grads,
    grads_own, grads_other, turned,
):
    step = pl.program_id(0)
    half_d = D // 2
    halves = ((own_to, grads_own), (other_to, grads_other))
    for when, left, right in (
        (step == 0, out_in_low, lambda span: context[:, span]),
        (step > 0, layer_input, lambda span: head_grads[0, :, span]),
    ):

        @pl.when(when)
        def _():
            @pl.when(step <= 1)
            def _():
                turned[...] = left[...].T

            for half, (place_to, grads) in enumerate(halves):
                span = slice(half * half_d, (half + 1) * half_d)
                put_blocks(grads, 0, dot_nn(turned[...], right(span)).astype(bf16), place_to)


def projection_grads(places, out_in_low, context, layer_input, head_grads, parts):
    rows = layer_input.shape[0]
    half = D // 2
    block_rows = D // parts
    grads = ((parts, 4, block_rows, half), bf16, (parts, 1, block_rows, half), lambda i, at: (0, i, 0, 0))
    return call(
        projection_grads_kernel, places, 4,
        [
            whole(out_in_low), whole(context), whole(layer_input),
            (head_grads, (1, rows, D), lambda i, at: (jnp.maximum(i - 1, 0), 0, 0)),
        ],
        [grads, grads],
        [pltpu.VMEM((D, rows), bf16)],
        name="projection_grads",
        time=9,
    )


def project_backward_kernel(
    own_at, other_at, own_to, other_to, head_grads, first_in_grad, own, other, input_grad
):
    half_d = D // 2

    @pl.when(pl.program_id(0) == 0)
    def _():
        input_grad[...] = first_in_grad[...]

    for half, (place_of, weight) in enumerate(((own_at, own), (other_at, other))):
        low = head_grads[0, :, half * half_d : (half + 1) * half_d]
        input_grad[...] += dot_nt(low, in_order(weight, place_of))


def project_backward(places, head_grads, first_in_grad, pair):
    rows = first_in_grad.shape[0]
    half = D // 2
    return call(
        project_backward_kernel, places, 3,
        [
            (head_grads, (1, rows, D), lambda i, at: (i, 0, 0)),
            whole(first_in_grad),
            *weight_tiles(pair, half, 3),
        ],
        [((rows, D), f32, (rows, D), lambda i, at: (0, 0))],
        name="project_backward",
        time=8,
    )[0]


def head_mask(width, scale):
    lane = lax.broadcasted_iota(jnp.int32, (1, 128), 1)
    return [jnp.where(lane // 64 == head, scale, 0.0).astype(bf16) for head in range(2)]

def attend_forward_kernel(lengths, *refs, depth):
    queries, keys, value_rows = refs[:depth], refs[depth:2*depth], refs[2*depth]
    context, log_norm = refs[2*depth+1:]
    length = lengths[pl.program_id(0)]
    key_all = [k[...] for k in keys]
    key_all = jnp.concatenate(key_all, axis=1) if depth>1 else key_all[0]
    turned = value_rows[...].T
    rows = key_all.shape[0]
    valid = lax.broadcasted_iota(jnp.int32, (rows, rows), 0) < length
    scaled = head_mask(64, 0.125)
    halves = []
    for head in range(2):
        query = [q[...] * scaled[head] for q in queries]
        query = jnp.concatenate(query, axis=1) if depth>1 else query[0]
        score = jnp.where(valid, dot_nt(key_all, query), masked_score)
        top = jnp.max(score, axis=0, keepdims=True)
        weight = jnp.exp(score - top)
        total = jnp.sum(weight, axis=0, keepdims=True)
        low = (weight * (1.0 / total)).astype(bf16)
        halves.append(jnp.dot(turned[64*head:64*head+64], low, preferred_element_type=f32))
        log_norm[0, head:head+1] = top + jnp.log(total)
    context[...] = jnp.concatenate(halves, axis=0).T.astype(bf16)

def attend_forward(lengths, projections, rows):
    depth=len(projections)
    seqs=lengths.shape[0]
    pairs=D//128
    col=lambda off: pl.BlockSpec((rows,128), lambda s,j,l,off=off:(s,off*pairs+j))
    return pl.pallas_call(
        partial(attend_forward_kernel, depth=depth),
        out_shape=[jax.ShapeDtypeStruct((seqs*rows,D),bf16), jax.ShapeDtypeStruct((seqs*pairs,8,rows),f32)],
        grid_spec=pltpu.PrefetchScalarGridSpec(num_scalar_prefetch=1, grid=(seqs,pairs),
            in_specs=[col(0)]*depth+[col(1)]*depth+[col(2)],
            out_specs=[pl.BlockSpec((rows,128),lambda s,j,l:(s,j)), pl.BlockSpec((1,8,rows),lambda s,j,l:(s*pairs+j,0,0))]),
        compiler_params=pltpu.CompilerParams(dimension_semantics=("arbitrary","arbitrary"),vmem_limit_bytes=48<<20),
        cost_estimate=cost(10),
        name="attend_forward",
    )(lengths, *projections, *projections, projections[0])

def attend_backward_kernel(lengths, *refs, depth, with_later, keep_total):
    queries, keys, value_rows = refs[:depth], refs[depth:2*depth], refs[2*depth]
    log_norm, context_grad = refs[2*depth+1:2*depth+3]
    at = 2*depth+3
    if with_later:
        later = refs[at]; at+=1
    grads, value_sum = refs[at:at+2]
    if keep_total: total_out = refs[at+2]
    length = lengths[pl.program_id(0)]
    key_all = [k[...] for k in keys]
    key_all = jnp.concatenate(key_all, axis=1) if depth>1 else key_all[0]
    rows = key_all.shape[0]
    valid = lax.broadcasted_iota(jnp.int32, (rows, rows), 0) < length
    scaled = head_mask(64, 0.125)
    plain = head_mask(64, 1.0)
    key_turned = (keys[0][...] * 0.125).astype(bf16).T
    query_halves = []
    key_grad = value_grad = None
    for head in range(2):
        query = [q[...] * scaled[head] for q in queries]
        query_own = query[0]
        query = jnp.concatenate(query, axis=1) if depth>1 else query[0]
        score = jnp.where(valid, dot_nt(key_all, query), masked_score)
        soft = jnp.exp(score - log_norm[0, head:head+1])
        grad_rows = context_grad[...] * plain[head]
        soft_grad = dot_nt(value_rows[...], grad_rows)
        product = soft * soft_grad
        total = product - soft * jnp.sum(product, axis=0, keepdims=True)
        if with_later: total = total + later[head]
        if keep_total: total_out[head] = total
        low = total.astype(bf16)
        query_halves.append(jnp.dot(key_turned[64*head:64*head+64], low, preferred_element_type=f32))
        kg = jnp.dot(low, query_own, preferred_element_type=f32)
        vg = jnp.dot(soft.astype(bf16), grad_rows, preferred_element_type=f32)
        key_grad = kg if key_grad is None else key_grad+kg
        value_grad = vg if value_grad is None else value_grad+vg
    grads[0] = jnp.concatenate(query_halves, axis=0).T.astype(bf16)
    grads[1] = key_grad.astype(bf16)
    grads[2] = value_grad.astype(bf16)
    sums = jnp.sum(value_grad, axis=0, keepdims=True)
    value_sum[0] = jnp.broadcast_to(sums, (8,128))

def attend_backward(lengths, projections, log_norm, context_grad, later, keep_total, rows):
    depth=len(projections)
    seqs=lengths.shape[0]
    pairs=D//128
    col=lambda off: pl.BlockSpec((rows,128), lambda s,j,l,off=off:(s,off*pairs+j))
    square=pl.BlockSpec((2,rows,rows),lambda s,j,l:(s*pairs+j,0,0))
    in_specs=[col(0)]*depth+[col(1)]*depth+[col(2)]+[pl.BlockSpec((1,8,rows),lambda s,j,l:(s*pairs+j,0,0)), col(0)]
    args=[*projections,*projections,projections[0],log_norm,context_grad]
    if later is not None:
        in_specs.append(square); args.append(later)
    out_shape=[jax.ShapeDtypeStruct((3,seqs*rows,D),bf16), jax.ShapeDtypeStruct((seqs,8,D),f32)]
    out_specs=[pl.BlockSpec((3,rows,128),lambda s,j,l:(0,s,j)), pl.BlockSpec((1,8,128),lambda s,j,l:(s,0,j))]
    if keep_total:
        out_shape.append(jax.ShapeDtypeStruct((seqs*pairs*2,rows,rows),f32)); out_specs.append(square)
    return pl.pallas_call(
        partial(attend_backward_kernel, depth=depth, with_later=later is not None, keep_total=keep_total),
        out_shape=out_shape,
        grid_spec=pltpu.PrefetchScalarGridSpec(num_scalar_prefetch=1, grid=(seqs,pairs), in_specs=in_specs, out_specs=out_specs),
        compiler_params=pltpu.CompilerParams(dimension_semantics=("arbitrary","arbitrary"),vmem_limit_bytes=48<<20),
        cost_estimate=cost(17),
        name="attend_backward",
    )(lengths,*args)


def adam_parts(gradient, first, second, factor):
    clipped = gradient * factor
    first_new = beta_one * first + (1.0 - beta_one) * clipped
    second_new = beta_two * second + (1.0 - beta_two) * clipped * clipped
    first_hat = first_new / (1.0 - beta_one**step_count)
    second_hat = second_new / (1.0 - beta_two**step_count)
    return (first_new, second_new, first_hat / (jnp.sqrt(second_hat) + adam_eps))


def local(
    tokens,
    cotangent,
    lengths,
    proj_weight,
    out_weight,
    up_weight,
    down_weight,
    small_params,
    proj_first,
    proj_second,
    out_first,
    out_second,
    up_first,
    up_second,
    down_first,
    down_second,
    small_first,
    small_second,
):
    layers = proj_weight.shape[0]
    seq_here = lengths.shape[0] // 2
    seq_len = tokens.shape[0] // lengths.shape[0]
    rows_here = seq_here * seq_len
    head_dim = D // HEADS
    half_d = proj_weight.shape[3]
    half_ff = up_weight.shape[2]
    row_count = proj_weight.shape[1]
    score_scale = 1.0 / math.sqrt(head_dim)
    core = lax.axis_index("tensor")
    parts = lax.axis_size("dp")
    links = Links(parts)
    at = lax.axis_index("dp")
    inverse = jnp.asarray(links.inverse)
    order = jnp.arange(parts, dtype=jnp.int32) ^ at
    own_at = inverse[core][order]
    other_at = inverse[1 - core][order]
    def with_half(places, half):
        return jnp.concatenate([places, half[None].astype(jnp.int32)])

    every = jnp.arange(parts, dtype=jnp.int32)
    exchanged = (own_at, other_at, own_at, other_at)
    in_turn = (with_half(every, core), with_half(every, 1 - core), own_at, other_at)
    turns = {(0, "proj"): exchanged, (0, "ff"): in_turn, (1, "proj"): in_turn, (1, "ff"): exchanged}

    table = {"proj": proj_weight, "out": out_weight, "up": up_weight, "down": down_weight}
    groups = [
        [(0, "proj")], [(0, "out"), (0, "up"), (0, "down")], [(1, "proj")], [(1, "out"), (1, "up"), (1, "down")],
    ]
    gathers = []
    for group in groups:
        share = [table[kind][layer_at].reshape(row_count, -1).astype(bf16) for layer_at, kind in group]
        gathers.append(links.gather(jnp.concatenate(share, axis=1) if len(share) > 1 else share[0]))
    one, two, three, four = gathers
    late = jnp.concatenate([two.pop("held")[0], three.pop("held")[0]], axis=1)
    late = lax.all_gather(late, ("dp", "tensor")).reshape(parts, 2, row_count, -1)
    two["pair"] = (late, late, 0)
    three["pair"] = (late, late, half_d + 2 * half_ff)

    def gathered(layer_at, kind):
        for group, move in zip(groups, gathers):
            widths = [math.prod(table[name].shape[2:]) for _, name in group]
            if (layer_at, kind) in group:
                while links.running(move):
                    links.advance([move])
                own, other, first = move["pair"]
                return own, other, first + sum(widths[: group.index((layer_at, kind))])

    def own_first(vector):
        half = vector.shape[-1] // 2
        return jnp.where(core == 0, vector, jnp.roll(vector, half, axis=-1))

    tokens = lax.dynamic_slice_in_dim(tokens, core * rows_here, rows_here)
    cotangent = lax.dynamic_slice_in_dim(cotangent, core * rows_here, rows_here)
    lengths = lax.dynamic_slice_in_dim(lengths, core * seq_here, seq_here)
    positions = jnp.arange(seq_len)
    key_valid = positions[None, :] < lengths[:, None]
    row_valid = key_valid.reshape(-1, 1)

    grad_rows = jnp.where(row_valid, cotangent.astype(f32), 0.0)
    vectors, value_bias, up_bias = [], [], []
    for layer_at in range(layers):
        bias_v, bias_o, bias_up, bias_down, gain_one, shift_one, gain_two, shift_two = split_vector(
            small_params[layer_at]
        )
        blank = jnp.zeros_like(bias_o)
        vectors.append(
            jnp.stack([bias_o, gain_one, shift_one, bias_down, gain_two, shift_two, blank, blank])
        )
        value_bias.append(jnp.concatenate([blank, blank, own_first(bias_v)])[None])
        up_bias.append(own_first(bias_up).reshape(2, 1, half_ff))
    masters = (proj_weight, out_weight, up_weight, down_weight)
    weight_square = jnp.stack(
        [jnp.sum(master * master, axis=tuple(range(1, master.ndim))) for master in masters], axis=1
    )

    links.advance([one])
    links.advance([one])
    links.advance([one])
    links.advance([one])
    prepared = (tokens, grad_rows, vectors, value_bias, up_bias, weight_square)
    (prepared,) = links.advance([four], (prepared,))
    tokens, grad_rows, vectors, value_bias, up_bias, weight_square = prepared
    (tokens,) = links.advance([one], (tokens,))

    saved = []
    hidden, hidden_low = tokens, tokens
    for layer_at in range(layers):
        places = turns[layer_at, "proj"]
        projected = project(places, hidden_low, gathered(layer_at, "proj"), value_bias[layer_at])
        if layer_at == 0:
            (projected,) = links.advance([four], (projected,))
        chain = [projected] + [earlier["projected"] for earlier in reversed(saved)]
        context, log_norm = attend_forward(lengths, chain, seq_len)
        if layer_at == 0:
            (context,) = links.advance([four], (context,))
            (context,) = links.advance([four], (context,))
        kept = {"layer_input": hidden_low, "projected": projected, "log_norm": log_norm, "context": context}
        (
            kept["first_in"], kept["first_low"], kept["active"], kept["slope"], kept["second_in"], hidden, hidden_low,
        ) = feed_forward(
            turns[layer_at, "ff"], hidden, context, gathered(layer_at, "out"),
            gathered(layer_at, "up"), gathered(layer_at, "down"), up_bias[layer_at], vectors[layer_at],
        )
        if layer_at == 0:
            (hidden_low,) = links.advance([four], (hidden_low,))
        saved.append(kept)

    sums = []
    smalls = [None] * layers
    later_total = None
    for layer_at in reversed(range(layers)):
        kept = saved[layer_at]
        places = turns[layer_at, "ff"]
        own, other, bias_sum, first_grad, second_small = feed_backward(
            places, grad_rows, [kept[name] for name in ("second_in", "first_low", "active", "slope")],
            gathered(layer_at, "up"), gathered(layer_at, "down"), vectors[layer_at],
        )
        ff_sum = links.scatter(own, other)
        (first_grad,) = links.advance(sums + [ff_sum], (first_grad,))
        first_in_grad, out_in_low, context_grad, first_small = context_backward(
            places, first_grad, kept["first_in"], gathered(layer_at, "out"), vectors[layer_at]
        )
        (context_grad,) = links.advance([ff_sum], (context_grad,))
        chain = [kept["projected"]] + [earlier["projected"] for earlier in reversed(saved[:layer_at])]
        results = attend_backward(
            lengths, chain, kept["log_norm"], context_grad, later_total, layer_at > 0, seq_len
        )
        head_grads, value_sum = results[:2]
        later_total = results[2] if layer_at > 0 else None
        (head_grads,) = links.advance(sums, (head_grads,))
        attention_sum = links.scatter(
            *projection_grads(exchanged, out_in_low, kept["context"], kept["layer_input"], head_grads, parts)
        )
        (head_grads,) = links.advance([ff_sum, attention_sum], (head_grads,))
        grad_rows = project_backward(turns[layer_at, "proj"], head_grads, first_in_grad, gathered(layer_at, "proj"))
        if layer_at > 0:
            (grad_rows,) = links.advance([attention_sum], (grad_rows,))
        sums += [ff_sum, attention_sum]
        smalls[layer_at] = jnp.concatenate(
            [
                own_first(jnp.sum(value_sum[:, 0], axis=0)),
                first_small[0],
                own_first(bias_sum[:, 0].reshape(-1)),
                second_small[0],
                first_small[1],
                first_small[2],
                second_small[1],
                second_small[2],
            ]
        )

    totals = links.finish(sums)[::-1]
    attention_sums, ff_sums = jnp.stack(totals[0::2]), jnp.stack(totals[1::2])
    grads = (
        attention_sums[:, 1:].transpose(0, 2, 1, 3), attention_sums[:, 0], ff_sums[:, 1], ff_sums[:, 0],
    )
    firsts = (proj_first, out_first, up_first, down_first)
    seconds = (proj_second, out_second, up_second, down_second)
    width = small_params.shape[1]
    pack = jnp.concatenate([jnp.stack(smalls), jnp.pad(weight_square, ((0, 0), (0, 124)))], axis=1)
    pack = links.total(pack)
    small_grad = pack[:, :width]
    weight_square = pack[:, width : width + 4].T

    square_part = sum(jnp.sum(grad * grad) for grad in grads)
    square_big = links.total(jnp.broadcast_to(square_part, (8, 128)))[0, 0]
    grad_norm = jnp.sqrt(square_big + jnp.sum(small_grad * small_grad))
    factor = clip_norm / jnp.maximum(grad_norm, clip_norm)
    moments = []
    updates = []
    for kind_at in range(4):
        first_new, second_new, direction = adam_parts(
            grads[kind_at], firsts[kind_at], seconds[kind_at], factor
        )
        moments.append((first_new, second_new))
        updates.append(direction + decay_rate * masters[kind_at])
    update_square = jnp.stack(
        [jnp.sum(update * update, axis=tuple(range(1, update.ndim))) for update in updates]
    )
    update_square = links.total(jnp.pad(update_square.reshape(1, -1), ((0, 7), (0, 128 - 4 * layers))))
    update_square = update_square[0, : 4 * layers].reshape(4, layers)
    ratio = jnp.sqrt(weight_square) / jnp.sqrt(update_square)

    gather_rows = partial(lax.all_gather, axis_name="tensor", axis=0, tiled=True)
    outputs = [gather_rows(hidden), gather_rows(grad_rows), grad_norm]
    for kind_at in range(4):
        master = masters[kind_at]
        scaled = ratio[kind_at].reshape((-1,) + (1,) * (master.ndim - 1))
        outputs += [
            moments[kind_at][0],
            moments[kind_at][1],
            master - matrix_rate * scaled * updates[kind_at],
        ]
    small_first_new, small_second_new, small_direction = adam_parts(
        small_grad, small_first, small_second, factor
    )
    outputs += [small_first_new, small_second_new, small_params - vector_rate * small_direction]
    return tuple(outputs)


def solution(mesh):
    proj = P(None, "dp", None, "tensor")
    matrix = P(None, "dp", "tensor")
    rows = P("dp", None)
    return jax.shard_map(
        local,
        mesh=mesh,
        in_specs=(rows, rows, P("dp"), proj, matrix, matrix, matrix, P())
        + (proj, proj)
        + (matrix,) * 6
        + (P(), P()),
        out_specs=(rows, rows, P()) + (proj,) * 3 + (matrix,) * 9 + (P(),) * 3,
        check_vma=False,
    )
```

```python
from functools import partial
import math

import jax
import jax.numpy as jnp
import numpy as np
from jax import lax
from jax.experimental import pallas as pl
from jax.experimental.pallas import tpu as pltpu
from jax.sharding import PartitionSpec as P

D = 768
HEADS = 12
FF = 3072


beta_one = 0.9
beta_two = 0.999
adam_eps = 1e-06
decay_rate = 0.01
matrix_rate = 1.0
vector_rate = 0.3
clip_norm = 1.0
step_count = 10.0
norm_eps = 1e-06
masked_score = -1e30

f32 = jnp.float32
bf16 = jnp.bfloat16


class Links:
    def __init__(self, parts):
        self.parts = parts
        count = parts.bit_length() - 1
        high = list(range(count - 1, -1, -1))
        other = high[:-2] + high[-2:][::-1]
        self.orders = (other, high)
        self.inverse = np.zeros((2, parts), np.int32)
        for core in range(2):
            for place in range(parts):
                mask = 0
                for stage in range(count):
                    if (place >> stage) & 1:
                        mask |= 1 << self.orders[core][stage]
                self.inverse[core, mask] = place
        self.stages = count
        self.last = ()
        every = np.arange(parts)
        self.table = np.zeros((2, parts, 6, parts + 1), np.int32)
        for core in range(2):
            for at in range(parts):
                for half, side in enumerate((core, 1 - core)):
                    differs = [((every ^ at) >> bit) & 1 for bit in self.orders[side][-2:]]
                    zoned = (2 * differs[1] + differs[0]) * (parts // 4) + every // 4
                    rows = (self.inverse[side, every ^ at], zoned, every)
                    for kind, row in enumerate(rows):
                        self.table[core, at, 2 * kind + half, :parts] = row
                        self.table[core, at, 2 * kind + half, parts] = side

    def swap(self, value, *stages):
        pairs = []
        for core in range(2):
            flip = sum(1 << self.orders[core][stage] for stage in stages)
            pairs += [(2 * at + core, 2 * (at ^ flip) + core) for at in range(self.parts)]
        return lax.ppermute(value, ("dp", "tensor"), pairs)

    def sibling(self, value):
        return lax.ppermute(value, "tensor", [(0, 1), (1, 0)])

    def gather(self, share):
        return {"held": share[None], "stage": 0}

    def gather_last(self, held):
        return {"held": held, "stage": self.stages - 2}

    def total(self, value):
        return {"value": value, "step": 0}

    def scatter(self, own, other):
        return {"pieces": [own], "other": other, "size": self.parts, "stage": self.stages}

    def advance(self, moves, rest=()):
        moves = [move for move in moves if self.running(move)]
        if not moves:
            return rest
        mine, rest, self.last = lax.optimization_barrier(
            ([move.get("held", move.get("value", move.get("pieces"))) for move in moves], rest, self.last)
        )
        sending = []
        for move, value in zip(moves, mine):
            if "held" in move:
                come = move.pop("come", None)
                sending.append(value if come is None else jnp.concatenate([value, come], axis=0))
            elif "value" in move:
                sending.append(self.summed(value, move.pop("come", [])))
            elif "other" in move:
                sending.append(move["other"])
            else:
                half, size = move["size"] // 2, move["size"]
                move["pieces"] = value + move.pop("come")
                sending.append(sum(piece[half:size].astype(f32) for piece in move["pieces"]).astype(bf16))
        sending, rest, _ = lax.optimization_barrier((sending, rest, self.last))
        self.last = sending[0]
        for move, value in zip(moves, sending):
            if "held" in move:
                move["held"] = value
                move["come"] = self.swap(value, move["stage"])
                move["stage"] += 1
            elif "value" in move:
                move["value"] = value
                low, high = 2 * move["step"] - 2, 2 * move["step"] - 1
                if move["step"] == 0:
                    move["come"] = [self.sibling(value)]
                elif high < self.stages:
                    move["come"] = [self.swap(value, low), self.swap(value, high), self.swap(value, low, high)]
                else:
                    move["come"] = [self.swap(value, low)]
                move["step"] += 1
            elif "other" in move:
                move["come"] = [self.sibling(value)]
                del move["other"]
            else:
                move["size"] //= 2
                move["stage"] -= 1
                move["come"] = [self.swap(value, move["stage"])]
        return rest

    def pair(self, move, rest=()):
        held, rest = lax.optimization_barrier((move.pop("held"), rest))
        held = jnp.concatenate([held, move.pop("come")], axis=0)
        move["pair"] = (held, self.sibling(held), 0)
        return rest

    def summed(self, value, come):
        if len(come) == 3:
            return (value + come[0]) + (come[1] + come[2])
        return value + come[0] if come else value

    def running(self, move):
        return move.get("stage", 0) < self.stages if "held" in move else move.get("size", 1) > 1 or 2 * move.get("step", self.stages) < self.stages + 2

    def settle(self, moves, rest):
        pieces, rest = lax.optimization_barrier(([move["pieces"] for move in moves], rest))
        for move, value in zip(moves, pieces):
            move["pieces"] = value
        return lax.optimization_barrier((self.finish(moves), rest))

    def finish(self, moves):
        for move in moves:
            while self.running(move):
                self.advance([move])
        if "value" in moves[0]:
            return [self.summed(move["value"], move["come"]) for move in moves]
        return [sum(piece[0].astype(f32) for piece in move["pieces"] + move["come"]) for move in moves]


def dot_nt(left, right):
    return lax.dot_general(left, right, (((1,), (1,)), ((), ())), preferred_element_type=f32)


def dot_nn(left, right):
    return jnp.dot(left, right, preferred_element_type=f32)


def in_order(blocks, place_of):
    some = (0,) if len(blocks.shape) == 4 else ()
    return jnp.concatenate([blocks[(place_of[block], *some)] for block in range(blocks.shape[0])], axis=0)


def put_blocks(out, at, product, place_of):
    parts, _, rows, _ = out.shape
    for block in range(parts):
        out[place_of[block], at] = product[block * rows : (block + 1) * rows]


def norm_parts(values):
    centered = values - jnp.mean(values, axis=1, keepdims=True)
    variance = jnp.mean(centered * centered, axis=1, keepdims=True)
    scale = lax.rsqrt(variance + norm_eps)
    return centered * scale, scale


def norm_backward(values, gain, grad):
    unit, scale = norm_parts(values)
    scaled = grad * gain
    inner = scaled - jnp.mean(scaled, axis=1, keepdims=True)
    result = scale * (inner - unit * jnp.mean(scaled * unit, axis=1, keepdims=True))
    return result, jnp.sum(grad * unit, axis=0, keepdims=True), jnp.sum(grad, axis=0, keepdims=True)


def project_kernel(own_at, other_at, own_to, other_to, rows_in, own, other, bias, out):
    width = own.shape[-1]
    for half, (blocks, place_of) in enumerate(((own, own_at), (other, other_at))):
        weight = in_order(blocks, place_of)
        span = slice(half * width, (half + 1) * width)
        out[:, span] = (dot_nn(rows_in[...], weight) + bias[:, span]).astype(bf16)


def cost(microseconds):
    return pl.CostEstimate(flops=0, bytes_accessed=int(microseconds * 2.5e6), transcendentals=0)


class Row:
    def __init__(self, table, row):
        self.table, self.row = table, row

    def __getitem__(self, place):
        return self.table[self.row, place]


def call(kernel, places, grid, ins, outs, scratch=(), name=None, time=1):
    table, pair = places
    weight_rows = lambda at: (Row(at, 2 * pair), Row(at, 2 * pair + 1))
    spec = lambda block, index: pl.BlockSpec(block, lambda i, at: index(i, weight_rows(at)))
    return pl.pallas_call(
        lambda at, *refs: kernel(*weight_rows(at), Row(at, 0), Row(at, 1), *refs),
        out_shape=[jax.ShapeDtypeStruct(shape, kind) for shape, kind, _, _ in outs],
        grid_spec=pltpu.PrefetchScalarGridSpec(
            num_scalar_prefetch=1,
            grid=(grid,),
            in_specs=[spec(block, index) for _, block, index in ins],
            out_specs=[spec(block, index) for _, _, block, index in outs],
            scratch_shapes=list(scratch),
        ),
        compiler_params=pltpu.CompilerParams(
            dimension_semantics=("arbitrary",), vmem_limit_bytes=60 << 20
        ),
        cost_estimate=cost(time),
        name=name,
    )(table, *[array for array, _, _ in ins])


def whole(array):
    return (array, array.shape, lambda i, at: (0,) * array.ndim)


def weight_tiles(pair, tile, count=1):
    own, other, first = pair
    tiles = []
    for half, array in enumerate((own, other)):
        parts, rows = array.shape[0], array.shape[-2]
        column = lambda i: first // tile + jnp.clip(i, 0, count - 1)
        if array.ndim == 3:
            tiles.append((array, (parts, rows, tile), lambda i, at: (0, 0, column(i))))
        else:
            index = lambda i, at, half=half, parts=parts: (0, at[half][parts], 0, column(i))
            tiles.append((array, (parts, 1, rows, tile), index))
    return tiles


def project(places, rows_in, pair, bias):
    rows = rows_in.shape[0]
    half = D // 2
    return call(
        project_kernel, places, 3,
        [whole(rows_in), *weight_tiles(pair, half, 3), (bias, (1, D), lambda i, at: (0, i))],
        [((rows, 3 * D), bf16, (rows, D), lambda i, at: (0, i))],
        name="project",
        time=7,
    )[0]


def feed_forward_kernel(
    own_at, other_at, own_to, other_to, hidden, context, out_own, out_other, up_own, up_other, down_own, down_other,
    bias_up, vectors, *refs, with_grad,
):
    if with_grad:
        grad, first_in, first_low, first_turned, active, slope, hidden_new, *turned, second_in = refs
        total = second_in
    else:
        first_in, first_low, first_turned, active, slope, hidden_new, second_in, hidden_low, hidden_turned = refs
        total = second_in
    step = pl.program_id(0)
    halves = ((own_at, up_own, down_own), (other_at, up_other, down_other))
    half_d = D // 2

    @pl.when(step == 0)
    def _():
        attended = dot_nt(context[:, :half_d], in_order(out_own, own_at))
        attended += dot_nt(context[:, half_d:], in_order(out_other, other_at))
        values = hidden[...].astype(f32) + attended + vectors[0:1]
        first_in[...] = values
        unit, _ = norm_parts(values)
        values = unit * vectors[1:2] + vectors[2:3]
        low = values.astype(bf16)
        first_low[...] = low
        first_turned[...] = low.T
        total[...] = values + vectors[3:4]

    for half, (place_of, up, down) in enumerate(halves):
        before = dot_nn(first_low[...], in_order(up, place_of)) + bias_up[half]
        shade = 0.5 * (1.0 + lax.erf(before * (1.0 / math.sqrt(2.0))))
        bell = jnp.exp(-0.5 * before * before) * (1.0 / math.sqrt(2.0 * math.pi))
        low = (before * shade).astype(bf16)
        active[half] = low
        slope[half] = shade + before * bell
        total[...] += dot_nt(low, in_order(down, place_of))

    @pl.when(step == pl.num_programs(0) - 1)
    def _():
        unit, _ = norm_parts(second_in[...])
        values = unit * vectors[4:5] + vectors[5:6]
        hidden_new[...] = values
        if with_grad:
            norm_turn(second_in[...], vectors[4:5], grad[...], *turned)
        else:
            low = values.astype(bf16)
            hidden_low[...] = low
            hidden_turned[...] = low.T


def feed_forward(places, hidden, context, out_pair, up_pair, down_pair, bias_up, vectors, grad=None, tile=384):
    rows = hidden.shape[0]
    half_ff = bias_up.shape[2]
    count = half_ff // tile
    flat = lambda kind: ((rows, D), kind, (rows, D), lambda i, at: (0, 0))
    tiled = lambda kind: ((2, rows, half_ff), kind, (2, rows, tile), lambda i, at: (0, 0, i))
    turned = ((D, rows), bf16, (D, rows), lambda i, at: (0, 0))
    return call(
        partial(feed_forward_kernel, with_grad=grad is not None), places, count,
        [
            whole(hidden),
            whole(context),
            *weight_tiles(out_pair, D // 2),
            *weight_tiles(up_pair, tile, count),
            *weight_tiles(down_pair, tile, count),
            (bias_up, (2, 1, tile), lambda i, at: (0, 0, i)),
            whole(vectors),
            *([] if grad is None else [whole(grad)]),
        ],
        [
            flat(f32), flat(bf16), turned, tiled(bf16), tiled(f32), flat(f32),
            *([flat(f32), flat(bf16), turned] if grad is None else norm_turn_outs(rows)),
        ],
        [] if grad is None else [pltpu.VMEM((rows, D), f32)],
        name="feed_forward",
        time=18,
    )


def norm_turn(values, gain, grad, total, down_low, down_turned, small):
    result, gain_grad, shift_grad = norm_backward(values, gain, grad)
    small[...] = jnp.zeros_like(small)
    small[0:1] = jnp.sum(result, axis=0, keepdims=True)
    small[1:2] = gain_grad
    small[2:3] = shift_grad
    total[...] = result
    low = result.astype(bf16)
    down_low[...] = low
    down_turned[...] = low.T


def norm_turn_outs(rows):
    flat = lambda kind: ((rows, D), kind, (rows, D), lambda i, at: (0, 0))
    turned = ((D, rows), bf16, (D, rows), lambda i, at: (0, 0))
    return [flat(f32), flat(bf16), turned, ((8, D), f32, (8, D), lambda i, at: (0, 0))]


def feed_backward_kernel(
    own_at, other_at, own_to, other_to, total_in, down_low, down_turned, first_turned, active, slope,
    up_own, up_other, down_own, down_other, grads_own, grads_other, bias_grads, total,
):
    halves = (
        (own_at, own_to, up_own, down_own, grads_own),
        (other_at, other_to, up_other, down_other, grads_other),
    )

    @pl.when(pl.program_id(0) == 0)
    def _():
        total[...] = total_in[...]

    for half, (place_of, place_to, up, down, grads) in enumerate(halves):
        act_grad = dot_nn(down_low[...], in_order(down, place_of))
        before_grad = act_grad * slope[half]
        bias_grads[half] = jnp.broadcast_to(jnp.sum(before_grad, axis=0, keepdims=True), bias_grads.shape[1:])
        low = before_grad.astype(bf16)
        put_blocks(grads, 0, dot_nn(down_turned[...], active[half]).astype(bf16), place_to)
        put_blocks(grads, 1, dot_nn(first_turned[...], low).astype(bf16), place_to)
        total[...] += dot_nt(low, in_order(up, place_of))


def context_backward_kernel(
    own_at, other_at, own_to, other_to, grad, first_in, out_own, out_other, vectors,
    first_in_grad, out_in_turned, context_grad, small,
):
    half_d = D // 2
    result, gain_grad, shift_grad = norm_backward(first_in[...], vectors[1:2], grad[...])
    small[...] = jnp.zeros_like(small)
    small[0:1] = jnp.sum(result, axis=0, keepdims=True)
    small[1:2] = gain_grad
    small[2:3] = shift_grad
    first_in_grad[...] = result
    low = result.astype(bf16)
    out_in_turned[...] = low.T
    context_grad[:, :half_d] = dot_nn(low, in_order(out_own, own_at)).astype(bf16)
    context_grad[:, half_d:] = dot_nn(low, in_order(out_other, other_at)).astype(bf16)


def context_backward(places, grad, first_in, out_pair, vectors):
    rows = grad.shape[0]
    flat = lambda kind: ((rows, D), kind, (rows, D), lambda i, at: (0, 0))
    return call(
        context_backward_kernel, places, 1,
        [
            whole(grad), whole(first_in),
            *weight_tiles(out_pair, D // 2),
            whole(vectors),
        ],
        [
            flat(f32), ((D, rows), bf16, (D, rows), lambda i, at: (0, 0)), flat(bf16),
            ((8, D), f32, (8, D), lambda i, at: (0, 0)),
        ],
        name="context_backward",
        time=6,
    )


def feed_backward(places, total, down_low, down_turned, kept, up_pair, down_pair, parts, tile=384):
    first_turned, active, slope = kept
    rows = total.shape[0]
    half_ff = active.shape[2]
    count = half_ff // tile
    block_rows = D // parts
    tiled = lambda array: (array, (2, rows, tile), lambda i, at: (0, 0, i))
    grads = ((parts, 2, block_rows, count * tile), bf16, (parts, 2, block_rows, tile), lambda i, at: (0, 0, 0, i))
    return call(
        feed_backward_kernel, places, count,
        [
            whole(total), whole(down_low), whole(down_turned), whole(first_turned), tiled(active), tiled(slope),
            *weight_tiles(up_pair, tile, count),
            *weight_tiles(down_pair, tile, count),
        ],
        [
            grads, grads,
            ((2, 8, count * tile), f32, (2, 8, tile), lambda i, at: (0, 0, i)),
            ((rows, D), f32, (rows, D), lambda i, at: (0, 0)),
        ],
        name="feed_backward",
        time=20,
    )


def projection_grads_kernel(
    own_at, other_at, own_to, other_to, out_in_turned, context, input_turned, head_grads,
    grads_own, grads_other,
):
    step = pl.program_id(0)
    half_d = D // 2
    halves = ((own_to, grads_own), (other_to, grads_other))
    for when, left, right in (
        (step == 0, out_in_turned, lambda span: context[:, span]),
        (step > 0, input_turned, lambda span: head_grads[0, :, span]),
    ):

        @pl.when(when)
        def _():
            for half, (place_to, grads) in enumerate(halves):
                span = slice(half * half_d, (half + 1) * half_d)
                put_blocks(grads, 0, dot_nn(left[...], right(span)).astype(bf16), place_to)


def projection_grads(places, out_in_turned, context, input_turned, head_grads, parts):
    rows = context.shape[0]
    half = D // 2
    block_rows = D // parts
    grads = ((parts, 4, block_rows, half), bf16, (parts, 1, block_rows, half), lambda i, at: (0, i, 0, 0))
    return call(
        projection_grads_kernel, places, 4,
        [
            whole(out_in_turned), whole(context), whole(input_turned),
            (head_grads, (1, rows, D), lambda i, at: (jnp.maximum(i - 1, 0), 0, 0)),
        ],
        [grads, grads],
        name="projection_grads",
        time=9,
    )


def project_backward_kernel(
    own_at, other_at, own_to, other_to, head_grads, first_in_grad, own, other, *refs, with_norm
):
    half_d = D // 2
    step = pl.program_id(0)
    if with_norm:
        second_in, vectors, *turned, input_grad = refs
    else:
        (input_grad,) = refs

    @pl.when(step == 0)
    def _():
        input_grad[...] = first_in_grad[...]

    for half, (place_of, weight) in enumerate(((own_at, own), (other_at, other))):
        low = head_grads[0, :, half * half_d : (half + 1) * half_d]
        input_grad[...] += dot_nt(low, in_order(weight, place_of))

    if with_norm:

        @pl.when(step == pl.num_programs(0) - 1)
        def _():
            norm_turn(second_in[...], vectors[4:5], input_grad[...], *turned)


def project_backward(places, head_grads, first_in_grad, pair, earlier=()):
    rows = first_in_grad.shape[0]
    half = D // 2
    return call(
        partial(project_backward_kernel, with_norm=bool(earlier)), places, 3,
        [
            (head_grads, (1, rows, D), lambda i, at: (i, 0, 0)),
            whole(first_in_grad),
            *weight_tiles(pair, half, 3),
            *map(whole, earlier),
        ],
        norm_turn_outs(rows) if earlier else [((rows, D), f32, (rows, D), lambda i, at: (0, 0))],
        [pltpu.VMEM((rows, D), f32)] if earlier else [],
        name="project_backward",
        time=8,
    )


def join_kernel(core, *refs):
    step = pl.program_id(0)
    count = len(refs) // 3
    for one in range(count):
        own, other, out = refs[2 * one], refs[2 * one + 1], refs[2 * count + one]

        @pl.when(step == core[0])
        def _():
            out[...] = own[...]

        @pl.when(step != core[0])
        def _():
            out[...] = other[...]


def join(core, pairs):
    rows, cols = pairs[0][0].shape
    spec = pl.BlockSpec((rows, cols), lambda i, at: (0, 0))
    return pl.pallas_call(
        join_kernel,
        out_shape=[jax.ShapeDtypeStruct((2 * rows, cols), f32) for _ in pairs],
        grid_spec=pltpu.PrefetchScalarGridSpec(
            num_scalar_prefetch=1,
            grid=(2,),
            in_specs=[spec] * (2 * len(pairs)),
            out_specs=[pl.BlockSpec((rows, cols), lambda i, at: (i, 0)) for _ in pairs],
        ),
        compiler_params=pltpu.CompilerParams(
            dimension_semantics=("arbitrary",), vmem_limit_bytes=60 << 20
        ),
        cost_estimate=cost(4),
        name="join",
    )(core, *[rows_of for pair in pairs for rows_of in pair])


bounds = [0, D, 2 * D, 2 * D + FF, 3 * D + FF, 4 * D + FF, 5 * D + FF, 6 * D + FF, 7 * D + FF]


def swapped(core, vector):
    half = vector.shape[1] // 2
    first, second = vector[:, :half], vector[:, half:]
    return jnp.where(core == 0, first, second), jnp.where(core == 0, second, first)


def prepare_kernel(core, lengths, tokens, cotangent, small, tokens_own, tokens_turned, grad, *outs):
    step = pl.program_id(0)
    length = lengths[core[0] * pl.num_programs(0) + step]
    tokens_own[...] = tokens[...]
    tokens_turned[...] = tokens[...].T
    valid = lax.broadcasted_iota(jnp.int32, grad.shape, 0) < length
    grad[...] = jnp.where(valid, cotangent[...].astype(f32), 0.0)

    @pl.when(step == 0)
    def _():
        for layer_at in range(small.shape[0]):
            vectors, value_bias, up_bias = outs[3 * layer_at : 3 * layer_at + 3]
            part = lambda place: small[layer_at : layer_at + 1, bounds[place] : bounds[place + 1]]
            vectors[...] = jnp.zeros_like(vectors)
            for row, place in enumerate((1, 4, 5, 3, 6, 7)):
                vectors[row : row + 1] = part(place)
            value_bias[...] = jnp.zeros_like(value_bias)
            first, second = swapped(core[0], part(0))
            value_bias[:, 2 * D : 2 * D + D // 2] = first
            value_bias[:, 2 * D + D // 2 :] = second
            up_bias[0], up_bias[1] = swapped(core[0], part(2))


def prepare(core, lengths, tokens, cotangent, small):
    layers = small.shape[0]
    seqs = lengths.shape[0] // 2
    rows = tokens.shape[0] // lengths.shape[0]
    mine = pl.BlockSpec((rows, D), lambda s, c, l: (c[0] * seqs + s, 0))
    fixed = lambda shape: pl.BlockSpec(shape, lambda s, c, l: (0,) * len(shape))
    shapes = [(8, D), (1, 3 * D), (2, 1, FF // 2)] * layers
    return pl.pallas_call(
        prepare_kernel,
        out_shape=[
            jax.ShapeDtypeStruct((seqs * rows, D), bf16),
            jax.ShapeDtypeStruct((D, seqs * rows), bf16),
            jax.ShapeDtypeStruct((seqs * rows, D), f32),
            *[jax.ShapeDtypeStruct(shape, f32) for shape in shapes],
        ],
        grid_spec=pltpu.PrefetchScalarGridSpec(
            num_scalar_prefetch=2,
            grid=(seqs,),
            in_specs=[mine, mine, fixed(small.shape)],
            out_specs=[
                pl.BlockSpec((rows, D), lambda s, c, l: (s, 0)),
                pl.BlockSpec((D, rows), lambda s, c, l: (0, s)),
                pl.BlockSpec((rows, D), lambda s, c, l: (s, 0)),
                *[fixed(shape) for shape in shapes],
            ],
        ),
        compiler_params=pltpu.CompilerParams(
            dimension_semantics=("arbitrary",), vmem_limit_bytes=48 << 20
        ),
        cost_estimate=cost(3),
        name="prepare",
    )(core, lengths, tokens, cotangent, small)


def pack_kernel(core, *refs, counts):
    out = refs[-1]
    squares = refs[-2]
    at = 0
    for layer_at, count in enumerate(counts):
        value_sum, first_small, second_small, *bias_sums = refs[at : at + 3 + count]
        at += 3 + count
        row = slice(layer_at, layer_at + 1)

        def put(place, values, start=0):
            first = bounds[place] + start
            out[row, first : first + values.shape[1]] = values

        total = value_sum[0, 0:1]
        for seq in range(1, value_sum.shape[0]):
            total = total + value_sum[seq, 0:1]
        for half, values in enumerate(swapped(core[0], total)):
            put(0, values, half * (D // 2))
        put(1, first_small[0:1])
        width = bias_sums[0].shape[2]
        for place, bias_sum in enumerate(bias_sums):
            own, other = bias_sum[0, 0:1], bias_sum[1, 0:1]
            put(2, jnp.where(core[0] == 0, own, other), place * width)
            put(2, jnp.where(core[0] == 0, other, own), FF // 2 + place * width)
        put(3, second_small[0:1])
        for place, values in ((4, first_small[1:2]), (5, first_small[2:3])):
            put(place, values)
        for place, values in ((6, second_small[1:2]), (7, second_small[2:3])):
            put(place, values)
        out[row, bounds[-1] :] = squares[row]


def pack(core, layers, squares):
    arrays = [array for value, first, second, sums in layers for array in (value, first, second, *sums)]
    arrays.append(squares)
    return pl.pallas_call(
        partial(pack_kernel, counts=[len(sums) for _, _, _, sums in layers]),
        out_shape=jax.ShapeDtypeStruct((len(layers), bounds[-1] + 128), f32),
        grid_spec=pltpu.PrefetchScalarGridSpec(
            num_scalar_prefetch=1,
            grid=(1,),
            in_specs=[pl.BlockSpec(array.shape, lambda i, c, n=array.ndim: (0,) * n) for array in arrays],
            out_specs=pl.BlockSpec((len(layers), bounds[-1] + 128), lambda i, c: (0, 0)),
        ),
        compiler_params=pltpu.CompilerParams(dimension_semantics=("arbitrary",)),
        cost_estimate=cost(2),
        name="pack",
    )(core, *arrays)


def head_mask(width, scale):
    lane = lax.broadcasted_iota(jnp.int32, (1, 128), 1)
    return [jnp.where(lane // 64 == head, scale, 0.0).astype(bf16) for head in range(2)]

def attend_forward_kernel(core, lengths, *refs, depth):
    queries, keys, value_rows = refs[:depth], refs[depth:2*depth], refs[2*depth]
    context, log_norm = refs[2*depth+1:]
    length = lengths[core[0] * pl.num_programs(0) + pl.program_id(0)]
    key_all = [k[...] for k in keys]
    key_all = jnp.concatenate(key_all, axis=1) if depth>1 else key_all[0]
    turned = value_rows[...].T
    rows = key_all.shape[0]
    valid = lax.broadcasted_iota(jnp.int32, (rows, rows), 0) < length
    scaled = head_mask(64, 0.125)
    halves = []
    for head in range(2):
        query = [q[...] * scaled[head] for q in queries]
        query = jnp.concatenate(query, axis=1) if depth>1 else query[0]
        score = jnp.where(valid, dot_nt(key_all, query), masked_score)
        top = jnp.max(score, axis=0, keepdims=True)
        weight = jnp.exp(score - top)
        total = jnp.sum(weight, axis=0, keepdims=True)
        low = (weight * (1.0 / total)).astype(bf16)
        halves.append(jnp.dot(turned[64*head:64*head+64], low, preferred_element_type=f32))
        log_norm[0, head:head+1] = top + jnp.log(total)
    context[...] = jnp.concatenate(halves, axis=0).T.astype(bf16)

def attend_forward(core, lengths, projections, rows):
    depth=len(projections)
    seqs = lengths.shape[0] // 2
    pairs=D//128
    col=lambda off: pl.BlockSpec((rows,128), lambda s,j,c,l,off=off:(s,off*pairs+j))
    return pl.pallas_call(
        partial(attend_forward_kernel, depth=depth),
        out_shape=[jax.ShapeDtypeStruct((seqs*rows,D),bf16), jax.ShapeDtypeStruct((seqs*pairs,8,rows),f32)],
        grid_spec=pltpu.PrefetchScalarGridSpec(num_scalar_prefetch=2, grid=(seqs,pairs),
            in_specs=[col(0)]*depth+[col(1)]*depth+[col(2)],
            out_specs=[pl.BlockSpec((rows,128),lambda s,j,c,l:(s,j)), pl.BlockSpec((1,8,rows),lambda s,j,c,l:(s*pairs+j,0,0))]),
        compiler_params=pltpu.CompilerParams(dimension_semantics=("arbitrary","arbitrary"),vmem_limit_bytes=48<<20),
        cost_estimate=cost(10),
        name="attend_forward",
    )(core, lengths, *projections, *projections, projections[0])

def attend_backward_kernel(core, lengths, *refs, depth, with_later, keep_total):
    queries, keys, value_rows = refs[:depth], refs[depth:2*depth], refs[2*depth]
    log_norm, context_grad = refs[2*depth+1:2*depth+3]
    at = 2*depth+3
    if with_later:
        later = refs[at]; at+=1
    grads, value_sum = refs[at:at+2]
    if keep_total: total_out = refs[at+2]
    length = lengths[core[0] * pl.num_programs(0) + pl.program_id(0)]
    key_all = [k[...] for k in keys]
    key_all = jnp.concatenate(key_all, axis=1) if depth>1 else key_all[0]
    rows = key_all.shape[0]
    valid = lax.broadcasted_iota(jnp.int32, (rows, rows), 0) < length
    scaled = head_mask(64, 0.125)
    plain = head_mask(64, 1.0)
    key_turned = (keys[0][...] * 0.125).astype(bf16).T
    query_halves = []
    key_grad = value_grad = None
    for head in range(2):
        query = [q[...] * scaled[head] for q in queries]
        query_own = query[0]
        query = jnp.concatenate(query, axis=1) if depth>1 else query[0]
        score = jnp.where(valid, dot_nt(key_all, query), masked_score)
        soft = jnp.exp(score - log_norm[0, head:head+1])
        grad_rows = context_grad[...] * plain[head]
        soft_grad = dot_nt(value_rows[...], grad_rows)
        product = soft * soft_grad
        total = product - soft * jnp.sum(product, axis=0, keepdims=True)
        if with_later: total = total + later[head]
        if keep_total: total_out[head] = total
        low = total.astype(bf16)
        query_halves.append(jnp.dot(key_turned[64*head:64*head+64], low, preferred_element_type=f32))
        kg = jnp.dot(low, query_own, preferred_element_type=f32)
        vg = jnp.dot(soft.astype(bf16), grad_rows, preferred_element_type=f32)
        key_grad = kg if key_grad is None else key_grad+kg
        value_grad = vg if value_grad is None else value_grad+vg
    grads[0] = jnp.concatenate(query_halves, axis=0).T.astype(bf16)
    grads[1] = key_grad.astype(bf16)
    grads[2] = value_grad.astype(bf16)
    sums = jnp.sum(value_grad, axis=0, keepdims=True)
    value_sum[0] = jnp.broadcast_to(sums, (8,128))

def attend_backward(core, lengths, projections, log_norm, context_grad, later, keep_total, rows):
    depth=len(projections)
    seqs = lengths.shape[0] // 2
    pairs=D//128
    col=lambda off: pl.BlockSpec((rows,128), lambda s,j,c,l,off=off:(s,off*pairs+j))
    square=pl.BlockSpec((2,rows,rows),lambda s,j,c,l:(s*pairs+j,0,0))
    in_specs=[col(0)]*depth+[col(1)]*depth+[col(2)]+[pl.BlockSpec((1,8,rows),lambda s,j,c,l:(s*pairs+j,0,0)), col(0)]
    args=[*projections,*projections,projections[0],log_norm,context_grad]
    if later is not None:
        in_specs.append(square); args.append(later)
    out_shape=[jax.ShapeDtypeStruct((3,seqs*rows,D),bf16), jax.ShapeDtypeStruct((seqs,8,D),f32)]
    out_specs=[pl.BlockSpec((3,rows,128),lambda s,j,c,l:(0,s,j)), pl.BlockSpec((1,8,128),lambda s,j,c,l:(s,0,j))]
    if keep_total:
        out_shape.append(jax.ShapeDtypeStruct((seqs*pairs*2,rows,rows),f32)); out_specs.append(square)
    return pl.pallas_call(
        partial(attend_backward_kernel, depth=depth, with_later=later is not None, keep_total=keep_total),
        out_shape=out_shape,
        grid_spec=pltpu.PrefetchScalarGridSpec(num_scalar_prefetch=2, grid=(seqs,pairs), in_specs=in_specs, out_specs=out_specs),
        compiler_params=pltpu.CompilerParams(dimension_semantics=("arbitrary","arbitrary"),vmem_limit_bytes=48<<20),
        cost_estimate=cost(17),
        name="attend_backward",
    )(core, lengths, *args)


def adam_parts(gradient, first, second, factor):
    clipped = gradient * factor
    first_new = beta_one * first + (1.0 - beta_one) * clipped
    second_new = beta_two * second + (1.0 - beta_two) * clipped * clipped
    first_hat = first_new / (1.0 - beta_one**step_count)
    second_hat = second_new / (1.0 - beta_two**step_count)
    return (first_new, second_new, first_hat / (jnp.sqrt(second_hat) + adam_eps))


def local(
    tokens,
    cotangent,
    lengths,
    proj_weight,
    out_weight,
    up_weight,
    down_weight,
    small_params,
    proj_first,
    proj_second,
    out_first,
    out_second,
    up_first,
    up_second,
    down_first,
    down_second,
    small_first,
    small_second,
):
    layers = proj_weight.shape[0]
    seq_len = tokens.shape[0] // lengths.shape[0]
    half_d = proj_weight.shape[3]
    half_ff = up_weight.shape[2]
    row_count = proj_weight.shape[1]
    parts = lax.axis_size("dp")
    links = Links(parts)
    places = lax.axis_index("tensor") * parts + lax.axis_index("dp")
    places = lax.dynamic_index_in_dim(
        jnp.asarray(links.table.reshape(2 * parts, 6, parts + 1)), places, 0, keepdims=False
    )
    exchanged, by_zone = (places, 0), (places, 1)
    in_turn = (places, 2)
    turns = {(0, "proj"): by_zone, (0, "ff"): by_zone, (1, "proj"): in_turn, (1, "ff"): in_turn}
    core = lax.axis_index("tensor")[None].astype(jnp.int32)

    table = {"proj": proj_weight, "out": out_weight, "up": up_weight, "down": down_weight}
    groups = [
        [(0, "proj")], [(0, "out"), (0, "up"), (0, "down")], [(1, "proj")], [(1, "out"), (1, "up"), (1, "down")],
    ]
    gathers = []
    for group in groups:
        share = [table[kind][layer_at].reshape(row_count, -1).astype(bf16) for layer_at, kind in group]
        gathers.append(links.gather(jnp.concatenate(share, axis=1) if len(share) > 1 else share[0]))
    one, two, three, four = gathers
    zone = [[first + 4 * step for step in range(parts // 4)] for first in range(4)]
    near = jnp.concatenate([move["held"][0] for move in (one, two)], axis=1)
    near = lax.all_gather(near, "dp", axis_index_groups=zone)
    prepared = prepare(core, lengths, tokens, cotangent, small_params)
    last = jnp.concatenate([move.pop("held")[0] for move in (three, four)], axis=1)
    near, last, prepared = lax.optimization_barrier((near, last, prepared))
    hidden, hidden_turned, grad_rows, *prepared = prepared
    vectors, value_bias, up_bias = prepared[0::3], prepared[1::3], prepared[2::3]
    last = lax.all_gather(last, ("dp", "tensor")).reshape(parts, 2, row_count, -1)
    three["pair"], four["pair"] = (last, last, 0), (last, last, 3 * half_d)
    one.update(links.gather_last(near[:, :, : 3 * half_d]))
    two.update(links.gather_last(near[:, :, 3 * half_d :]))
    links.advance([one])
    links.advance([one])
    (hidden,) = links.advance([two], (hidden,))

    def gathered(layer_at, kind):
        for group, move in zip(groups, gathers):
            widths = [math.prod(table[name].shape[2:]) for _, name in group]
            if (layer_at, kind) in group:
                while links.running(move):
                    links.advance([move])
                if "held" in move:
                    links.pair(move)
                own, other, first = move["pair"]
                return own, other, first + sum(widths[: group.index((layer_at, kind))])

    saved = []
    hidden_low = hidden
    masters = (proj_weight, out_weight, up_weight, down_weight)
    for layer_at in range(layers):
        projected = project(
            turns[layer_at, "proj"], hidden_low, gathered(layer_at, "proj"), value_bias[layer_at]
        )
        if layer_at == 0:
            (projected,) = links.advance([two], (projected,))
        chain = [projected] + [earlier["projected"] for earlier in reversed(saved)]
        context, log_norm = attend_forward(core, lengths, chain, seq_len)
        if layer_at == 0:
            late_masters, context = lax.optimization_barrier((masters, context))
            squares = [jnp.sum(one * one, axis=tuple(range(1, one.ndim))) for one in late_masters]
            squares = jnp.pad(jnp.stack(squares, axis=1), ((0, 0), (0, 124)))
            squares, context = links.pair(two, (squares, context))
        kept = {
            "input_turned": hidden_turned, "projected": projected, "log_norm": log_norm, "context": context,
        }
        (
            kept["first_in"], kept["first_low"], kept["first_turned"], kept["active"], kept["slope"], hidden, *rest,
        ) = feed_forward(
            turns[layer_at, "ff"], hidden, context, gathered(layer_at, "out"), gathered(layer_at, "up"),
            gathered(layer_at, "down"), up_bias[layer_at], vectors[layer_at],
            grad_rows if layer_at == layers - 1 else None,
        )
        if layer_at == layers - 1:
            turned_grad = rest
        else:
            kept["second_in"], hidden_low, hidden_turned = rest
        saved.append(kept)

    smalls = [None] * layers
    later_total = None
    before = []
    for layer_at in reversed(range(layers)):
        kept = saved[layer_at]
        places_ff = turns[layer_at, "ff"]
        first_grad, down_low, down_turned, second_small = turned_grad
        own, other, bias_sum, first_grad = feed_backward(
            places_ff, first_grad, down_low, down_turned,
            [kept[name] for name in ("first_turned", "active", "slope")],
            gathered(layer_at, "up"), gathered(layer_at, "down"), parts,
        )
        ff_sum = links.scatter(own, other)
        (first_grad,) = links.advance(before + [ff_sum], (first_grad,))
        first_in_grad, out_in_turned, context_grad, first_small = context_backward(
            places_ff, first_grad, kept["first_in"], gathered(layer_at, "out"), vectors[layer_at]
        )
        (context_grad,) = links.advance([ff_sum] + before[1:], (context_grad,))
        chain = [kept["projected"]] + [earlier["projected"] for earlier in reversed(saved[:layer_at])]
        results = attend_backward(
            core, lengths, chain, kept["log_norm"], context_grad, later_total, layer_at > 0, seq_len
        )
        head_grads, value_sum = results[:2]
        later_total = results[2] if layer_at > 0 else None
        smalls[layer_at] = (value_sum, first_small, second_small, [bias_sum])
        if layer_at == 0:
            (head_grads,) = links.advance(before, (head_grads,))
            packed = pack(core, smalls, squares)
            packed, head_grads = links.advance([ff_sum], (packed, head_grads))
            packed = links.total(packed)
        attention_sum = links.scatter(
            *projection_grads(
                exchanged, out_in_turned, kept["context"], kept["input_turned"], head_grads, parts
            )
        )
        if layer_at > 0:
            (head_grads,) = links.advance([ff_sum, attention_sum], (head_grads,))
            turned_grad = project_backward(
                turns[layer_at, "proj"], head_grads, first_in_grad, gathered(layer_at, "proj"),
                (saved[layer_at - 1]["second_in"], vectors[layer_at - 1]),
            )
            turned_grad = links.advance([attention_sum], turned_grad)
        else:
            links.advance([attention_sum, packed])
            (head_grads,) = links.advance([attention_sum, before[1]], (head_grads,))
            (grad_rows,) = project_backward(
                turns[layer_at, "proj"], head_grads, first_in_grad, gathered(layer_at, "proj")
            )
        before += [ff_sum, attention_sum]

    width = small_params.shape[1]
    (grad_rows,) = links.advance([ff_sum, attention_sum], (grad_rows,))
    later_sums, grad_rows = links.settle(before[:2], grad_rows)
    sent = (links.sibling(grad_rows), links.sibling(hidden))
    links.advance([packed])
    links.advance([attention_sum])
    links.advance([ff_sum])
    hidden, grad_rows = join(core, ((hidden, sent[1]), (grad_rows, sent[0])))
    hidden, grad_rows = links.advance([packed], (hidden, grad_rows))
    links.advance([attention_sum])
    packed = links.finish([packed])[0]
    small_grad = packed[:, :width]
    weight_square = packed[:, width : width + 4].T

    ff_sums, attention_sums = (
        jnp.stack([earlier, later]) for earlier, later in zip(links.finish([ff_sum, attention_sum]), later_sums)
    )
    grads = (
        attention_sums[:, 1:].transpose(0, 2, 1, 3), attention_sums[:, 0], ff_sums[:, 1], ff_sums[:, 0],
    )
    firsts = (proj_first, out_first, up_first, down_first)
    seconds = (proj_second, out_second, up_second, down_second)
    square_part = sum(jnp.sum(grad * grad) for grad in grads)
    square_big = links.finish([links.total(jnp.broadcast_to(square_part, (8, 128)))])[0][0, 0]
    grad_norm = jnp.sqrt(square_big + jnp.sum(small_grad * small_grad))
    factor = clip_norm / jnp.maximum(grad_norm, clip_norm)
    moments = []
    updates = []
    for kind_at in range(4):
        first_new, second_new, direction = adam_parts(
            grads[kind_at], firsts[kind_at], seconds[kind_at], factor
        )
        moments.append((first_new, second_new))
        updates.append(direction + decay_rate * masters[kind_at])
    update_square = jnp.stack(
        [jnp.sum(update * update, axis=tuple(range(1, update.ndim))) for update in updates]
    )
    update_square = jnp.pad(update_square.reshape(1, -1), ((0, 7), (0, 128 - 4 * layers)))
    update_square = links.finish([links.total(update_square)])[0]
    update_square = update_square[0, : 4 * layers].reshape(4, layers)
    ratio = jnp.sqrt(weight_square) / jnp.sqrt(update_square)

    outputs = [hidden, grad_rows, grad_norm]
    for kind_at in range(4):
        master = masters[kind_at]
        scaled = ratio[kind_at].reshape((-1,) + (1,) * (master.ndim - 1))
        outputs += [
            moments[kind_at][0],
            moments[kind_at][1],
            master - matrix_rate * scaled * updates[kind_at],
        ]
    small_first_new, small_second_new, small_direction = adam_parts(
        small_grad, small_first, small_second, factor
    )
    outputs += [small_first_new, small_second_new, small_params - vector_rate * small_direction]
    return tuple(outputs)


def solution(mesh):
    proj = P(None, "dp", None, "tensor")
    matrix = P(None, "dp", "tensor")
    rows = P("dp", None)
    return jax.shard_map(
        local,
        mesh=mesh,
        in_specs=(rows, rows, P("dp"), proj, matrix, matrix, matrix, P())
        + (proj, proj)
        + (matrix,) * 6
        + (P(), P()),
        out_specs=(rows, rows, P()) + (proj,) * 3 + (matrix,) * 9 + (P(),) * 3,
        check_vma=False,
    )
```

```python
from functools import partial
import math

import jax
import jax.numpy as jnp
import numpy as np
from jax import lax
from jax.experimental import pallas as pl
from jax.experimental.pallas import tpu as pltpu
from jax.sharding import PartitionSpec as P

D = 768
HEADS = 12
FF = 3072


beta_one = 0.9
beta_two = 0.999
adam_eps = 1e-06
decay_rate = 0.01
matrix_rate = 1.0
vector_rate = 0.3
clip_norm = 1.0
step_count = 10.0
norm_eps = 1e-06
masked_score = -1e30

f32 = jnp.float32
bf16 = jnp.bfloat16


class Links:
    def __init__(self, parts):
        self.parts = parts
        count = parts.bit_length() - 1
        high = list(range(count - 1, -1, -1))
        other = high[:-2] + high[-2:][::-1]
        self.orders = (other, high)
        self.inverse = np.zeros((2, parts), np.int32)
        for core in range(2):
            for place in range(parts):
                mask = 0
                for stage in range(count):
                    if (place >> stage) & 1:
                        mask |= 1 << self.orders[core][stage]
                self.inverse[core, mask] = place
        self.stages = count
        self.last = ()
        every = np.arange(parts)
        self.table = np.zeros((2, parts, 4, parts + 1), np.int32)
        for core in range(2):
            for at in range(parts):
                for half, side in enumerate((core, 1 - core)):
                    rows = (self.inverse[side, every ^ at], every)
                    for kind, row in enumerate(rows):
                        self.table[core, at, 2 * kind + half, :parts] = row
                        self.table[core, at, 2 * kind + half, parts] = side

    def swap(self, value, *stages):
        pairs = []
        for core in range(2):
            flip = sum(1 << self.orders[core][stage] for stage in stages)
            pairs += [(2 * at + core, 2 * (at ^ flip) + core) for at in range(self.parts)]
        return lax.ppermute(value, ("dp", "tensor"), pairs)

    def sibling(self, value):
        return lax.ppermute(value, "tensor", [(0, 1), (1, 0)])

    def gather(self, share):
        return {"held": share[None], "stage": 0}

    def total(self, value):
        return {"value": value, "step": 0}

    def scatter(self, own, other):
        return {"pieces": [own], "other": other, "size": self.parts, "stage": self.stages}

    def advance(self, moves, rest=()):
        moves = [move for move in moves if self.running(move)]
        if not moves:
            return rest
        mine, rest, self.last = lax.optimization_barrier(
            ([move.get("held", move.get("value", move.get("pieces"))) for move in moves], rest, self.last)
        )
        sending = []
        for move, value in zip(moves, mine):
            if "held" in move:
                come = move.pop("come", None)
                sending.append(value if come is None else jnp.concatenate([value, come], axis=0))
            elif "value" in move:
                sending.append(self.summed(value, move.pop("come", [])))
            elif "other" in move:
                sending.append(move["other"])
            else:
                half, size = move["size"] // 2, move["size"]
                move["pieces"] = value + move.pop("come")
                sending.append(sum(piece[half:size].astype(f32) for piece in move["pieces"]).astype(bf16))
        sending, rest, _ = lax.optimization_barrier((sending, rest, self.last))
        self.last = sending[0]
        for move, value in zip(moves, sending):
            if "held" in move:
                move["held"] = value
                move["come"] = self.swap(value, move["stage"])
                move["stage"] += 1
            elif "value" in move:
                move["value"] = value
                low, high = 2 * move["step"] - 2, 2 * move["step"] - 1
                if move["step"] == 0:
                    move["come"] = [self.sibling(value)]
                elif high < self.stages:
                    move["come"] = [self.swap(value, low), self.swap(value, high), self.swap(value, low, high)]
                else:
                    move["come"] = [self.swap(value, low)]
                move["step"] += 1
            elif "other" in move:
                move["come"] = [self.sibling(value)]
                del move["other"]
            else:
                move["size"] //= 2
                move["stage"] -= 1
                move["come"] = [self.swap(value, move["stage"])]
        return rest

    def pair(self, move, rest=()):
        while self.running(move):
            self.advance([move])
        held, rest = lax.optimization_barrier((move.pop("held"), rest))
        held = jnp.concatenate([held, move.pop("come")], axis=0)
        move["pair"] = (held, self.sibling(held), 0)
        return rest

    def summed(self, value, come):
        if len(come) == 3:
            return (value + come[0]) + (come[1] + come[2])
        return value + come[0] if come else value

    def running(self, move):
        return move.get("stage", 0) < self.stages if "held" in move else move.get("size", 1) > 1 or 2 * move.get("step", self.stages) < self.stages + 2

    def settle(self, moves, rest):
        pieces, rest = lax.optimization_barrier(([move["pieces"] for move in moves], rest))
        for move, value in zip(moves, pieces):
            move["pieces"] = value
        return lax.optimization_barrier((self.finish(moves), rest))

    def finish(self, moves):
        for move in moves:
            while self.running(move):
                self.advance([move])
        if "value" in moves[0]:
            return [self.summed(move["value"], move["come"]) for move in moves]
        return [sum(piece[0].astype(f32) for piece in move["pieces"] + move["come"]) for move in moves]


def dot_nt(left, right):
    return lax.dot_general(left, right, (((1,), (1,)), ((), ())), preferred_element_type=f32)


def dot_nn(left, right):
    return jnp.dot(left, right, preferred_element_type=f32)


def in_order(blocks, place_of):
    some = (0,) if len(blocks.shape) == 4 else ()
    return jnp.concatenate([blocks[(place_of[block], *some)] for block in range(blocks.shape[0])], axis=0)


def put_blocks(out, at, product, place_of):
    parts, _, rows, _ = out.shape
    for block in range(parts):
        out[place_of[block], at] = product[block * rows : (block + 1) * rows]


def norm_parts(values):
    centered = values - jnp.mean(values, axis=1, keepdims=True)
    variance = jnp.mean(centered * centered, axis=1, keepdims=True)
    scale = lax.rsqrt(variance + norm_eps)
    return centered * scale, scale


def norm_backward(values, gain, grad):
    unit, scale = norm_parts(values)
    scaled = grad * gain
    inner = scaled - jnp.mean(scaled, axis=1, keepdims=True)
    result = scale * (inner - unit * jnp.mean(scaled * unit, axis=1, keepdims=True))
    return result, jnp.sum(grad * unit, axis=0, keepdims=True), jnp.sum(grad, axis=0, keepdims=True)


def project_kernel(own_at, other_at, own_to, other_to, rows_in, own, other, bias, out):
    width = own.shape[-1]
    for half, (blocks, place_of) in enumerate(((own, own_at), (other, other_at))):
        weight = in_order(blocks, place_of)
        span = slice(half * width, (half + 1) * width)
        out[:, span] = (dot_nn(rows_in[...], weight) + bias[:, span]).astype(bf16)


def cost(microseconds):
    return pl.CostEstimate(flops=0, bytes_accessed=int(microseconds * 2.5e6), transcendentals=0)


class Row:
    def __init__(self, table, row):
        self.table, self.row = table, row

    def __getitem__(self, place):
        return self.table[self.row, place]


def call(kernel, places, grid, ins, outs, scratch=(), name=None, time=1):
    table, pair = places
    weight_rows = lambda at: (Row(at, 2 * pair), Row(at, 2 * pair + 1))
    spec = lambda block, index: pl.BlockSpec(block, lambda i, at: index(i, weight_rows(at)))
    return pl.pallas_call(
        lambda at, *refs: kernel(*weight_rows(at), Row(at, 0), Row(at, 1), *refs),
        out_shape=[jax.ShapeDtypeStruct(shape, kind) for shape, kind, _, _ in outs],
        grid_spec=pltpu.PrefetchScalarGridSpec(
            num_scalar_prefetch=1,
            grid=(grid,),
            in_specs=[spec(block, index) for _, block, index in ins],
            out_specs=[spec(block, index) for _, _, block, index in outs],
            scratch_shapes=list(scratch),
        ),
        compiler_params=pltpu.CompilerParams(
            dimension_semantics=("arbitrary",), vmem_limit_bytes=44 << 20
        ),
        cost_estimate=cost(time),
        name=name,
    )(table, *[array for array, _, _ in ins])


def whole(array):
    return (array, array.shape, lambda i, at: (0,) * array.ndim)


def weight_tiles(pair, tile, count=1):
    own, other, first = pair
    tiles = []
    for half, array in enumerate((own, other)):
        parts, rows = array.shape[0], array.shape[-2]
        column = lambda i: first // tile + jnp.clip(i, 0, count - 1)
        if array.ndim == 3:
            tiles.append((array, (parts, rows, tile), lambda i, at: (0, 0, column(i))))
        else:
            index = lambda i, at, half=half, parts=parts: (0, at[half][parts], 0, column(i))
            tiles.append((array, (parts, 1, rows, tile), index))
    return tiles


def project(places, rows_in, pair, bias):
    rows = rows_in.shape[0]
    half = D // 2
    return call(
        project_kernel, places, 3,
        [whole(rows_in), *weight_tiles(pair, half, 3), (bias, (1, D), lambda i, at: (0, i))],
        [((rows, 3 * D), bf16, (rows, D), lambda i, at: (0, i))],
        name="project",
        time=7,
    )[0]


def feed_forward_kernel(
    own_at, other_at, own_to, other_to, hidden, context, out_own, out_other, up_own, up_other, down_own, down_other,
    bias_up, vectors, *refs, with_grad,
):
    if with_grad:
        grad, first_in, first_turned, active, slope, hidden_new, *turned, first_low, second_in = refs
        total = second_in
    else:
        first_in, first_turned, active, slope, hidden_new, second_in, hidden_low, hidden_turned, first_low = refs
        total = second_in
    step = pl.program_id(0)
    halves = ((own_at, up_own, down_own), (other_at, up_other, down_other))
    half_d = D // 2

    @pl.when(step == 0)
    def _():
        attended = dot_nt(context[:, :half_d], in_order(out_own, own_at))
        attended += dot_nt(context[:, half_d:], in_order(out_other, other_at))
        values = hidden[...].astype(f32) + attended + vectors[0:1]
        first_in[...] = values
        unit, _ = norm_parts(values)
        values = unit * vectors[1:2] + vectors[2:3]
        low = values.astype(bf16)
        first_low[...] = low
        first_turned[...] = low.T
        total[...] = values + vectors[3:4]

    for half, (place_of, up, down) in enumerate(halves):
        before = dot_nn(first_low[...], in_order(up, place_of)) + bias_up[half]
        shade = 0.5 * (1.0 + lax.erf(before * (1.0 / math.sqrt(2.0))))
        bell = jnp.exp(-0.5 * before * before) * (1.0 / math.sqrt(2.0 * math.pi))
        low = (before * shade).astype(bf16)
        active[half] = low
        slope[half] = shade + before * bell
        total[...] += dot_nt(low, in_order(down, place_of))

    @pl.when(step == pl.num_programs(0) - 1)
    def _():
        unit, _ = norm_parts(second_in[...])
        values = unit * vectors[4:5] + vectors[5:6]
        hidden_new[...] = values
        if with_grad:
            norm_turn(second_in[...], vectors[4:5], grad[...], *turned)
        else:
            low = values.astype(bf16)
            hidden_low[...] = low
            hidden_turned[...] = low.T


def feed_forward(places, hidden, context, out_pair, up_pair, down_pair, bias_up, vectors, grad=None, tile=512):
    rows = hidden.shape[0]
    half_ff = bias_up.shape[2]
    count = half_ff // tile
    flat = lambda kind: ((rows, D), kind, (rows, D), lambda i, at: (0, 0))
    tiled = lambda kind: ((2, rows, half_ff), kind, (2, rows, tile), lambda i, at: (0, 0, i))
    turned = ((D, rows), bf16, (D, rows), lambda i, at: (0, 0))
    return call(
        partial(feed_forward_kernel, with_grad=grad is not None), places, count,
        [
            whole(hidden),
            whole(context),
            *weight_tiles(out_pair, D // 2),
            *weight_tiles(up_pair, tile, count),
            *weight_tiles(down_pair, tile, count),
            (bias_up, (2, 1, tile), lambda i, at: (0, 0, i)),
            whole(vectors),
            *([] if grad is None else [whole(grad)]),
        ],
        [
            flat(f32), turned, tiled(bf16), tiled(f32), flat(f32),
            *([flat(f32), flat(bf16), turned] if grad is None else norm_turn_outs(rows)),
        ],
        [pltpu.VMEM((rows, D), bf16)] + ([] if grad is None else [pltpu.VMEM((rows, D), f32)]),
        name="feed_forward",
        time=18,
    )


def norm_turn(values, gain, grad, total, down_low, down_turned, small):
    result, gain_grad, shift_grad = norm_backward(values, gain, grad)
    small[...] = jnp.zeros_like(small)
    small[0:1] = jnp.sum(result, axis=0, keepdims=True)
    small[1:2] = gain_grad
    small[2:3] = shift_grad
    total[...] = result
    low = result.astype(bf16)
    down_low[...] = low
    down_turned[...] = low.T


def norm_turn_outs(rows):
    flat = lambda kind: ((rows, D), kind, (rows, D), lambda i, at: (0, 0))
    turned = ((D, rows), bf16, (D, rows), lambda i, at: (0, 0))
    return [flat(f32), flat(bf16), turned, ((8, D), f32, (8, D), lambda i, at: (0, 0))]


def feed_backward_kernel(
    own_at, other_at, own_to, other_to, total_in, down_low, down_turned, first_turned, active, slope,
    up_own, up_other, down_own, down_other, grads_own, grads_other, bias_grads, total,
):
    halves = (
        (own_at, own_to, up_own, down_own, grads_own),
        (other_at, other_to, up_other, down_other, grads_other),
    )

    @pl.when(pl.program_id(0) == 0)
    def _():
        total[...] = total_in[...]

    for half, (place_of, place_to, up, down, grads) in enumerate(halves):
        act_grad = dot_nn(down_low[...], in_order(down, place_of))
        before_grad = act_grad * slope[half]
        bias_grads[half] = jnp.broadcast_to(jnp.sum(before_grad, axis=0, keepdims=True), bias_grads.shape[1:])
        low = before_grad.astype(bf16)
        put_blocks(grads, 0, dot_nn(down_turned[...], active[half]).astype(bf16), place_to)
        put_blocks(grads, 1, dot_nn(first_turned[...], low).astype(bf16), place_to)
        total[...] += dot_nt(low, in_order(up, place_of))


def context_backward_kernel(
    own_at, other_at, own_to, other_to, grad, first_in, out_own, out_other, vectors,
    first_in_grad, out_in_turned, context_grad, small,
):
    half_d = D // 2
    result, gain_grad, shift_grad = norm_backward(first_in[...], vectors[1:2], grad[...])
    small[...] = jnp.zeros_like(small)
    small[0:1] = jnp.sum(result, axis=0, keepdims=True)
    small[1:2] = gain_grad
    small[2:3] = shift_grad
    first_in_grad[...] = result
    low = result.astype(bf16)
    out_in_turned[...] = low.T
    context_grad[:, :half_d] = dot_nn(low, in_order(out_own, own_at)).astype(bf16)
    context_grad[:, half_d:] = dot_nn(low, in_order(out_other, other_at)).astype(bf16)


def context_backward(places, grad, first_in, out_pair, vectors):
    rows = grad.shape[0]
    flat = lambda kind: ((rows, D), kind, (rows, D), lambda i, at: (0, 0))
    return call(
        context_backward_kernel, places, 1,
        [
            whole(grad), whole(first_in),
            *weight_tiles(out_pair, D // 2),
            whole(vectors),
        ],
        [
            flat(f32), ((D, rows), bf16, (D, rows), lambda i, at: (0, 0)), flat(bf16),
            ((8, D), f32, (8, D), lambda i, at: (0, 0)),
        ],
        name="context_backward",
        time=6,
    )


def feed_backward(places, total, down_low, down_turned, kept, up_pair, down_pair, parts, tile=512):
    first_turned, active, slope = kept
    rows = total.shape[0]
    half_ff = active.shape[2]
    count = half_ff // tile
    block_rows = D // parts
    tiled = lambda array: (array, (2, rows, tile), lambda i, at: (0, 0, i))
    grads = ((parts, 2, block_rows, count * tile), bf16, (parts, 2, block_rows, tile), lambda i, at: (0, 0, 0, i))
    return call(
        feed_backward_kernel, places, count,
        [
            whole(total), whole(down_low), whole(down_turned), whole(first_turned), tiled(active), tiled(slope),
            *weight_tiles(up_pair, tile, count),
            *weight_tiles(down_pair, tile, count),
        ],
        [
            grads, grads,
            ((2, 8, count * tile), f32, (2, 8, tile), lambda i, at: (0, 0, i)),
            ((rows, D), f32, (rows, D), lambda i, at: (0, 0)),
        ],
        name="feed_backward",
        time=20,
    )


def projection_grads_kernel(
    own_at, other_at, own_to, other_to, out_in_turned, context, input_turned, head_grads,
    grads_own, grads_other,
):
    step = pl.program_id(0)
    half_d = D // 2
    halves = ((own_to, grads_own), (other_to, grads_other))
    for when, left, right in (
        (step == 0, out_in_turned, lambda span: context[:, span]),
        (step > 0, input_turned, lambda span: head_grads[0, :, span]),
    ):

        @pl.when(when)
        def _():
            for half, (place_to, grads) in enumerate(halves):
                span = slice(half * half_d, (half + 1) * half_d)
                put_blocks(grads, 0, dot_nn(left[...], right(span)).astype(bf16), place_to)


def projection_grads(places, out_in_turned, context, input_turned, head_grads, parts):
    rows = context.shape[0]
    half = D // 2
    block_rows = D // parts
    grads = ((parts, 4, block_rows, half), bf16, (parts, 1, block_rows, half), lambda i, at: (0, i, 0, 0))
    return call(
        projection_grads_kernel, places, 4,
        [
            whole(out_in_turned), whole(context), whole(input_turned),
            (head_grads, (1, rows, D), lambda i, at: (jnp.maximum(i - 1, 0), 0, 0)),
        ],
        [grads, grads],
        name="projection_grads",
        time=9,
    )


def project_backward_kernel(
    own_at, other_at, own_to, other_to, head_grads, first_in_grad, own, other, *refs, with_norm
):
    half_d = D // 2
    step = pl.program_id(0)
    if with_norm:
        second_in, vectors, *turned, input_grad = refs
    else:
        (input_grad,) = refs

    @pl.when(step == 0)
    def _():
        input_grad[...] = first_in_grad[...]

    for half, (place_of, weight) in enumerate(((own_at, own), (other_at, other))):
        low = head_grads[0, :, half * half_d : (half + 1) * half_d]
        input_grad[...] += dot_nt(low, in_order(weight, place_of))

    if with_norm:

        @pl.when(step == pl.num_programs(0) - 1)
        def _():
            norm_turn(second_in[...], vectors[4:5], input_grad[...], *turned)


def project_backward(places, head_grads, first_in_grad, pair, earlier=()):
    rows = first_in_grad.shape[0]
    half = D // 2
    return call(
        partial(project_backward_kernel, with_norm=bool(earlier)), places, 3,
        [
            (head_grads, (1, rows, D), lambda i, at: (i, 0, 0)),
            whole(first_in_grad),
            *weight_tiles(pair, half, 3),
            *map(whole, earlier),
        ],
        norm_turn_outs(rows) if earlier else [((rows, D), f32, (rows, D), lambda i, at: (0, 0))],
        [pltpu.VMEM((rows, D), f32)] if earlier else [],
        name="project_backward",
        time=8,
    )


def join_kernel(core, *refs):
    step = pl.program_id(0)
    count = len(refs) // 3
    for one in range(count):
        own, other, out = refs[2 * one], refs[2 * one + 1], refs[2 * count + one]

        @pl.when(step == core[0])
        def _():
            out[...] = own[...]

        @pl.when(step != core[0])
        def _():
            out[...] = other[...]


def join(core, pairs):
    rows, cols = pairs[0][0].shape
    spec = pl.BlockSpec((rows, cols), lambda i, at: (0, 0))
    return pl.pallas_call(
        join_kernel,
        out_shape=[jax.ShapeDtypeStruct((2 * rows, cols), f32) for _ in pairs],
        grid_spec=pltpu.PrefetchScalarGridSpec(
            num_scalar_prefetch=1,
            grid=(2,),
            in_specs=[spec] * (2 * len(pairs)),
            out_specs=[pl.BlockSpec((rows, cols), lambda i, at: (i, 0)) for _ in pairs],
        ),
        compiler_params=pltpu.CompilerParams(
            dimension_semantics=("arbitrary",), vmem_limit_bytes=44 << 20
        ),
        cost_estimate=cost(4),
        name="join",
    )(core, *[rows_of for pair in pairs for rows_of in pair])


bounds = [0, D, 2 * D, 2 * D + FF, 3 * D + FF, 4 * D + FF, 5 * D + FF, 6 * D + FF, 7 * D + FF]


def swapped(core, vector):
    half = vector.shape[1] // 2
    first, second = vector[:, :half], vector[:, half:]
    return jnp.where(core == 0, first, second), jnp.where(core == 0, second, first)


def prepare_kernel(core, lengths, tokens, cotangent, small, tokens_own, tokens_turned, grad, *outs):
    step = pl.program_id(0)
    length = lengths[core[0] * pl.num_programs(0) + step]
    tokens_own[...] = tokens[...]
    tokens_turned[...] = tokens[...].T
    valid = lax.broadcasted_iota(jnp.int32, grad.shape, 0) < length
    grad[...] = jnp.where(valid, cotangent[...].astype(f32), 0.0)

    @pl.when(step == 0)
    def _():
        for layer_at in range(small.shape[0]):
            vectors, value_bias, up_bias = outs[3 * layer_at : 3 * layer_at + 3]
            part = lambda place: small[layer_at : layer_at + 1, bounds[place] : bounds[place + 1]]
            vectors[...] = jnp.zeros_like(vectors)
            for row, place in enumerate((1, 4, 5, 3, 6, 7)):
                vectors[row : row + 1] = part(place)
            value_bias[...] = jnp.zeros_like(value_bias)
            first, second = swapped(core[0], part(0))
            value_bias[:, 2 * D : 2 * D + D // 2] = first
            value_bias[:, 2 * D + D // 2 :] = second
            up_bias[0], up_bias[1] = swapped(core[0], part(2))


def prepare(core, lengths, tokens, cotangent, small):
    layers = small.shape[0]
    seqs = lengths.shape[0] // 2
    rows = tokens.shape[0] // lengths.shape[0]
    mine = pl.BlockSpec((rows, D), lambda s, c, l: (c[0] * seqs + s, 0))
    fixed = lambda shape: pl.BlockSpec(shape, lambda s, c, l: (0,) * len(shape))
    shapes = [(8, D), (1, 3 * D), (2, 1, FF // 2)] * layers
    return pl.pallas_call(
        prepare_kernel,
        out_shape=[
            jax.ShapeDtypeStruct((seqs * rows, D), bf16),
            jax.ShapeDtypeStruct((D, seqs * rows), bf16),
            jax.ShapeDtypeStruct((seqs * rows, D), f32),
            *[jax.ShapeDtypeStruct(shape, f32) for shape in shapes],
        ],
        grid_spec=pltpu.PrefetchScalarGridSpec(
            num_scalar_prefetch=2,
            grid=(seqs,),
            in_specs=[mine, mine, fixed(small.shape)],
            out_specs=[
                pl.BlockSpec((rows, D), lambda s, c, l: (s, 0)),
                pl.BlockSpec((D, rows), lambda s, c, l: (0, s)),
                pl.BlockSpec((rows, D), lambda s, c, l: (s, 0)),
                *[fixed(shape) for shape in shapes],
            ],
        ),
        compiler_params=pltpu.CompilerParams(
            dimension_semantics=("arbitrary",), vmem_limit_bytes=24 << 20
        ),
        cost_estimate=cost(3),
        name="prepare",
    )(core, lengths, tokens, cotangent, small)


def pack_kernel(core, *refs, counts):
    out = refs[-1]
    squares = refs[-2]
    at = 0
    for layer_at, count in enumerate(counts):
        value_sum, first_small, second_small, *bias_sums = refs[at : at + 3 + count]
        at += 3 + count
        row = slice(layer_at, layer_at + 1)

        def put(place, values, start=0):
            first = bounds[place] + start
            out[row, first : first + values.shape[1]] = values

        total = value_sum[0, 0:1]
        for seq in range(1, value_sum.shape[0]):
            total = total + value_sum[seq, 0:1]
        for half, values in enumerate(swapped(core[0], total)):
            put(0, values, half * (D // 2))
        put(1, first_small[0:1])
        width = bias_sums[0].shape[2]
        for place, bias_sum in enumerate(bias_sums):
            own, other = bias_sum[0, 0:1], bias_sum[1, 0:1]
            put(2, jnp.where(core[0] == 0, own, other), place * width)
            put(2, jnp.where(core[0] == 0, other, own), FF // 2 + place * width)
        put(3, second_small[0:1])
        for place, values in ((4, first_small[1:2]), (5, first_small[2:3])):
            put(place, values)
        for place, values in ((6, second_small[1:2]), (7, second_small[2:3])):
            put(place, values)
        out[row, bounds[-1] :] = squares[row]


def pack(core, layers, squares):
    arrays = [array for value, first, second, sums in layers for array in (value, first, second, *sums)]
    arrays.append(squares)
    return pl.pallas_call(
        partial(pack_kernel, counts=[len(sums) for _, _, _, sums in layers]),
        out_shape=jax.ShapeDtypeStruct((len(layers), bounds[-1] + 128), f32),
        grid_spec=pltpu.PrefetchScalarGridSpec(
            num_scalar_prefetch=1,
            grid=(1,),
            in_specs=[pl.BlockSpec(array.shape, lambda i, c, n=array.ndim: (0,) * n) for array in arrays],
            out_specs=pl.BlockSpec((len(layers), bounds[-1] + 128), lambda i, c: (0, 0)),
        ),
        compiler_params=pltpu.CompilerParams(dimension_semantics=("arbitrary",)),
        cost_estimate=cost(2),
        name="pack",
    )(core, *arrays)


def head_mask(width, scale):
    lane = lax.broadcasted_iota(jnp.int32, (1, 128), 1)
    return [jnp.where(lane // 64 == head, scale, 0.0).astype(bf16) for head in range(2)]

def attend_forward_kernel(core, lengths, *refs, depth):
    queries, keys, value_rows = refs[:depth], refs[depth:2*depth], refs[2*depth]
    context, log_norm = refs[2*depth+1:]
    length = lengths[core[0] * pl.num_programs(0) + pl.program_id(0)]
    key_all = [k[...] for k in keys]
    key_all = jnp.concatenate(key_all, axis=1) if depth>1 else key_all[0]
    turned = value_rows[...].T
    rows = key_all.shape[0]
    valid = lax.broadcasted_iota(jnp.int32, (rows, rows), 0) < length
    scaled = head_mask(64, 0.125)
    halves = []
    for head in range(2):
        query = [q[...] * scaled[head] for q in queries]
        query = jnp.concatenate(query, axis=1) if depth>1 else query[0]
        score = jnp.where(valid, dot_nt(key_all, query), masked_score)
        top = jnp.max(score, axis=0, keepdims=True)
        weight = jnp.exp(score - top)
        total = jnp.sum(weight, axis=0, keepdims=True)
        low = (weight * (1.0 / total)).astype(bf16)
        halves.append(jnp.dot(turned[64*head:64*head+64], low, preferred_element_type=f32))
        log_norm[0, head:head+1] = top + jnp.log(total)
    context[...] = jnp.concatenate(halves, axis=0).T.astype(bf16)

def attend_forward(core, lengths, projections, rows):
    depth=len(projections)
    seqs = lengths.shape[0] // 2
    pairs=D//128
    col=lambda off: pl.BlockSpec((rows,128), lambda s,j,c,l,off=off:(s,off*pairs+j))
    return pl.pallas_call(
        partial(attend_forward_kernel, depth=depth),
        out_shape=[jax.ShapeDtypeStruct((seqs*rows,D),bf16), jax.ShapeDtypeStruct((seqs*pairs,8,rows),f32)],
        grid_spec=pltpu.PrefetchScalarGridSpec(num_scalar_prefetch=2, grid=(seqs,pairs),
            in_specs=[col(0)]*depth+[col(1)]*depth+[col(2)],
            out_specs=[pl.BlockSpec((rows,128),lambda s,j,c,l:(s,j)), pl.BlockSpec((1,8,rows),lambda s,j,c,l:(s*pairs+j,0,0))]),
        compiler_params=pltpu.CompilerParams(dimension_semantics=("arbitrary","arbitrary"),vmem_limit_bytes=24 << 20),
        cost_estimate=cost(10),
        name="attend_forward",
    )(core, lengths, *projections, *projections, projections[0])

def attend_backward_kernel(core, lengths, *refs, depth, with_later, keep_total):
    queries, keys, value_rows = refs[:depth], refs[depth:2*depth], refs[2*depth]
    log_norm, context_grad = refs[2*depth+1:2*depth+3]
    at = 2*depth+3
    if with_later:
        later = refs[at]; at+=1
    grads, value_sum = refs[at:at+2]
    if keep_total: total_out = refs[at+2]
    length = lengths[core[0] * pl.num_programs(0) + pl.program_id(0)]
    key_all = [k[...] for k in keys]
    key_all = jnp.concatenate(key_all, axis=1) if depth>1 else key_all[0]
    rows = key_all.shape[0]
    valid = lax.broadcasted_iota(jnp.int32, (rows, rows), 0) < length
    scaled = head_mask(64, 0.125)
    plain = head_mask(64, 1.0)
    key_turned = (keys[0][...] * 0.125).astype(bf16).T
    query_halves = []
    key_grad = value_grad = None
    for head in range(2):
        query = [q[...] * scaled[head] for q in queries]
        query_own = query[0]
        query = jnp.concatenate(query, axis=1) if depth>1 else query[0]
        score = jnp.where(valid, dot_nt(key_all, query), masked_score)
        soft = jnp.exp(score - log_norm[0, head:head+1])
        grad_rows = context_grad[...] * plain[head]
        soft_grad = dot_nt(value_rows[...], grad_rows)
        product = soft * soft_grad
        total = product - soft * jnp.sum(product, axis=0, keepdims=True)
        if with_later: total = total + later[head]
        if keep_total: total_out[head] = total
        low = total.astype(bf16)
        query_halves.append(jnp.dot(key_turned[64*head:64*head+64], low, preferred_element_type=f32))
        kg = jnp.dot(low, query_own, preferred_element_type=f32)
        vg = jnp.dot(soft.astype(bf16), grad_rows, preferred_element_type=f32)
        key_grad = kg if key_grad is None else key_grad+kg
        value_grad = vg if value_grad is None else value_grad+vg
    grads[0] = jnp.concatenate(query_halves, axis=0).T.astype(bf16)
    grads[1] = key_grad.astype(bf16)
    grads[2] = value_grad.astype(bf16)
    sums = jnp.sum(value_grad, axis=0, keepdims=True)
    value_sum[0] = jnp.broadcast_to(sums, (8,128))

def attend_backward(core, lengths, projections, log_norm, context_grad, later, keep_total, rows):
    depth=len(projections)
    seqs = lengths.shape[0] // 2
    pairs=D//128
    col=lambda off: pl.BlockSpec((rows,128), lambda s,j,c,l,off=off:(s,off*pairs+j))
    square=pl.BlockSpec((2,rows,rows),lambda s,j,c,l:(s*pairs+j,0,0))
    in_specs=[col(0)]*depth+[col(1)]*depth+[col(2)]+[pl.BlockSpec((1,8,rows),lambda s,j,c,l:(s*pairs+j,0,0)), col(0)]
    args=[*projections,*projections,projections[0],log_norm,context_grad]
    if later is not None:
        in_specs.append(square); args.append(later)
    out_shape=[jax.ShapeDtypeStruct((3,seqs*rows,D),bf16), jax.ShapeDtypeStruct((seqs,8,D),f32)]
    out_specs=[pl.BlockSpec((3,rows,128),lambda s,j,c,l:(0,s,j)), pl.BlockSpec((1,8,128),lambda s,j,c,l:(s,0,j))]
    if keep_total:
        out_shape.append(jax.ShapeDtypeStruct((seqs*pairs*2,rows,rows),f32)); out_specs.append(square)
    return pl.pallas_call(
        partial(attend_backward_kernel, depth=depth, with_later=later is not None, keep_total=keep_total),
        out_shape=out_shape,
        grid_spec=pltpu.PrefetchScalarGridSpec(num_scalar_prefetch=2, grid=(seqs,pairs), in_specs=in_specs, out_specs=out_specs),
        compiler_params=pltpu.CompilerParams(dimension_semantics=("arbitrary","arbitrary"),vmem_limit_bytes=24 << 20),
        cost_estimate=cost(17),
        name="attend_backward",
    )(core, lengths, *args)


def adam_parts(gradient, first, second, factor):
    clipped = gradient * factor
    first_new = beta_one * first + (1.0 - beta_one) * clipped
    second_new = beta_two * second + (1.0 - beta_two) * clipped * clipped
    first_hat = first_new / (1.0 - beta_one**step_count)
    second_hat = second_new / (1.0 - beta_two**step_count)
    return (first_new, second_new, first_hat / (jnp.sqrt(second_hat) + adam_eps))


def local(
    tokens,
    cotangent,
    lengths,
    proj_weight,
    out_weight,
    up_weight,
    down_weight,
    small_params,
    proj_first,
    proj_second,
    out_first,
    out_second,
    up_first,
    up_second,
    down_first,
    down_second,
    small_first,
    small_second,
):
    layers = proj_weight.shape[0]
    seq_len = tokens.shape[0] // lengths.shape[0]
    half_d = proj_weight.shape[3]
    half_ff = up_weight.shape[2]
    row_count = proj_weight.shape[1]
    parts = lax.axis_size("dp")
    links = Links(parts)
    places = lax.axis_index("tensor") * parts + lax.axis_index("dp")
    places = lax.dynamic_index_in_dim(
        jnp.asarray(links.table.reshape(2 * parts, 4, parts + 1)), places, 0, keepdims=False
    )
    exchanged, in_turn = (places, 0), (places, 1)
    turns = {(0, "proj"): exchanged, (0, "ff"): in_turn, (1, "proj"): in_turn, (1, "ff"): exchanged}
    core = lax.axis_index("tensor")[None].astype(jnp.int32)

    table = {"proj": proj_weight, "out": out_weight, "up": up_weight, "down": down_weight}
    groups = [
        [(0, "proj")], [(0, "up"), (0, "down"), (0, "out")], [(1, "proj")], [(1, "up"), (1, "down"), (1, "out")],
    ]
    gathers = []
    for group in groups:
        share = [table[kind][layer_at].reshape(row_count, -1).astype(bf16) for layer_at, kind in group]
        gathers.append(links.gather(jnp.concatenate(share, axis=1) if len(share) > 1 else share[0]))
    one, two, three, four = gathers
    last = jnp.concatenate([move.pop("held")[0] for move in (two, three)], axis=1)
    last = lax.all_gather(last, ("dp", "tensor")).reshape(parts, 2, row_count, -1)
    two["pair"], three["pair"] = (last, last, 0), (last, last, half_d + 2 * half_ff)
    links.advance([one])
    prepared = links.advance([one], prepare(core, lengths, tokens, cotangent, small_params))
    hidden, hidden_turned, grad_rows, *prepared = prepared
    vectors, value_bias, up_bias = prepared[0::3], prepared[1::3], prepared[2::3]
    links.advance([one])
    links.advance([one])
    (hidden,) = links.advance([four], (hidden,))

    def gathered(layer_at, kind):
        for group, move in zip(groups, gathers):
            widths = [math.prod(table[name].shape[2:]) for _, name in group]
            if (layer_at, kind) in group:
                while links.running(move):
                    links.advance([move])
                if "held" in move:
                    links.pair(move)
                own, other, first = move["pair"]
                return own, other, first + sum(widths[: group.index((layer_at, kind))])

    saved = []
    hidden_low = hidden
    masters = (proj_weight, out_weight, up_weight, down_weight)
    for layer_at in range(layers):
        projected = project(
            turns[layer_at, "proj"], hidden_low, gathered(layer_at, "proj"), value_bias[layer_at]
        )
        if layer_at == 0:
            (projected,) = links.advance([four], (projected,))
        chain = [projected] + [earlier["projected"] for earlier in reversed(saved)]
        context, log_norm = attend_forward(core, lengths, chain, seq_len)
        if layer_at > 0:
            (context,) = links.pair(four, (context,))
        if layer_at == 0:
            late_masters, context = lax.optimization_barrier((masters, context))
            squares = [jnp.sum(one * one, axis=tuple(range(1, one.ndim))) for one in late_masters]
            squares = jnp.pad(jnp.stack(squares, axis=1), ((0, 0), (0, 124)))
            squares, context = links.advance([four], (squares, context))
            (context,) = links.advance([four], (context,))
        kept = {
            "input_turned": hidden_turned, "projected": projected, "log_norm": log_norm, "context": context,
        }
        (
            kept["first_in"], kept["first_turned"], kept["active"], kept["slope"], hidden, *rest,
        ) = feed_forward(
            turns[layer_at, "ff"], hidden, context, gathered(layer_at, "out"), gathered(layer_at, "up"),
            gathered(layer_at, "down"), up_bias[layer_at], vectors[layer_at],
            grad_rows if layer_at == layers - 1 else None,
        )
        if layer_at == layers - 1:
            turned_grad = rest
        else:
            kept["second_in"], hidden_low, hidden_turned = rest
        saved.append(kept)

    smalls = [None] * layers
    later_total = None
    before = []
    for layer_at in reversed(range(layers)):
        kept = saved[layer_at]
        places_ff = turns[layer_at, "ff"]
        first_grad, down_low, down_turned, second_small = turned_grad
        own, other, bias_sum, first_grad = feed_backward(
            places_ff, first_grad, down_low, down_turned,
            [kept[name] for name in ("first_turned", "active", "slope")],
            gathered(layer_at, "up"), gathered(layer_at, "down"), parts,
        )
        ff_sum = links.scatter(own, other)
        (first_grad,) = links.advance(before + [ff_sum], (first_grad,))
        first_in_grad, out_in_turned, context_grad, first_small = context_backward(
            places_ff, first_grad, kept["first_in"], gathered(layer_at, "out"), vectors[layer_at]
        )
        (context_grad,) = links.advance([ff_sum] + before[1:], (context_grad,))
        chain = [kept["projected"]] + [earlier["projected"] for earlier in reversed(saved[:layer_at])]
        results = attend_backward(
            core, lengths, chain, kept["log_norm"], context_grad, later_total, layer_at > 0, seq_len
        )
        head_grads, value_sum = results[:2]
        later_total = results[2] if layer_at > 0 else None
        smalls[layer_at] = (value_sum, first_small, second_small, [bias_sum])
        if layer_at == 0:
            (head_grads,) = links.advance(before, (head_grads,))
            packed = pack(core, smalls, squares)
            packed, head_grads = links.advance([ff_sum], (packed, head_grads))
            packed = links.total(packed)
        attention_sum = links.scatter(
            *projection_grads(
                exchanged, out_in_turned, kept["context"], kept["input_turned"], head_grads, parts
            )
        )
        if layer_at > 0:
            (head_grads,) = links.advance([ff_sum, attention_sum], (head_grads,))
            turned_grad = project_backward(
                turns[layer_at, "proj"], head_grads, first_in_grad, gathered(layer_at, "proj"),
                (saved[layer_at - 1]["second_in"], vectors[layer_at - 1]),
            )
            turned_grad = links.advance([attention_sum], turned_grad)
        else:
            links.advance([attention_sum, packed])
            (head_grads,) = links.advance([attention_sum, before[1]], (head_grads,))
            (grad_rows,) = project_backward(
                turns[layer_at, "proj"], head_grads, first_in_grad, gathered(layer_at, "proj")
            )
        before += [ff_sum, attention_sum]

    width = small_params.shape[1]
    (grad_rows,) = links.advance([ff_sum, attention_sum], (grad_rows,))
    later_sums, grad_rows = links.settle(before[:2], grad_rows)
    sent = (links.sibling(grad_rows), links.sibling(hidden))
    links.advance([packed])
    links.advance([attention_sum])
    links.advance([ff_sum])
    hidden, grad_rows = join(core, ((hidden, sent[1]), (grad_rows, sent[0])))
    hidden, grad_rows = links.advance([packed], (hidden, grad_rows))
    links.advance([attention_sum])
    packed = links.finish([packed])[0]
    small_grad = packed[:, :width]
    weight_square = packed[:, width : width + 4].T

    ff_sums, attention_sums = (
        jnp.stack([earlier, later]) for earlier, later in zip(links.finish([ff_sum, attention_sum]), later_sums)
    )
    grads = (
        attention_sums[:, 1:].transpose(0, 2, 1, 3), attention_sums[:, 0], ff_sums[:, 1], ff_sums[:, 0],
    )
    firsts = (proj_first, out_first, up_first, down_first)
    seconds = (proj_second, out_second, up_second, down_second)
    square_part = sum(jnp.sum(grad * grad) for grad in grads)
    square_big = links.finish([links.total(jnp.broadcast_to(square_part, (8, 128)))])[0][0, 0]
    grad_norm = jnp.sqrt(square_big + jnp.sum(small_grad * small_grad))
    factor = clip_norm / jnp.maximum(grad_norm, clip_norm)
    moments = []
    updates = []
    for kind_at in range(4):
        first_new, second_new, direction = adam_parts(
            grads[kind_at], firsts[kind_at], seconds[kind_at], factor
        )
        moments.append((first_new, second_new))
        updates.append(direction + decay_rate * masters[kind_at])
    update_square = jnp.stack(
        [jnp.sum(update * update, axis=tuple(range(1, update.ndim))) for update in updates]
    )
    update_square = jnp.pad(update_square.reshape(1, -1), ((0, 7), (0, 128 - 4 * layers)))
    update_square = links.finish([links.total(update_square)])[0]
    update_square = update_square[0, : 4 * layers].reshape(4, layers)
    ratio = jnp.sqrt(weight_square) / jnp.sqrt(update_square)

    outputs = [hidden, grad_rows, grad_norm]
    for kind_at in range(4):
        master = masters[kind_at]
        scaled = ratio[kind_at].reshape((-1,) + (1,) * (master.ndim - 1))
        outputs += [
            moments[kind_at][0],
            moments[kind_at][1],
            master - matrix_rate * scaled * updates[kind_at],
        ]
    small_first_new, small_second_new, small_direction = adam_parts(
        small_grad, small_first, small_second, factor
    )
    outputs += [small_first_new, small_second_new, small_params - vector_rate * small_direction]
    return tuple(outputs)


def solution(mesh):
    proj = P(None, "dp", None, "tensor")
    matrix = P(None, "dp", "tensor")
    rows = P("dp", None)
    return jax.shard_map(
        local,
        mesh=mesh,
        in_specs=(rows, rows, P("dp"), proj, matrix, matrix, matrix, P())
        + (proj, proj)
        + (matrix,) * 6
        + (P(), P()),
        out_specs=(rows, rows, P()) + (proj,) * 3 + (matrix,) * 9 + (P(),) * 3,
        check_vma=False,
    )
```

```python
from functools import partial
import math

import jax
import jax.numpy as jnp
import numpy as np
from jax import lax
from jax.experimental import pallas as pl
from jax.experimental.pallas import tpu as pltpu
from jax.sharding import PartitionSpec as P

D = 768
HEADS = 12
FF = 3072


beta_one = 0.9
beta_two = 0.999
adam_eps = 1e-06
decay_rate = 0.01
matrix_rate = 1.0
vector_rate = 0.3
clip_norm = 1.0
step_count = 10.0
norm_eps = 1e-06
masked_score = -1e30

f32 = jnp.float32
bf16 = jnp.bfloat16


class Links:
    def __init__(self, parts):
        self.parts = parts
        count = parts.bit_length() - 1
        high = list(range(count - 1, -1, -1))
        other = high[:-2] + high[-2:][::-1]
        self.orders = (other, high)
        self.inverse = np.zeros((2, parts), np.int32)
        for core in range(2):
            for place in range(parts):
                mask = 0
                for stage in range(count):
                    if (place >> stage) & 1:
                        mask |= 1 << self.orders[core][stage]
                self.inverse[core, mask] = place
        self.stages = count
        self.last = ()
        every = np.arange(parts)
        self.table = np.zeros((2, parts, 4, parts + 1), np.int32)
        for core in range(2):
            for at in range(parts):
                for half, side in enumerate((core, 1 - core)):
                    rows = (self.inverse[side, every ^ at], every)
                    for kind, row in enumerate(rows):
                        self.table[core, at, 2 * kind + half, :parts] = row
                        self.table[core, at, 2 * kind + half, parts] = side

    def swap(self, value, *stages):
        pairs = []
        for core in range(2):
            flip = sum(1 << self.orders[core][stage] for stage in stages)
            pairs += [(2 * at + core, 2 * (at ^ flip) + core) for at in range(self.parts)]
        return lax.ppermute(value, ("dp", "tensor"), pairs)

    def sibling(self, value):
        return lax.ppermute(value, "tensor", [(0, 1), (1, 0)])

    def gather(self, share):
        return {"held": share[None], "stage": 0}

    def total(self, value):
        return {"value": value, "step": 0}

    def scatter(self, own, other):
        return {"pieces": [own], "other": other, "size": self.parts, "stage": self.stages}

    def advance(self, moves, rest=()):
        moves = [move for move in moves if self.running(move)]
        if not moves:
            return rest
        mine, rest, self.last = lax.optimization_barrier(
            ([move.get("held", move.get("value", move.get("pieces"))) for move in moves], rest, self.last)
        )
        sending = []
        for move, value in zip(moves, mine):
            if "held" in move:
                come = move.pop("come", None)
                sending.append(value if come is None else jnp.concatenate([value, come], axis=0))
            elif "value" in move:
                sending.append(self.summed(value, move.pop("come", [])))
            elif "other" in move:
                sending.append(move["other"])
            else:
                half, size = move["size"] // 2, move["size"]
                move["pieces"] = value + move.pop("come")
                sending.append(sum(piece[half:size].astype(f32) for piece in move["pieces"]).astype(bf16))
        sending, rest, _ = lax.optimization_barrier((sending, rest, self.last))
        self.last = sending[0]
        for move, value in zip(moves, sending):
            if "held" in move:
                move["held"] = value
                move["come"] = self.swap(value, move["stage"])
                move["stage"] += 1
            elif "value" in move:
                move["value"] = value
                low, high = 2 * move["step"] - 2, 2 * move["step"] - 1
                if move["step"] == 0:
                    move["come"] = [self.sibling(value)]
                elif high < self.stages:
                    move["come"] = [self.swap(value, low), self.swap(value, high), self.swap(value, low, high)]
                else:
                    move["come"] = [self.swap(value, low)]
                move["step"] += 1
            elif "other" in move:
                move["come"] = [self.sibling(value)]
                del move["other"]
            else:
                move["size"] //= 2
                move["stage"] -= 1
                move["come"] = [self.swap(value, move["stage"])]
        return rest

    def pair(self, move, rest=()):
        while self.running(move):
            self.advance([move])
        held, come = move.pop("held"), move.pop("come")
        if "swapped" not in move:
            move["swapped"] = self.sibling(held)
        held, come, rest = lax.optimization_barrier((held, come, rest))
        swapped = [move.pop("swapped"), self.sibling(come)]
        held = jnp.concatenate([held, come], axis=0)
        move["pair"] = (held, jnp.concatenate(swapped, axis=0), 0)
        return rest

    def swap_early(self, move, rest):
        value, rest, self.last = lax.optimization_barrier((move["held"], rest, self.last))
        move["swapped"] = self.sibling(value)
        return rest

    def summed(self, value, come):
        if len(come) == 3:
            return (value + come[0]) + (come[1] + come[2])
        return value + come[0] if come else value

    def running(self, move):
        return move.get("stage", 0) < self.stages if "held" in move else move.get("size", 1) > 1 or 2 * move.get("step", self.stages) < self.stages + 2

    def settle(self, moves, rest):
        pieces, rest = lax.optimization_barrier(([move["pieces"] for move in moves], rest))
        for move, value in zip(moves, pieces):
            move["pieces"] = value
        return lax.optimization_barrier((self.finish(moves), rest))

    def finish(self, moves):
        for move in moves:
            while self.running(move):
                self.advance([move])
        if "value" in moves[0]:
            return [self.summed(move["value"], move["come"]) for move in moves]
        return [sum(piece[0].astype(f32) for piece in move["pieces"] + move["come"]) for move in moves]


def dot_nt(left, right):
    return lax.dot_general(left, right, (((1,), (1,)), ((), ())), preferred_element_type=f32)


def dot_nn(left, right):
    return jnp.dot(left, right, preferred_element_type=f32)


def in_order(blocks, place_of):
    some = (0,) if len(blocks.shape) == 4 else ()
    return jnp.concatenate([blocks[(place_of[block], *some)] for block in range(blocks.shape[0])], axis=0)


def put_blocks(out, at, product, place_of):
    parts, _, rows, _ = out.shape
    for block in range(parts):
        out[place_of[block], at] = product[block * rows : (block + 1) * rows]


def norm_parts(values):
    centered = values - jnp.mean(values, axis=1, keepdims=True)
    variance = jnp.mean(centered * centered, axis=1, keepdims=True)
    scale = lax.rsqrt(variance + norm_eps)
    return centered * scale, scale


def norm_backward(values, gain, grad):
    unit, scale = norm_parts(values)
    scaled = grad * gain
    inner = scaled - jnp.mean(scaled, axis=1, keepdims=True)
    result = scale * (inner - unit * jnp.mean(scaled * unit, axis=1, keepdims=True))
    return result, jnp.sum(grad * unit, axis=0, keepdims=True), jnp.sum(grad, axis=0, keepdims=True)


def project_kernel(own_at, other_at, own_to, other_to, rows_in, own, other, bias, out):
    width = own.shape[-1]
    for half, (blocks, place_of) in enumerate(((own, own_at), (other, other_at))):
        weight = in_order(blocks, place_of)
        span = slice(half * width, (half + 1) * width)
        out[:, span] = (dot_nn(rows_in[...], weight) + bias[:, span]).astype(bf16)


def cost(microseconds):
    return pl.CostEstimate(flops=0, bytes_accessed=int(microseconds * 2.5e6), transcendentals=0)


class Row:
    def __init__(self, table, row):
        self.table, self.row = table, row

    def __getitem__(self, place):
        return self.table[self.row, place]


def call(kernel, places, grid, ins, outs, scratch=(), name=None, time=1):
    table, pair = places
    weight_rows = lambda at: (Row(at, 2 * pair), Row(at, 2 * pair + 1))
    spec = lambda block, index: pl.BlockSpec(block, lambda i, at: index(i, weight_rows(at)))
    return pl.pallas_call(
        lambda at, *refs: kernel(*weight_rows(at), Row(at, 0), Row(at, 1), *refs),
        out_shape=[jax.ShapeDtypeStruct(shape, kind) for shape, kind, _, _ in outs],
        grid_spec=pltpu.PrefetchScalarGridSpec(
            num_scalar_prefetch=1,
            grid=(grid,),
            in_specs=[spec(block, index) for _, block, index in ins],
            out_specs=[spec(block, index) for _, _, block, index in outs],
            scratch_shapes=list(scratch),
        ),
        compiler_params=pltpu.CompilerParams(
            dimension_semantics=("arbitrary",), vmem_limit_bytes=38 << 20
        ),
        cost_estimate=cost(time),
        name=name,
    )(table, *[array for array, _, _ in ins])


def whole(array):
    return (array, array.shape, lambda i, at: (0,) * array.ndim)


def weight_tiles(pair, tile, count=1):
    own, other, first = pair
    tiles = []
    for half, array in enumerate((own, other)):
        parts, rows = array.shape[0], array.shape[-2]
        column = lambda i: first // tile + jnp.clip(i, 0, count - 1)
        if array.ndim == 3:
            tiles.append((array, (parts, rows, tile), lambda i, at: (0, 0, column(i))))
        else:
            index = lambda i, at, half=half, parts=parts: (0, at[half][parts], 0, column(i))
            tiles.append((array, (parts, 1, rows, tile), index))
    return tiles


def project(places, rows_in, pair, bias):
    rows = rows_in.shape[0]
    half = D // 2
    return call(
        project_kernel, places, 3,
        [whole(rows_in), *weight_tiles(pair, half, 3), (bias, (1, D), lambda i, at: (0, i))],
        [((rows, 3 * D), bf16, (rows, D), lambda i, at: (0, i))],
        name="project",
        time=7,
    )[0]


def feed_forward_kernel(
    own_at, other_at, own_to, other_to, hidden, context, out_own, out_other, up_own, up_other, down_own, down_other,
    bias_up, vectors, *refs, with_grad,
):
    if with_grad:
        grad, first_in, first_turned, active, slope, hidden_new, *turned, first_low, second_in = refs
        total = second_in
    else:
        first_in, first_turned, active, slope, hidden_new, second_in, hidden_low, hidden_turned, first_low = refs
        total = second_in
    step = pl.program_id(0)
    halves = ((own_at, up_own, down_own), (other_at, up_other, down_other))
    half_d = D // 2

    @pl.when(step == 0)
    def _():
        attended = dot_nt(context[:, :half_d], in_order(out_own, own_at))
        attended += dot_nt(context[:, half_d:], in_order(out_other, other_at))
        values = hidden[...].astype(f32) + attended + vectors[0:1]
        first_in[...] = values
        unit, _ = norm_parts(values)
        values = unit * vectors[1:2] + vectors[2:3]
        low = values.astype(bf16)
        first_low[...] = low
        first_turned[...] = low.T
        total[...] = values + vectors[3:4]

    for half, (place_of, up, down) in enumerate(halves):
        before = dot_nn(first_low[...], in_order(up, place_of)) + bias_up[half]
        shade = 0.5 * (1.0 + lax.erf(before * (1.0 / math.sqrt(2.0))))
        bell = jnp.exp(-0.5 * before * before) * (1.0 / math.sqrt(2.0 * math.pi))
        low = (before * shade).astype(bf16)
        active[half] = low
        slope[half] = shade + before * bell
        total[...] += dot_nt(low, in_order(down, place_of))

    @pl.when(step == pl.num_programs(0) - 1)
    def _():
        unit, _ = norm_parts(second_in[...])
        values = unit * vectors[4:5] + vectors[5:6]
        hidden_new[...] = values
        if with_grad:
            norm_turn(second_in[...], vectors[4:5], grad[...], *turned)
        else:
            low = values.astype(bf16)
            hidden_low[...] = low
            hidden_turned[...] = low.T


def feed_forward(places, hidden, context, out_pair, up_pair, down_pair, bias_up, vectors, grad=None, tile=512):
    rows = hidden.shape[0]
    half_ff = bias_up.shape[2]
    count = half_ff // tile
    flat = lambda kind: ((rows, D), kind, (rows, D), lambda i, at: (0, 0))
    tiled = lambda kind: ((2, rows, half_ff), kind, (2, rows, tile), lambda i, at: (0, 0, i))
    turned = ((D, rows), bf16, (D, rows), lambda i, at: (0, 0))
    return call(
        partial(feed_forward_kernel, with_grad=grad is not None), places, count,
        [
            whole(hidden),
            whole(context),
            *weight_tiles(out_pair, D // 2),
            *weight_tiles(up_pair, tile, count),
            *weight_tiles(down_pair, tile, count),
            (bias_up, (2, 1, tile), lambda i, at: (0, 0, i)),
            whole(vectors),
            *([] if grad is None else [whole(grad)]),
        ],
        [
            flat(f32), turned, tiled(bf16), tiled(f32), flat(f32),
            *([flat(f32), flat(bf16), turned] if grad is None else norm_turn_outs(rows)),
        ],
        [pltpu.VMEM((rows, D), bf16)] + ([] if grad is None else [pltpu.VMEM((rows, D), f32)]),
        name="feed_forward",
        time=18,
    )


def norm_turn(values, gain, grad, total, down_low, down_turned, small):
    result, gain_grad, shift_grad = norm_backward(values, gain, grad)
    small[...] = jnp.zeros_like(small)
    small[0:1] = jnp.sum(result, axis=0, keepdims=True)
    small[1:2] = gain_grad
    small[2:3] = shift_grad
    total[...] = result
    low = result.astype(bf16)
    down_low[...] = low
    down_turned[...] = low.T


def norm_turn_outs(rows):
    flat = lambda kind: ((rows, D), kind, (rows, D), lambda i, at: (0, 0))
    turned = ((D, rows), bf16, (D, rows), lambda i, at: (0, 0))
    return [flat(f32), flat(bf16), turned, ((8, D), f32, (8, D), lambda i, at: (0, 0))]


def feed_backward_kernel(
    own_at, other_at, own_to, other_to, total_in, down_low, down_turned, first_turned, active, slope,
    up_own, up_other, down_own, down_other, grads_own, grads_other, bias_grads, total,
):
    halves = (
        (own_at, own_to, up_own, down_own, grads_own),
        (other_at, other_to, up_other, down_other, grads_other),
    )

    @pl.when(pl.program_id(0) == 0)
    def _():
        total[...] = total_in[...]

    for half, (place_of, place_to, up, down, grads) in enumerate(halves):
        act_grad = dot_nn(down_low[...], in_order(down, place_of))
        before_grad = act_grad * slope[half]
        bias_grads[half] = jnp.broadcast_to(jnp.sum(before_grad, axis=0, keepdims=True), bias_grads.shape[1:])
        low = before_grad.astype(bf16)
        put_blocks(grads, 0, dot_nn(down_turned[...], active[half]).astype(bf16), place_to)
        put_blocks(grads, 1, dot_nn(first_turned[...], low).astype(bf16), place_to)
        total[...] += dot_nt(low, in_order(up, place_of))


def context_backward_kernel(
    own_at, other_at, own_to, other_to, grad, first_in, out_own, out_other, vectors,
    first_in_grad, out_in_turned, context_grad, small,
):
    half_d = D // 2
    result, gain_grad, shift_grad = norm_backward(first_in[...], vectors[1:2], grad[...])
    small[...] = jnp.zeros_like(small)
    small[0:1] = jnp.sum(result, axis=0, keepdims=True)
    small[1:2] = gain_grad
    small[2:3] = shift_grad
    first_in_grad[...] = result
    low = result.astype(bf16)
    out_in_turned[...] = low.T
    context_grad[:, :half_d] = dot_nn(low, in_order(out_own, own_at)).astype(bf16)
    context_grad[:, half_d:] = dot_nn(low, in_order(out_other, other_at)).astype(bf16)


def context_backward(places, grad, first_in, out_pair, vectors):
    rows = grad.shape[0]
    flat = lambda kind: ((rows, D), kind, (rows, D), lambda i, at: (0, 0))
    return call(
        context_backward_kernel, places, 1,
        [
            whole(grad), whole(first_in),
            *weight_tiles(out_pair, D // 2),
            whole(vectors),
        ],
        [
            flat(f32), ((D, rows), bf16, (D, rows), lambda i, at: (0, 0)), flat(bf16),
            ((8, D), f32, (8, D), lambda i, at: (0, 0)),
        ],
        name="context_backward",
        time=6,
    )


def feed_backward(places, total, down_low, down_turned, kept, up_pair, down_pair, parts, tile=512):
    first_turned, active, slope = kept
    rows = total.shape[0]
    half_ff = active.shape[2]
    count = half_ff // tile
    block_rows = D // parts
    tiled = lambda array: (array, (2, rows, tile), lambda i, at: (0, 0, i))
    grads = ((parts, 2, block_rows, count * tile), bf16, (parts, 2, block_rows, tile), lambda i, at: (0, 0, 0, i))
    return call(
        feed_backward_kernel, places, count,
        [
            whole(total), whole(down_low), whole(down_turned), whole(first_turned), tiled(active), tiled(slope),
            *weight_tiles(up_pair, tile, count),
            *weight_tiles(down_pair, tile, count),
        ],
        [
            grads, grads,
            ((2, 8, count * tile), f32, (2, 8, tile), lambda i, at: (0, 0, i)),
            ((rows, D), f32, (rows, D), lambda i, at: (0, 0)),
        ],
        name="feed_backward",
        time=20,
    )


def projection_grads_kernel(
    own_at, other_at, own_to, other_to, out_in_turned, context, input_turned, head_grads,
    grads_own, grads_other,
):
    step = pl.program_id(0)
    half_d = D // 2
    halves = ((own_to, grads_own), (other_to, grads_other))
    for when, left, right in (
        (step == 0, out_in_turned, lambda span: context[:, span]),
        (step > 0, input_turned, lambda span: head_grads[0, :, span]),
    ):

        @pl.when(when)
        def _():
            for half, (place_to, grads) in enumerate(halves):
                span = slice(half * half_d, (half + 1) * half_d)
                put_blocks(grads, 0, dot_nn(left[...], right(span)).astype(bf16), place_to)


def projection_grads(places, out_in_turned, context, input_turned, head_grads, parts):
    rows = context.shape[0]
    half = D // 2
    block_rows = D // parts
    grads = ((parts, 4, block_rows, half), bf16, (parts, 1, block_rows, half), lambda i, at: (0, i, 0, 0))
    return call(
        projection_grads_kernel, places, 4,
        [
            whole(out_in_turned), whole(context), whole(input_turned),
            (head_grads, (1, rows, D), lambda i, at: (jnp.maximum(i - 1, 0), 0, 0)),
        ],
        [grads, grads],
        name="projection_grads",
        time=9,
    )


def project_backward_kernel(
    own_at, other_at, own_to, other_to, head_grads, first_in_grad, own, other, *refs, with_norm
):
    half_d = D // 2
    step = pl.program_id(0)
    if with_norm:
        second_in, vectors, *turned, input_grad = refs
    else:
        (input_grad,) = refs

    @pl.when(step == 0)
    def _():
        input_grad[...] = first_in_grad[...]

    for half, (place_of, weight) in enumerate(((own_at, own), (other_at, other))):
        low = head_grads[0, :, half * half_d : (half + 1) * half_d]
        input_grad[...] += dot_nt(low, in_order(weight, place_of))

    if with_norm:

        @pl.when(step == pl.num_programs(0) - 1)
        def _():
            norm_turn(second_in[...], vectors[4:5], input_grad[...], *turned)


def project_backward(places, head_grads, first_in_grad, pair, earlier=()):
    rows = first_in_grad.shape[0]
    half = D // 2
    return call(
        partial(project_backward_kernel, with_norm=bool(earlier)), places, 3,
        [
            (head_grads, (1, rows, D), lambda i, at: (i, 0, 0)),
            whole(first_in_grad),
            *weight_tiles(pair, half, 3),
            *map(whole, earlier),
        ],
        norm_turn_outs(rows) if earlier else [((rows, D), f32, (rows, D), lambda i, at: (0, 0))],
        [pltpu.VMEM((rows, D), f32)] if earlier else [],
        name="project_backward",
        time=8,
    )


def join_kernel(core, *refs):
    step = pl.program_id(0)
    count = len(refs) // 3
    for one in range(count):
        own, other, out = refs[2 * one], refs[2 * one + 1], refs[2 * count + one]

        @pl.when(step == core[0])
        def _():
            out[...] = own[...]

        @pl.when(step != core[0])
        def _():
            out[...] = other[...]


def join(core, pairs):
    rows, cols = pairs[0][0].shape
    spec = pl.BlockSpec((rows, cols), lambda i, at: (0, 0))
    return pl.pallas_call(
        join_kernel,
        out_shape=[jax.ShapeDtypeStruct((2 * rows, cols), f32) for _ in pairs],
        grid_spec=pltpu.PrefetchScalarGridSpec(
            num_scalar_prefetch=1,
            grid=(2,),
            in_specs=[spec] * (2 * len(pairs)),
            out_specs=[pl.BlockSpec((rows, cols), lambda i, at: (i, 0)) for _ in pairs],
        ),
        compiler_params=pltpu.CompilerParams(
            dimension_semantics=("arbitrary",), vmem_limit_bytes=38 << 20
        ),
        cost_estimate=cost(4),
        name="join",
    )(core, *[rows_of for pair in pairs for rows_of in pair])


bounds = [0, D, 2 * D, 2 * D + FF, 3 * D + FF, 4 * D + FF, 5 * D + FF, 6 * D + FF, 7 * D + FF]


def swapped(core, vector):
    half = vector.shape[1] // 2
    first, second = vector[:, :half], vector[:, half:]
    return jnp.where(core == 0, first, second), jnp.where(core == 0, second, first)


def prepare_kernel(core, lengths, tokens, cotangent, small, tokens_own, tokens_turned, grad, *outs):
    step = pl.program_id(0)
    length = lengths[core[0] * pl.num_programs(0) + step]
    tokens_own[...] = tokens[...]
    tokens_turned[...] = tokens[...].T
    valid = lax.broadcasted_iota(jnp.int32, grad.shape, 0) < length
    grad[...] = jnp.where(valid, cotangent[...].astype(f32), 0.0)

    @pl.when(step == 0)
    def _():
        for layer_at in range(small.shape[0]):
            vectors, value_bias, up_bias = outs[3 * layer_at : 3 * layer_at + 3]
            part = lambda place: small[layer_at : layer_at + 1, bounds[place] : bounds[place + 1]]
            vectors[...] = jnp.zeros_like(vectors)
            for row, place in enumerate((1, 4, 5, 3, 6, 7)):
                vectors[row : row + 1] = part(place)
            value_bias[...] = jnp.zeros_like(value_bias)
            first, second = swapped(core[0], part(0))
            value_bias[:, 2 * D : 2 * D + D // 2] = first
            value_bias[:, 2 * D + D // 2 :] = second
            up_bias[0], up_bias[1] = swapped(core[0], part(2))


def prepare(core, lengths, tokens, cotangent, small):
    layers = small.shape[0]
    seqs = lengths.shape[0] // 2
    rows = tokens.shape[0] // lengths.shape[0]
    mine = pl.BlockSpec((rows, D), lambda s, c, l: (c[0] * seqs + s, 0))
    fixed = lambda shape: pl.BlockSpec(shape, lambda s, c, l: (0,) * len(shape))
    shapes = [(8, D), (1, 3 * D), (2, 1, FF // 2)] * layers
    return pl.pallas_call(
        prepare_kernel,
        out_shape=[
            jax.ShapeDtypeStruct((seqs * rows, D), bf16),
            jax.ShapeDtypeStruct((D, seqs * rows), bf16),
            jax.ShapeDtypeStruct((seqs * rows, D), f32),
            *[jax.ShapeDtypeStruct(shape, f32) for shape in shapes],
        ],
        grid_spec=pltpu.PrefetchScalarGridSpec(
            num_scalar_prefetch=2,
            grid=(seqs,),
            in_specs=[mine, mine, fixed(small.shape)],
            out_specs=[
                pl.BlockSpec((rows, D), lambda s, c, l: (s, 0)),
                pl.BlockSpec((D, rows), lambda s, c, l: (0, s)),
                pl.BlockSpec((rows, D), lambda s, c, l: (s, 0)),
                *[fixed(shape) for shape in shapes],
            ],
        ),
        compiler_params=pltpu.CompilerParams(
            dimension_semantics=("arbitrary",), vmem_limit_bytes=44 << 20
        ),
        cost_estimate=cost(3),
        name="prepare",
    )(core, lengths, tokens, cotangent, small)


def pack_kernel(core, *refs, counts):
    out = refs[-1]
    squares = refs[-2]
    at = 0
    for layer_at, count in enumerate(counts):
        value_sum, first_small, second_small, *bias_sums = refs[at : at + 3 + count]
        at += 3 + count
        row = slice(layer_at, layer_at + 1)

        def put(place, values, start=0):
            first = bounds[place] + start
            out[row, first : first + values.shape[1]] = values

        total = value_sum[0, 0:1]
        for seq in range(1, value_sum.shape[0]):
            total = total + value_sum[seq, 0:1]
        for half, values in enumerate(swapped(core[0], total)):
            put(0, values, half * (D // 2))
        put(1, first_small[0:1])
        width = bias_sums[0].shape[2]
        for place, bias_sum in enumerate(bias_sums):
            own, other = bias_sum[0, 0:1], bias_sum[1, 0:1]
            put(2, jnp.where(core[0] == 0, own, other), place * width)
            put(2, jnp.where(core[0] == 0, other, own), FF // 2 + place * width)
        put(3, second_small[0:1])
        for place, values in ((4, first_small[1:2]), (5, first_small[2:3])):
            put(place, values)
        for place, values in ((6, second_small[1:2]), (7, second_small[2:3])):
            put(place, values)
        out[row, bounds[-1] :] = squares[row]


def pack(core, layers, squares):
    arrays = [array for value, first, second, sums in layers for array in (value, first, second, *sums)]
    arrays.append(squares)
    return pl.pallas_call(
        partial(pack_kernel, counts=[len(sums) for _, _, _, sums in layers]),
        out_shape=jax.ShapeDtypeStruct((len(layers), bounds[-1] + 128), f32),
        grid_spec=pltpu.PrefetchScalarGridSpec(
            num_scalar_prefetch=1,
            grid=(1,),
            in_specs=[pl.BlockSpec(array.shape, lambda i, c, n=array.ndim: (0,) * n) for array in arrays],
            out_specs=pl.BlockSpec((len(layers), bounds[-1] + 128), lambda i, c: (0, 0)),
        ),
        compiler_params=pltpu.CompilerParams(dimension_semantics=("arbitrary",)),
        cost_estimate=cost(2),
        name="pack",
    )(core, *arrays)


def head_mask(width, scale):
    lane = lax.broadcasted_iota(jnp.int32, (1, 128), 1)
    return [jnp.where(lane // 64 == head, scale, 0.0).astype(bf16) for head in range(2)]

def attend_forward_kernel(core, lengths, *refs, depth):
    queries, keys, value_rows = refs[:depth], refs[depth:2*depth], refs[2*depth]
    context, log_norm = refs[2*depth+1:]
    length = lengths[core[0] * pl.num_programs(0) + pl.program_id(0)]
    key_all = [k[...] for k in keys]
    key_all = jnp.concatenate(key_all, axis=1) if depth>1 else key_all[0]
    turned = value_rows[...].T
    rows = key_all.shape[0]
    valid = lax.broadcasted_iota(jnp.int32, (rows, rows), 0) < length
    scaled = head_mask(64, 0.125)
    halves = []
    for head in range(2):
        query = [q[...] * scaled[head] for q in queries]
        query = jnp.concatenate(query, axis=1) if depth>1 else query[0]
        score = jnp.where(valid, dot_nt(key_all, query), masked_score)
        top = jnp.max(score, axis=0, keepdims=True)
        weight = jnp.exp(score - top)
        total = jnp.sum(weight, axis=0, keepdims=True)
        low = (weight * (1.0 / total)).astype(bf16)
        halves.append(jnp.dot(turned[64*head:64*head+64], low, preferred_element_type=f32))
        log_norm[0, head:head+1] = top + jnp.log(total)
    context[...] = jnp.concatenate(halves, axis=0).T.astype(bf16)

def attend_forward(core, lengths, projections, rows):
    depth=len(projections)
    seqs = lengths.shape[0] // 2
    pairs=D//128
    col=lambda off: pl.BlockSpec((rows,128), lambda s,j,c,l,off=off:(s,off*pairs+j))
    return pl.pallas_call(
        partial(attend_forward_kernel, depth=depth),
        out_shape=[jax.ShapeDtypeStruct((seqs*rows,D),bf16), jax.ShapeDtypeStruct((seqs*pairs,8,rows),f32)],
        grid_spec=pltpu.PrefetchScalarGridSpec(num_scalar_prefetch=2, grid=(seqs,pairs),
            in_specs=[col(0)]*depth+[col(1)]*depth+[col(2)],
            out_specs=[pl.BlockSpec((rows,128),lambda s,j,c,l:(s,j)), pl.BlockSpec((1,8,rows),lambda s,j,c,l:(s*pairs+j,0,0))]),
        compiler_params=pltpu.CompilerParams(dimension_semantics=("arbitrary","arbitrary"),vmem_limit_bytes=44 << 20),
        cost_estimate=cost(10),
        name="attend_forward",
    )(core, lengths, *projections, *projections, projections[0])

def attend_backward_kernel(core, lengths, *refs, depth, with_later, keep_total):
    queries, keys, value_rows = refs[:depth], refs[depth:2*depth], refs[2*depth]
    log_norm, context_grad = refs[2*depth+1:2*depth+3]
    at = 2*depth+3
    if with_later:
        later = refs[at]; at+=1
    grads, value_sum = refs[at:at+2]
    if keep_total: total_out = refs[at+2]
    length = lengths[core[0] * pl.num_programs(0) + pl.program_id(0)]
    key_all = [k[...] for k in keys]
    key_all = jnp.concatenate(key_all, axis=1) if depth>1 else key_all[0]
    rows = key_all.shape[0]
    valid = lax.broadcasted_iota(jnp.int32, (rows, rows), 0) < length
    scaled = head_mask(64, 0.125)
    plain = head_mask(64, 1.0)
    key_turned = (keys[0][...] * 0.125).astype(bf16).T
    query_halves = []
    key_grad = value_grad = None
    for head in range(2):
        query = [q[...] * scaled[head] for q in queries]
        query_own = query[0]
        query = jnp.concatenate(query, axis=1) if depth>1 else query[0]
        score = jnp.where(valid, dot_nt(key_all, query), masked_score)
        soft = jnp.exp(score - log_norm[0, head:head+1])
        grad_rows = context_grad[...] * plain[head]
        soft_grad = dot_nt(value_rows[...], grad_rows)
        product = soft * soft_grad
        total = product - soft * jnp.sum(product, axis=0, keepdims=True)
        if with_later: total = total + later[head]
        if keep_total: total_out[head] = total
        low = total.astype(bf16)
        query_halves.append(jnp.dot(key_turned[64*head:64*head+64], low, preferred_element_type=f32))
        kg = jnp.dot(low, query_own, preferred_element_type=f32)
        vg = jnp.dot(soft.astype(bf16), grad_rows, preferred_element_type=f32)
        key_grad = kg if key_grad is None else key_grad+kg
        value_grad = vg if value_grad is None else value_grad+vg
    grads[0] = jnp.concatenate(query_halves, axis=0).T.astype(bf16)
    grads[1] = key_grad.astype(bf16)
    grads[2] = value_grad.astype(bf16)
    sums = jnp.sum(value_grad, axis=0, keepdims=True)
    value_sum[0] = jnp.broadcast_to(sums, (8,128))

def attend_backward(core, lengths, projections, log_norm, context_grad, later, keep_total, rows):
    depth=len(projections)
    seqs = lengths.shape[0] // 2
    pairs=D//128
    col=lambda off: pl.BlockSpec((rows,128), lambda s,j,c,l,off=off:(s,off*pairs+j))
    square=pl.BlockSpec((2,rows,rows),lambda s,j,c,l:(s*pairs+j,0,0))
    in_specs=[col(0)]*depth+[col(1)]*depth+[col(2)]+[pl.BlockSpec((1,8,rows),lambda s,j,c,l:(s*pairs+j,0,0)), col(0)]
    args=[*projections,*projections,projections[0],log_norm,context_grad]
    if later is not None:
        in_specs.append(square); args.append(later)
    out_shape=[jax.ShapeDtypeStruct((3,seqs*rows,D),bf16), jax.ShapeDtypeStruct((seqs,8,D),f32)]
    out_specs=[pl.BlockSpec((3,rows,128),lambda s,j,c,l:(0,s,j)), pl.BlockSpec((1,8,128),lambda s,j,c,l:(s,0,j))]
    if keep_total:
        out_shape.append(jax.ShapeDtypeStruct((seqs*pairs*2,rows,rows),f32)); out_specs.append(square)
    return pl.pallas_call(
        partial(attend_backward_kernel, depth=depth, with_later=later is not None, keep_total=keep_total),
        out_shape=out_shape,
        grid_spec=pltpu.PrefetchScalarGridSpec(num_scalar_prefetch=2, grid=(seqs,pairs), in_specs=in_specs, out_specs=out_specs),
        compiler_params=pltpu.CompilerParams(dimension_semantics=("arbitrary","arbitrary"),vmem_limit_bytes=44 << 20),
        cost_estimate=cost(17),
        name="attend_backward",
    )(core, lengths, *args)


def adam_parts(gradient, first, second, factor):
    clipped = gradient * factor
    first_new = beta_one * first + (1.0 - beta_one) * clipped
    second_new = beta_two * second + (1.0 - beta_two) * clipped * clipped
    first_hat = first_new / (1.0 - beta_one**step_count)
    second_hat = second_new / (1.0 - beta_two**step_count)
    return (first_new, second_new, first_hat / (jnp.sqrt(second_hat) + adam_eps))


def local(
    tokens,
    cotangent,
    lengths,
    proj_weight,
    out_weight,
    up_weight,
    down_weight,
    small_params,
    proj_first,
    proj_second,
    out_first,
    out_second,
    up_first,
    up_second,
    down_first,
    down_second,
    small_first,
    small_second,
):
    layers = proj_weight.shape[0]
    seq_len = tokens.shape[0] // lengths.shape[0]
    half_d = proj_weight.shape[3]
    half_ff = up_weight.shape[2]
    row_count = proj_weight.shape[1]
    parts = lax.axis_size("dp")
    links = Links(parts)
    places = lax.axis_index("tensor") * parts + lax.axis_index("dp")
    places = lax.dynamic_index_in_dim(
        jnp.asarray(links.table.reshape(2 * parts, 4, parts + 1)), places, 0, keepdims=False
    )
    exchanged, in_turn = (places, 0), (places, 1)
    turns = {(0, "proj"): exchanged, (0, "ff"): in_turn, (1, "proj"): in_turn, (1, "ff"): exchanged}
    core = lax.axis_index("tensor")[None].astype(jnp.int32)

    table = {"proj": proj_weight, "out": out_weight, "up": up_weight, "down": down_weight}
    groups = [
        [(0, "proj")], [(0, "up"), (0, "down"), (0, "out")], [(1, "proj")], [(1, "up"), (1, "down"), (1, "out")],
    ]
    gathers = []
    for group in groups:
        share = [table[kind][layer_at].reshape(row_count, -1).astype(bf16) for layer_at, kind in group]
        gathers.append(links.gather(jnp.concatenate(share, axis=1) if len(share) > 1 else share[0]))
    one, two, three, four = gathers
    last = jnp.concatenate([move.pop("held")[0] for move in (two, three)], axis=1)
    last = lax.all_gather(last, ("dp", "tensor")).reshape(parts, 2, row_count, -1)
    two["pair"], three["pair"] = (last, last, 0), (last, last, half_d + 2 * half_ff)
    links.advance([one])
    prepared = links.advance([one], prepare(core, lengths, tokens, cotangent, small_params))
    hidden, hidden_turned, grad_rows, *prepared = prepared
    vectors, value_bias, up_bias = prepared[0::3], prepared[1::3], prepared[2::3]
    links.advance([one])
    links.advance([one])
    if not links.running(one):
        (hidden,) = links.swap_early(one, (hidden,))
    (hidden,) = links.advance([four], (hidden,))

    def gathered(layer_at, kind):
        for group, move in zip(groups, gathers):
            widths = [math.prod(table[name].shape[2:]) for _, name in group]
            if (layer_at, kind) in group:
                while links.running(move):
                    links.advance([move])
                if "held" in move:
                    links.pair(move)
                own, other, first = move["pair"]
                return own, other, first + sum(widths[: group.index((layer_at, kind))])

    saved = []
    hidden_low = hidden
    masters = (proj_weight, out_weight, up_weight, down_weight)
    for layer_at in range(layers):
        projected = project(
            turns[layer_at, "proj"], hidden_low, gathered(layer_at, "proj"), value_bias[layer_at]
        )
        if layer_at == 0:
            (projected,) = links.advance([four], (projected,))
        chain = [projected] + [earlier["projected"] for earlier in reversed(saved)]
        context, log_norm = attend_forward(core, lengths, chain, seq_len)
        if layer_at > 0:
            (context,) = links.pair(four, (context,))
        if layer_at == 0:
            late_masters, context = lax.optimization_barrier((masters, context))
            squares = [jnp.sum(one * one, axis=tuple(range(1, one.ndim))) for one in late_masters]
            squares = jnp.pad(jnp.stack(squares, axis=1), ((0, 0), (0, 124)))
            squares, context = links.advance([four], (squares, context))
            (context,) = links.advance([four], (context,))
            if not links.running(four):
                (context,) = links.swap_early(four, (context,))
        kept = {
            "input_turned": hidden_turned, "projected": projected, "log_norm": log_norm, "context": context,
        }
        (
            kept["first_in"], kept["first_turned"], kept["active"], kept["slope"], hidden, *rest,
        ) = feed_forward(
            turns[layer_at, "ff"], hidden, context, gathered(layer_at, "out"), gathered(layer_at, "up"),
            gathered(layer_at, "down"), up_bias[layer_at], vectors[layer_at],
            grad_rows if layer_at == layers - 1 else None,
        )
        if layer_at == layers - 1:
            turned_grad = rest
        else:
            kept["second_in"], hidden_low, hidden_turned = rest
        saved.append(kept)

    smalls = [None] * layers
    later_total = None
    before = []
    for layer_at in reversed(range(layers)):
        kept = saved[layer_at]
        places_ff = turns[layer_at, "ff"]
        first_grad, down_low, down_turned, second_small = turned_grad
        own, other, bias_sum, first_grad = feed_backward(
            places_ff, first_grad, down_low, down_turned,
            [kept[name] for name in ("first_turned", "active", "slope")],
            gathered(layer_at, "up"), gathered(layer_at, "down"), parts,
        )
        ff_sum = links.scatter(own, other)
        (first_grad,) = links.advance(before + [ff_sum], (first_grad,))
        first_in_grad, out_in_turned, context_grad, first_small = context_backward(
            places_ff, first_grad, kept["first_in"], gathered(layer_at, "out"), vectors[layer_at]
        )
        (context_grad,) = links.advance([ff_sum] + before[1:], (context_grad,))
        chain = [kept["projected"]] + [earlier["projected"] for earlier in reversed(saved[:layer_at])]
        results = attend_backward(
            core, lengths, chain, kept["log_norm"], context_grad, later_total, layer_at > 0, seq_len
        )
        head_grads, value_sum = results[:2]
        later_total = results[2] if layer_at > 0 else None
        smalls[layer_at] = (value_sum, first_small, second_small, [bias_sum])
        if layer_at == 0:
            (head_grads,) = links.advance(before, (head_grads,))
            packed = pack(core, smalls, squares)
            packed, head_grads = links.advance([ff_sum], (packed, head_grads))
            packed = links.total(packed)
        attention_sum = links.scatter(
            *projection_grads(
                exchanged, out_in_turned, kept["context"], kept["input_turned"], head_grads, parts
            )
        )
        if layer_at > 0:
            (head_grads,) = links.advance([ff_sum, attention_sum], (head_grads,))
            turned_grad = project_backward(
                turns[layer_at, "proj"], head_grads, first_in_grad, gathered(layer_at, "proj"),
                (saved[layer_at - 1]["second_in"], vectors[layer_at - 1]),
            )
            turned_grad = links.advance([attention_sum], turned_grad)
        else:
            links.advance([attention_sum, packed])
            (head_grads,) = links.advance([attention_sum, before[1]], (head_grads,))
            (grad_rows,) = project_backward(
                turns[layer_at, "proj"], head_grads, first_in_grad, gathered(layer_at, "proj")
            )
        before += [ff_sum, attention_sum]

    width = small_params.shape[1]
    (grad_rows,) = links.advance([ff_sum, attention_sum], (grad_rows,))
    later_sums, grad_rows = links.settle(before[:2], grad_rows)
    sent = (links.sibling(grad_rows), links.sibling(hidden))
    links.advance([packed])
    links.advance([attention_sum])
    links.advance([ff_sum])
    hidden, grad_rows = join(core, ((hidden, sent[1]), (grad_rows, sent[0])))
    hidden, grad_rows = links.advance([packed], (hidden, grad_rows))
    links.advance([attention_sum])
    packed = links.finish([packed])[0]
    small_grad = packed[:, :width]
    weight_square = packed[:, width : width + 4].T

    ff_sums, attention_sums = (
        jnp.stack([earlier, later]) for earlier, later in zip(links.finish([ff_sum, attention_sum]), later_sums)
    )
    grads = (
        attention_sums[:, 1:].transpose(0, 2, 1, 3), attention_sums[:, 0], ff_sums[:, 1], ff_sums[:, 0],
    )
    firsts = (proj_first, out_first, up_first, down_first)
    seconds = (proj_second, out_second, up_second, down_second)
    square_part = sum(jnp.sum(grad * grad) for grad in grads)
    square_big = links.finish([links.total(jnp.broadcast_to(square_part, (8, 128)))])[0][0, 0]
    grad_norm = jnp.sqrt(square_big + jnp.sum(small_grad * small_grad))
    factor = clip_norm / jnp.maximum(grad_norm, clip_norm)
    moments = []
    updates = []
    for kind_at in range(4):
        first_new, second_new, direction = adam_parts(
            grads[kind_at], firsts[kind_at], seconds[kind_at], factor
        )
        moments.append((first_new, second_new))
        updates.append(direction + decay_rate * masters[kind_at])
    update_square = jnp.stack(
        [jnp.sum(update * update, axis=tuple(range(1, update.ndim))) for update in updates]
    )
    update_square = jnp.pad(update_square.reshape(1, -1), ((0, 7), (0, 128 - 4 * layers)))
    update_square = links.finish([links.total(update_square)])[0]
    update_square = update_square[0, : 4 * layers].reshape(4, layers)
    ratio = jnp.sqrt(weight_square) / jnp.sqrt(update_square)

    outputs = [hidden, grad_rows, grad_norm]
    for kind_at in range(4):
        master = masters[kind_at]
        scaled = ratio[kind_at].reshape((-1,) + (1,) * (master.ndim - 1))
        outputs += [
            moments[kind_at][0],
            moments[kind_at][1],
            master - matrix_rate * scaled * updates[kind_at],
        ]
    small_first_new, small_second_new, small_direction = adam_parts(
        small_grad, small_first, small_second, factor
    )
    outputs += [small_first_new, small_second_new, small_params - vector_rate * small_direction]
    return tuple(outputs)


def solution(mesh):
    proj = P(None, "dp", None, "tensor")
    matrix = P(None, "dp", "tensor")
    rows = P("dp", None)
    return jax.shard_map(
        local,
        mesh=mesh,
        in_specs=(rows, rows, P("dp"), proj, matrix, matrix, matrix, P())
        + (proj, proj)
        + (matrix,) * 6
        + (P(), P()),
        out_specs=(rows, rows, P()) + (proj,) * 3 + (matrix,) * 9 + (P(),) * 3,
        check_vma=False,
    )
```

```python
from functools import partial
import math

import jax
import jax.numpy as jnp
import numpy as np
from jax import lax
from jax.experimental import pallas as pl
from jax.experimental.pallas import tpu as pltpu
from jax.sharding import PartitionSpec as P

D = 768
HEADS = 12
FF = 3072


beta_one = 0.9
beta_two = 0.999
adam_eps = 1e-06
decay_rate = 0.01
matrix_rate = 1.0
vector_rate = 0.3
clip_norm = 1.0
step_count = 10.0
norm_eps = 1e-06
masked_score = -1e30

f32 = jnp.float32
bf16 = jnp.bfloat16


class Links:
    def __init__(self, parts):
        self.parts = parts
        count = parts.bit_length() - 1
        high = list(range(count - 1, -1, -1))
        other = high[:-2] + high[-2:][::-1]
        self.orders = (other, high)
        self.inverse = np.zeros((2, parts), np.int32)
        for core in range(2):
            for place in range(parts):
                mask = 0
                for stage in range(count):
                    if (place >> stage) & 1:
                        mask |= 1 << self.orders[core][stage]
                self.inverse[core, mask] = place
        self.stages = count
        self.last = ()
        every = np.arange(parts)
        self.table = np.zeros((2, parts, 4, parts + 1), np.int32)
        for core in range(2):
            for at in range(parts):
                for half, side in enumerate((core, 1 - core)):
                    rows = (self.inverse[side, every ^ at], every)
                    for kind, row in enumerate(rows):
                        self.table[core, at, 2 * kind + half, :parts] = row
                        self.table[core, at, 2 * kind + half, parts] = side

    def swap(self, value, *stages):
        pairs = []
        for core in range(2):
            flip = sum(1 << self.orders[core][stage] for stage in stages)
            pairs += [(2 * at + core, 2 * (at ^ flip) + core) for at in range(self.parts)]
        return lax.ppermute(value, ("dp", "tensor"), pairs)

    def sibling(self, value):
        return lax.ppermute(value, "tensor", [(0, 1), (1, 0)])

    def gather(self, share):
        return {"held": share[None], "stage": 0}

    def total(self, value):
        return {"value": value, "step": 0}

    def scatter(self, own, other):
        return {"pieces": [own], "other": other, "size": self.parts, "stage": self.stages}

    def advance(self, moves, rest=()):
        moves = [move for move in moves if self.running(move)]
        if not moves:
            return rest
        mine, rest, self.last = lax.optimization_barrier(
            ([move.get("held", move.get("value", move.get("pieces"))) for move in moves], rest, self.last)
        )
        sending = []
        for move, value in zip(moves, mine):
            if "held" in move:
                come = move.pop("come", None)
                sending.append(value if come is None else jnp.concatenate([value, come], axis=0))
            elif "value" in move:
                sending.append(self.summed(value, move.pop("come", [])))
            elif "other" in move:
                sending.append(move["other"])
            else:
                half, size = move["size"] // 2, move["size"]
                move["pieces"] = value + move.pop("come")
                sending.append(sum(piece[half:size].astype(f32) for piece in move["pieces"]).astype(bf16))
        sending, rest, _ = lax.optimization_barrier((sending, rest, self.last))
        self.last = sending[0]
        for move, value in zip(moves, sending):
            if "held" in move:
                move["held"] = value
                move["come"] = self.swap(value, move["stage"])
                move["stage"] += 1
            elif "value" in move:
                move["value"] = value
                low, high = 2 * move["step"] - 2, 2 * move["step"] - 1
                if move["step"] == 0:
                    move["come"] = [self.sibling(value)]
                elif high < self.stages:
                    move["come"] = [self.swap(value, low), self.swap(value, high), self.swap(value, low, high)]
                else:
                    move["come"] = [self.swap(value, low)]
                move["step"] += 1
            elif "other" in move:
                move["come"] = [self.sibling(value)]
                del move["other"]
            else:
                move["size"] //= 2
                move["stage"] -= 1
                move["come"] = [self.swap(value, move["stage"])]
        return rest

    def pair(self, move, rest=()):
        while self.running(move):
            self.advance([move])
        held, come = move.pop("held"), move.pop("come")
        if "swapped" not in move:
            move["swapped"] = self.sibling(held)
        held, come, rest = lax.optimization_barrier((held, come, rest))
        swapped = [move.pop("swapped"), self.sibling(come)]
        held = jnp.concatenate([held, come], axis=0)
        move["pair"] = (held, jnp.concatenate(swapped, axis=0), 0)
        return rest

    def swap_early(self, move, rest):
        value, rest, self.last = lax.optimization_barrier((move["held"], rest, self.last))
        move["swapped"] = self.sibling(value)
        return rest

    def summed(self, value, come):
        if len(come) == 3:
            return (value + come[0]) + (come[1] + come[2])
        return value + come[0] if come else value

    def running(self, move):
        return move.get("stage", 0) < self.stages if "held" in move else move.get("size", 1) > 1 or 2 * move.get("step", self.stages) < self.stages + 2

    def settle(self, moves, rest):
        pieces, rest = lax.optimization_barrier(([move["pieces"] for move in moves], rest))
        for move, value in zip(moves, pieces):
            move["pieces"] = value
        return lax.optimization_barrier((self.finish(moves), rest))

    def finish(self, moves):
        for move in moves:
            while self.running(move):
                self.advance([move])
        if "value" in moves[0]:
            return [self.summed(move["value"], move["come"]) for move in moves]
        return [sum(piece[0].astype(f32) for piece in move["pieces"] + move["come"]) for move in moves]


def dot_nt(left, right):
    return lax.dot_general(left, right, (((1,), (1,)), ((), ())), preferred_element_type=f32)


def dot_nn(left, right):
    return jnp.dot(left, right, preferred_element_type=f32)


def in_order(blocks, place_of):
    some = (0,) if len(blocks.shape) == 4 else ()
    return jnp.concatenate([blocks[(place_of[block], *some)] for block in range(blocks.shape[0])], axis=0)


def put_blocks(out, at, product, place_of):
    parts, _, rows, _ = out.shape
    for block in range(parts):
        out[place_of[block], at] = product[block * rows : (block + 1) * rows]


def norm_parts(values):
    centered = values - jnp.mean(values, axis=1, keepdims=True)
    variance = jnp.mean(centered * centered, axis=1, keepdims=True)
    scale = lax.rsqrt(variance + norm_eps)
    return centered * scale, scale


def norm_backward(values, gain, grad):
    unit, scale = norm_parts(values)
    scaled = grad * gain
    inner = scaled - jnp.mean(scaled, axis=1, keepdims=True)
    result = scale * (inner - unit * jnp.mean(scaled * unit, axis=1, keepdims=True))
    return result, jnp.sum(grad * unit, axis=0, keepdims=True), jnp.sum(grad, axis=0, keepdims=True)


def project_kernel(own_at, other_at, own_to, other_to, rows_in, own, other, bias, out):
    width = own.shape[-1]
    for half, (blocks, place_of) in enumerate(((own, own_at), (other, other_at))):
        weight = in_order(blocks, place_of)
        span = slice(half * width, (half + 1) * width)
        out[:, span] = (dot_nn(rows_in[...], weight) + bias[:, span]).astype(bf16)


def cost(microseconds):
    return pl.CostEstimate(flops=0, bytes_accessed=int(microseconds * 2.5e6), transcendentals=0)


class Row:
    def __init__(self, table, row):
        self.table, self.row = table, row

    def __getitem__(self, place):
        return self.table[self.row, place]


def call(kernel, places, grid, ins, outs, scratch=(), name=None, time=1):
    table, pair = places
    weight_rows = lambda at: (Row(at, 2 * pair), Row(at, 2 * pair + 1))
    spec = lambda block, index: pl.BlockSpec(block, lambda i, at: index(i, weight_rows(at)))
    return pl.pallas_call(
        lambda at, *refs: kernel(*weight_rows(at), Row(at, 0), Row(at, 1), *refs),
        out_shape=[jax.ShapeDtypeStruct(shape, kind) for shape, kind, _, _ in outs],
        grid_spec=pltpu.PrefetchScalarGridSpec(
            num_scalar_prefetch=1,
            grid=(grid,),
            in_specs=[spec(block, index) for _, block, index in ins],
            out_specs=[spec(block, index) for _, _, block, index in outs],
            scratch_shapes=list(scratch),
        ),
        compiler_params=pltpu.CompilerParams(
            dimension_semantics=("arbitrary",), vmem_limit_bytes=38 << 20
        ),
        cost_estimate=cost(time),
        name=name,
    )(table, *[array for array, _, _ in ins])


def whole(array):
    return (array, array.shape, lambda i, at: (0,) * array.ndim)


def weight_tiles(pair, tile, count=1):
    own, other, first = pair
    tiles = []
    for half, array in enumerate((own, other)):
        parts, rows = array.shape[0], array.shape[-2]
        column = lambda i: first // tile + jnp.clip(i, 0, count - 1)
        if array.ndim == 3:
            tiles.append((array, (parts, rows, tile), lambda i, at: (0, 0, column(i))))
        else:
            index = lambda i, at, half=half, parts=parts: (0, at[half][parts], 0, column(i))
            tiles.append((array, (parts, 1, rows, tile), index))
    return tiles


def project(places, rows_in, pair, bias):
    rows = rows_in.shape[0]
    half = D // 2
    return call(
        project_kernel, places, 3,
        [whole(rows_in), *weight_tiles(pair, half, 3), (bias, (1, D), lambda i, at: (0, i))],
        [((rows, 3 * D), bf16, (rows, D), lambda i, at: (0, i))],
        name="project",
        time=7,
    )[0]


def feed_forward_kernel(
    own_at, other_at, own_to, other_to, hidden, context, out_own, out_other, up_own, up_other, down_own, down_other,
    bias_up, vectors, *refs, with_grad,
):
    if with_grad:
        grad, first_in, first_turned, active, slope, hidden_new, *turned, first_low, second_in = refs
        total = second_in
    else:
        first_in, first_turned, active, slope, hidden_new, second_in, hidden_low, hidden_turned, first_low = refs
        total = second_in
    step = pl.program_id(0)
    halves = ((own_at, up_own, down_own), (other_at, up_other, down_other))
    half_d = D // 2

    @pl.when(step == 0)
    def _():
        attended = dot_nt(context[:, :half_d], in_order(out_own, own_at))
        attended += dot_nt(context[:, half_d:], in_order(out_other, other_at))
        values = hidden[...].astype(f32) + attended + vectors[0:1]
        first_in[...] = values
        unit, _ = norm_parts(values)
        values = unit * vectors[1:2] + vectors[2:3]
        low = values.astype(bf16)
        first_low[...] = low
        first_turned[...] = low.T
        total[...] = values + vectors[3:4]

    for half, (place_of, up, down) in enumerate(halves):
        before = dot_nn(first_low[...], in_order(up, place_of)) + bias_up[half]
        shade = 0.5 * (1.0 + lax.erf(before * (1.0 / math.sqrt(2.0))))
        bell = jnp.exp(-0.5 * before * before) * (1.0 / math.sqrt(2.0 * math.pi))
        low = (before * shade).astype(bf16)
        active[half] = low
        slope[half] = shade + before * bell
        total[...] += dot_nt(low, in_order(down, place_of))

    @pl.when(step == pl.num_programs(0) - 1)
    def _():
        unit, _ = norm_parts(second_in[...])
        values = unit * vectors[4:5] + vectors[5:6]
        hidden_new[...] = values
        if with_grad:
            norm_turn(second_in[...], vectors[4:5], grad[...], *turned)
        else:
            low = values.astype(bf16)
            hidden_low[...] = low
            hidden_turned[...] = low.T


def feed_forward(places, hidden, context, out_pair, up_pair, down_pair, bias_up, vectors, grad=None, tile=512):
    rows = hidden.shape[0]
    half_ff = bias_up.shape[2]
    count = half_ff // tile
    flat = lambda kind: ((rows, D), kind, (rows, D), lambda i, at: (0, 0))
    tiled = lambda kind: ((2, rows, half_ff), kind, (2, rows, tile), lambda i, at: (0, 0, i))
    turned = ((D, rows), bf16, (D, rows), lambda i, at: (0, 0))
    return call(
        partial(feed_forward_kernel, with_grad=grad is not None), places, count,
        [
            whole(hidden),
            whole(context),
            *weight_tiles(out_pair, D // 2),
            *weight_tiles(up_pair, tile, count),
            *weight_tiles(down_pair, tile, count),
            (bias_up, (2, 1, tile), lambda i, at: (0, 0, i)),
            whole(vectors),
            *([] if grad is None else [whole(grad)]),
        ],
        [
            flat(f32), turned, tiled(bf16), tiled(f32), flat(f32),
            *([flat(f32), flat(bf16), turned] if grad is None else norm_turn_outs(rows)),
        ],
        [pltpu.VMEM((rows, D), bf16)] + ([] if grad is None else [pltpu.VMEM((rows, D), f32)]),
        name="feed_forward",
        time=18,
    )


def norm_turn(values, gain, grad, total, down_low, down_turned, small):
    result, gain_grad, shift_grad = norm_backward(values, gain, grad)
    small[...] = jnp.zeros_like(small)
    small[0:1] = jnp.sum(result, axis=0, keepdims=True)
    small[1:2] = gain_grad
    small[2:3] = shift_grad
    total[...] = result
    low = result.astype(bf16)
    down_low[...] = low
    down_turned[...] = low.T


def norm_turn_outs(rows):
    flat = lambda kind: ((rows, D), kind, (rows, D), lambda i, at: (0, 0))
    turned = ((D, rows), bf16, (D, rows), lambda i, at: (0, 0))
    return [flat(f32), flat(bf16), turned, ((8, D), f32, (8, D), lambda i, at: (0, 0))]


def feed_backward_kernel(
    own_at, other_at, own_to, other_to, total_in, down_low, down_turned, first_turned, active, slope,
    up_own, up_other, down_own, down_other, grads_own, grads_other, bias_grads, total,
):
    halves = (
        (own_at, own_to, up_own, down_own, grads_own),
        (other_at, other_to, up_other, down_other, grads_other),
    )

    @pl.when(pl.program_id(0) == 0)
    def _():
        total[...] = total_in[...]

    for half, (place_of, place_to, up, down, grads) in enumerate(halves):
        act_grad = dot_nn(down_low[...], in_order(down, place_of))
        before_grad = act_grad * slope[half]
        bias_grads[half] = jnp.broadcast_to(jnp.sum(before_grad, axis=0, keepdims=True), bias_grads.shape[1:])
        low = before_grad.astype(bf16)
        put_blocks(grads, 0, dot_nn(down_turned[...], active[half]).astype(bf16), place_to)
        put_blocks(grads, 1, dot_nn(first_turned[...], low).astype(bf16), place_to)
        total[...] += dot_nt(low, in_order(up, place_of))


def context_backward_kernel(
    own_at, other_at, own_to, other_to, grad, first_in, out_own, out_other, vectors,
    first_in_grad, out_in_turned, context_grad, small,
):
    half_d = D // 2
    result, gain_grad, shift_grad = norm_backward(first_in[...], vectors[1:2], grad[...])
    small[...] = jnp.zeros_like(small)
    small[0:1] = jnp.sum(result, axis=0, keepdims=True)
    small[1:2] = gain_grad
    small[2:3] = shift_grad
    first_in_grad[...] = result
    low = result.astype(bf16)
    out_in_turned[...] = low.T
    context_grad[:, :half_d] = dot_nn(low, in_order(out_own, own_at)).astype(bf16)
    context_grad[:, half_d:] = dot_nn(low, in_order(out_other, other_at)).astype(bf16)


def context_backward(places, grad, first_in, out_pair, vectors):
    rows = grad.shape[0]
    flat = lambda kind: ((rows, D), kind, (rows, D), lambda i, at: (0, 0))
    return call(
        context_backward_kernel, places, 1,
        [
            whole(grad), whole(first_in),
            *weight_tiles(out_pair, D // 2),
            whole(vectors),
        ],
        [
            flat(f32), ((D, rows), bf16, (D, rows), lambda i, at: (0, 0)), flat(bf16),
            ((8, D), f32, (8, D), lambda i, at: (0, 0)),
        ],
        name="context_backward",
        time=6,
    )


def feed_backward(places, total, down_low, down_turned, kept, up_pair, down_pair, parts, tile=512):
    first_turned, active, slope = kept
    rows = total.shape[0]
    half_ff = active.shape[2]
    count = half_ff // tile
    block_rows = D // parts
    tiled = lambda array: (array, (2, rows, tile), lambda i, at: (0, 0, i))
    grads = ((parts, 2, block_rows, count * tile), bf16, (parts, 2, block_rows, tile), lambda i, at: (0, 0, 0, i))
    return call(
        feed_backward_kernel, places, count,
        [
            whole(total), whole(down_low), whole(down_turned), whole(first_turned), tiled(active), tiled(slope),
            *weight_tiles(up_pair, tile, count),
            *weight_tiles(down_pair, tile, count),
        ],
        [
            grads, grads,
            ((2, 8, count * tile), f32, (2, 8, tile), lambda i, at: (0, 0, i)),
            ((rows, D), f32, (rows, D), lambda i, at: (0, 0)),
        ],
        name="feed_backward",
        time=20,
    )


def projection_grads_kernel(
    own_at, other_at, own_to, other_to, out_in_turned, context, input_turned, head_grads,
    grads_own, grads_other,
):
    step = pl.program_id(0)
    half_d = D // 2
    halves = ((own_to, grads_own), (other_to, grads_other))
    for when, left, right in (
        (step == 0, out_in_turned, lambda span: context[:, span]),
        (step > 0, input_turned, lambda span: head_grads[0, :, span]),
    ):

        @pl.when(when)
        def _():
            for half, (place_to, grads) in enumerate(halves):
                span = slice(half * half_d, (half + 1) * half_d)
                put_blocks(grads, 0, dot_nn(left[...], right(span)).astype(bf16), place_to)


def projection_grads(places, out_in_turned, context, input_turned, head_grads, parts):
    rows = context.shape[0]
    half = D // 2
    block_rows = D // parts
    grads = ((parts, 4, block_rows, half), bf16, (parts, 1, block_rows, half), lambda i, at: (0, i, 0, 0))
    return call(
        projection_grads_kernel, places, 4,
        [
            whole(out_in_turned), whole(context), whole(input_turned),
            (head_grads, (1, rows, D), lambda i, at: (jnp.maximum(i - 1, 0), 0, 0)),
        ],
        [grads, grads],
        name="projection_grads",
        time=9,
    )


def project_backward_kernel(
    own_at, other_at, own_to, other_to, head_grads, first_in_grad, own, other, *refs, with_norm
):
    half_d = D // 2
    step = pl.program_id(0)
    if with_norm:
        second_in, vectors, *turned, input_grad = refs
    else:
        (input_grad,) = refs

    @pl.when(step == 0)
    def _():
        input_grad[...] = first_in_grad[...]

    for half, (place_of, weight) in enumerate(((own_at, own), (other_at, other))):
        low = head_grads[0, :, half * half_d : (half + 1) * half_d]
        input_grad[...] += dot_nt(low, in_order(weight, place_of))

    if with_norm:

        @pl.when(step == pl.num_programs(0) - 1)
        def _():
            norm_turn(second_in[...], vectors[4:5], input_grad[...], *turned)


def project_backward(places, head_grads, first_in_grad, pair, earlier=()):
    rows = first_in_grad.shape[0]
    half = D // 2
    return call(
        partial(project_backward_kernel, with_norm=bool(earlier)), places, 3,
        [
            (head_grads, (1, rows, D), lambda i, at: (i, 0, 0)),
            whole(first_in_grad),
            *weight_tiles(pair, half, 3),
            *map(whole, earlier),
        ],
        norm_turn_outs(rows) if earlier else [((rows, D), f32, (rows, D), lambda i, at: (0, 0))],
        [pltpu.VMEM((rows, D), f32)] if earlier else [],
        name="project_backward",
        time=8,
    )


def join_kernel(core, *refs):
    step = pl.program_id(0)
    count = len(refs) // 3
    for one in range(count):
        own, other, out = refs[2 * one], refs[2 * one + 1], refs[2 * count + one]

        @pl.when(step == core[0])
        def _():
            out[...] = own[...]

        @pl.when(step != core[0])
        def _():
            out[...] = other[...]


def join(core, pairs):
    rows, cols = pairs[0][0].shape
    spec = pl.BlockSpec((rows, cols), lambda i, at: (0, 0))
    return pl.pallas_call(
        join_kernel,
        out_shape=[jax.ShapeDtypeStruct((2 * rows, cols), f32) for _ in pairs],
        grid_spec=pltpu.PrefetchScalarGridSpec(
            num_scalar_prefetch=1,
            grid=(2,),
            in_specs=[spec] * (2 * len(pairs)),
            out_specs=[pl.BlockSpec((rows, cols), lambda i, at: (i, 0)) for _ in pairs],
        ),
        compiler_params=pltpu.CompilerParams(
            dimension_semantics=("arbitrary",), vmem_limit_bytes=38 << 20
        ),
        cost_estimate=cost(4),
        name="join",
    )(core, *[rows_of for pair in pairs for rows_of in pair])


bounds = [0, D, 2 * D, 2 * D + FF, 3 * D + FF, 4 * D + FF, 5 * D + FF, 6 * D + FF, 7 * D + FF]


def swapped(core, vector):
    half = vector.shape[1] // 2
    first, second = vector[:, :half], vector[:, half:]
    return jnp.where(core == 0, first, second), jnp.where(core == 0, second, first)


def prepare_kernel(core, lengths, tokens, cotangent, small, tokens_own, tokens_turned, grad, *outs):
    step = pl.program_id(0)
    length = lengths[core[0] * pl.num_programs(0) + step]
    tokens_own[...] = tokens[...]
    tokens_turned[...] = tokens[...].T
    valid = lax.broadcasted_iota(jnp.int32, grad.shape, 0) < length
    grad[...] = jnp.where(valid, cotangent[...].astype(f32), 0.0)

    @pl.when(step == 0)
    def _():
        for layer_at in range(small.shape[0]):
            vectors, value_bias, up_bias = outs[3 * layer_at : 3 * layer_at + 3]
            part = lambda place: small[layer_at : layer_at + 1, bounds[place] : bounds[place + 1]]
            vectors[...] = jnp.zeros_like(vectors)
            for row, place in enumerate((1, 4, 5, 3, 6, 7)):
                vectors[row : row + 1] = part(place)
            value_bias[...] = jnp.zeros_like(value_bias)
            first, second = swapped(core[0], part(0))
            value_bias[:, 2 * D : 2 * D + D // 2] = first
            value_bias[:, 2 * D + D // 2 :] = second
            up_bias[0], up_bias[1] = swapped(core[0], part(2))


def prepare(core, lengths, tokens, cotangent, small):
    layers = small.shape[0]
    seqs = lengths.shape[0] // 2
    rows = tokens.shape[0] // lengths.shape[0]
    mine = pl.BlockSpec((rows, D), lambda s, c, l: (c[0] * seqs + s, 0))
    fixed = lambda shape: pl.BlockSpec(shape, lambda s, c, l: (0,) * len(shape))
    shapes = [(8, D), (1, 3 * D), (2, 1, FF // 2)] * layers
    return pl.pallas_call(
        prepare_kernel,
        out_shape=[
            jax.ShapeDtypeStruct((seqs * rows, D), bf16),
            jax.ShapeDtypeStruct((D, seqs * rows), bf16),
            jax.ShapeDtypeStruct((seqs * rows, D), f32),
            *[jax.ShapeDtypeStruct(shape, f32) for shape in shapes],
        ],
        grid_spec=pltpu.PrefetchScalarGridSpec(
            num_scalar_prefetch=2,
            grid=(seqs,),
            in_specs=[mine, mine, fixed(small.shape)],
            out_specs=[
                pl.BlockSpec((rows, D), lambda s, c, l: (s, 0)),
                pl.BlockSpec((D, rows), lambda s, c, l: (0, s)),
                pl.BlockSpec((rows, D), lambda s, c, l: (s, 0)),
                *[fixed(shape) for shape in shapes],
            ],
        ),
        compiler_params=pltpu.CompilerParams(
            dimension_semantics=("arbitrary",), vmem_limit_bytes=50 << 20
        ),
        cost_estimate=cost(3),
        name="prepare",
    )(core, lengths, tokens, cotangent, small)


def pack_kernel(core, *refs, counts):
    out = refs[-1]
    squares = refs[-2]
    at = 0
    for layer_at, count in enumerate(counts):
        value_sum, first_small, second_small, *bias_sums = refs[at : at + 3 + count]
        at += 3 + count
        row = slice(layer_at, layer_at + 1)

        def put(place, values, start=0):
            first = bounds[place] + start
            out[row, first : first + values.shape[1]] = values

        total = value_sum[0, 0:1]
        for seq in range(1, value_sum.shape[0]):
            total = total + value_sum[seq, 0:1]
        for half, values in enumerate(swapped(core[0], total)):
            put(0, values, half * (D // 2))
        put(1, first_small[0:1])
        width = bias_sums[0].shape[2]
        for place, bias_sum in enumerate(bias_sums):
            own, other = bias_sum[0, 0:1], bias_sum[1, 0:1]
            put(2, jnp.where(core[0] == 0, own, other), place * width)
            put(2, jnp.where(core[0] == 0, other, own), FF // 2 + place * width)
        put(3, second_small[0:1])
        for place, values in ((4, first_small[1:2]), (5, first_small[2:3])):
            put(place, values)
        for place, values in ((6, second_small[1:2]), (7, second_small[2:3])):
            put(place, values)
        out[row, bounds[-1] :] = squares[row]


def pack(core, layers, squares):
    arrays = [array for value, first, second, sums in layers for array in (value, first, second, *sums)]
    arrays.append(squares)
    return pl.pallas_call(
        partial(pack_kernel, counts=[len(sums) for _, _, _, sums in layers]),
        out_shape=jax.ShapeDtypeStruct((len(layers), bounds[-1] + 128), f32),
        grid_spec=pltpu.PrefetchScalarGridSpec(
            num_scalar_prefetch=1,
            grid=(1,),
            in_specs=[pl.BlockSpec(array.shape, lambda i, c, n=array.ndim: (0,) * n) for array in arrays],
            out_specs=pl.BlockSpec((len(layers), bounds[-1] + 128), lambda i, c: (0, 0)),
        ),
        compiler_params=pltpu.CompilerParams(dimension_semantics=("arbitrary",)),
        cost_estimate=cost(2),
        name="pack",
    )(core, *arrays)


def head_mask(width, scale):
    lane = lax.broadcasted_iota(jnp.int32, (1, 128), 1)
    return [jnp.where(lane // 64 == head, scale, 0.0).astype(bf16) for head in range(2)]

def attend_forward_kernel(core, lengths, *refs, depth):
    queries, keys, value_rows = refs[:depth], refs[depth:2*depth], refs[2*depth]
    context, log_norm = refs[2*depth+1:]
    length = lengths[core[0] * pl.num_programs(0) + pl.program_id(0)]
    key_all = [k[...] for k in keys]
    key_all = jnp.concatenate(key_all, axis=1) if depth>1 else key_all[0]
    turned = value_rows[...].T
    rows = key_all.shape[0]
    valid = lax.broadcasted_iota(jnp.int32, (rows, rows), 0) < length
    scaled = head_mask(64, 0.125)
    halves = []
    for head in range(2):
        query = [q[...] * scaled[head] for q in queries]
        query = jnp.concatenate(query, axis=1) if depth>1 else query[0]
        score = jnp.where(valid, dot_nt(key_all, query), masked_score)
        top = jnp.max(score, axis=0, keepdims=True)
        weight = jnp.exp(score - top)
        total = jnp.sum(weight, axis=0, keepdims=True)
        low = (weight * (1.0 / total)).astype(bf16)
        halves.append(jnp.dot(turned[64*head:64*head+64], low, preferred_element_type=f32))
        log_norm[0, head:head+1] = top + jnp.log(total)
    context[...] = jnp.concatenate(halves, axis=0).T.astype(bf16)

def attend_forward(core, lengths, projections, rows):
    depth=len(projections)
    seqs = lengths.shape[0] // 2
    pairs=D//128
    col=lambda off: pl.BlockSpec((rows,128), lambda s,j,c,l,off=off:(s,off*pairs+j))
    return pl.pallas_call(
        partial(attend_forward_kernel, depth=depth),
        out_shape=[jax.ShapeDtypeStruct((seqs*rows,D),bf16), jax.ShapeDtypeStruct((seqs*pairs,8,rows),f32)],
        grid_spec=pltpu.PrefetchScalarGridSpec(num_scalar_prefetch=2, grid=(seqs,pairs),
            in_specs=[col(0)]*depth+[col(1)]*depth+[col(2)],
            out_specs=[pl.BlockSpec((rows,128),lambda s,j,c,l:(s,j)), pl.BlockSpec((1,8,rows),lambda s,j,c,l:(s*pairs+j,0,0))]),
        compiler_params=pltpu.CompilerParams(dimension_semantics=("arbitrary","arbitrary"),vmem_limit_bytes=50 << 20),
        cost_estimate=cost(10),
        name="attend_forward",
    )(core, lengths, *projections, *projections, projections[0])

def attend_backward_kernel(core, lengths, *refs, depth, with_later, keep_total):
    queries, keys, value_rows = refs[:depth], refs[depth:2*depth], refs[2*depth]
    log_norm, context_grad = refs[2*depth+1:2*depth+3]
    at = 2*depth+3
    if with_later:
        later = refs[at]; at+=1
    grads, value_sum = refs[at:at+2]
    if keep_total: total_out = refs[at+2]
    length = lengths[core[0] * pl.num_programs(0) + pl.program_id(0)]
    key_all = [k[...] for k in keys]
    key_all = jnp.concatenate(key_all, axis=1) if depth>1 else key_all[0]
    rows = key_all.shape[0]
    valid = lax.broadcasted_iota(jnp.int32, (rows, rows), 0) < length
    scaled = head_mask(64, 0.125)
    plain = head_mask(64, 1.0)
    key_turned = (keys[0][...] * 0.125).astype(bf16).T
    query_halves = []
    key_grad = value_grad = None
    for head in range(2):
        query = [q[...] * scaled[head] for q in queries]
        query_own = query[0]
        query = jnp.concatenate(query, axis=1) if depth>1 else query[0]
        score = jnp.where(valid, dot_nt(key_all, query), masked_score)
        soft = jnp.exp(score - log_norm[0, head:head+1])
        grad_rows = context_grad[...] * plain[head]
        soft_grad = dot_nt(value_rows[...], grad_rows)
        product = soft * soft_grad
        total = product - soft * jnp.sum(product, axis=0, keepdims=True)
        if with_later: total = total + later[head]
        if keep_total: total_out[head] = total
        low = total.astype(bf16)
        query_halves.append(jnp.dot(key_turned[64*head:64*head+64], low, preferred_element_type=f32))
        kg = jnp.dot(low, query_own, preferred_element_type=f32)
        vg = jnp.dot(soft.astype(bf16), grad_rows, preferred_element_type=f32)
        key_grad = kg if key_grad is None else key_grad+kg
        value_grad = vg if value_grad is None else value_grad+vg
    grads[0] = jnp.concatenate(query_halves, axis=0).T.astype(bf16)
    grads[1] = key_grad.astype(bf16)
    grads[2] = value_grad.astype(bf16)
    sums = jnp.sum(value_grad, axis=0, keepdims=True)
    value_sum[0] = jnp.broadcast_to(sums, (8,128))

def attend_backward(core, lengths, projections, log_norm, context_grad, later, keep_total, rows):
    depth=len(projections)
    seqs = lengths.shape[0] // 2
    pairs=D//128
    col=lambda off: pl.BlockSpec((rows,128), lambda s,j,c,l,off=off:(s,off*pairs+j))
    square=pl.BlockSpec((2,rows,rows),lambda s,j,c,l:(s*pairs+j,0,0))
    in_specs=[col(0)]*depth+[col(1)]*depth+[col(2)]+[pl.BlockSpec((1,8,rows),lambda s,j,c,l:(s*pairs+j,0,0)), col(0)]
    args=[*projections,*projections,projections[0],log_norm,context_grad]
    if later is not None:
        in_specs.append(square); args.append(later)
    out_shape=[jax.ShapeDtypeStruct((3,seqs*rows,D),bf16), jax.ShapeDtypeStruct((seqs,8,D),f32)]
    out_specs=[pl.BlockSpec((3,rows,128),lambda s,j,c,l:(0,s,j)), pl.BlockSpec((1,8,128),lambda s,j,c,l:(s,0,j))]
    if keep_total:
        out_shape.append(jax.ShapeDtypeStruct((seqs*pairs*2,rows,rows),f32)); out_specs.append(square)
    return pl.pallas_call(
        partial(attend_backward_kernel, depth=depth, with_later=later is not None, keep_total=keep_total),
        out_shape=out_shape,
        grid_spec=pltpu.PrefetchScalarGridSpec(num_scalar_prefetch=2, grid=(seqs,pairs), in_specs=in_specs, out_specs=out_specs),
        compiler_params=pltpu.CompilerParams(dimension_semantics=("arbitrary","arbitrary"),vmem_limit_bytes=50 << 20),
        cost_estimate=cost(17),
        name="attend_backward",
    )(core, lengths, *args)


def adam_parts(gradient, first, second, factor):
    clipped = gradient * factor
    first_new = beta_one * first + (1.0 - beta_one) * clipped
    second_new = beta_two * second + (1.0 - beta_two) * clipped * clipped
    first_hat = first_new / (1.0 - beta_one**step_count)
    second_hat = second_new / (1.0 - beta_two**step_count)
    return (first_new, second_new, first_hat / (jnp.sqrt(second_hat) + adam_eps))


def local(
    tokens,
    cotangent,
    lengths,
    proj_weight,
    out_weight,
    up_weight,
    down_weight,
    small_params,
    proj_first,
    proj_second,
    out_first,
    out_second,
    up_first,
    up_second,
    down_first,
    down_second,
    small_first,
    small_second,
):
    layers = proj_weight.shape[0]
    seq_len = tokens.shape[0] // lengths.shape[0]
    half_d = proj_weight.shape[3]
    half_ff = up_weight.shape[2]
    row_count = proj_weight.shape[1]
    parts = lax.axis_size("dp")
    links = Links(parts)
    places = lax.axis_index("tensor") * parts + lax.axis_index("dp")
    places = lax.dynamic_index_in_dim(
        jnp.asarray(links.table.reshape(2 * parts, 4, parts + 1)), places, 0, keepdims=False
    )
    exchanged, in_turn = (places, 0), (places, 1)
    turns = {(0, "proj"): exchanged, (0, "ff"): in_turn, (1, "proj"): in_turn, (1, "ff"): exchanged}
    core = lax.axis_index("tensor")[None].astype(jnp.int32)

    table = {"proj": proj_weight, "out": out_weight, "up": up_weight, "down": down_weight}
    groups = [
        [(0, "proj")], [(0, "up"), (0, "down"), (0, "out")], [(1, "proj")], [(1, "up"), (1, "down"), (1, "out")],
    ]
    gathers = []
    for group in groups:
        share = [table[kind][layer_at].reshape(row_count, -1).astype(bf16) for layer_at, kind in group]
        gathers.append(links.gather(jnp.concatenate(share, axis=1) if len(share) > 1 else share[0]))
    one, two, three, four = gathers
    last = jnp.concatenate([move.pop("held")[0] for move in (two, three)], axis=1)
    last = lax.all_gather(last, ("dp", "tensor")).reshape(parts, 2, row_count, -1)
    two["pair"], three["pair"] = (last, last, 0), (last, last, half_d + 2 * half_ff)
    links.advance([one])
    prepared = links.advance([one], prepare(core, lengths, tokens, cotangent, small_params))
    hidden, hidden_turned, grad_rows, *prepared = prepared
    vectors, value_bias, up_bias = prepared[0::3], prepared[1::3], prepared[2::3]
    links.advance([one])
    links.advance([one])
    if not links.running(one):
        (hidden,) = links.swap_early(one, (hidden,))
    (hidden,) = links.advance([four], (hidden,))

    def gathered(layer_at, kind):
        for group, move in zip(groups, gathers):
            widths = [math.prod(table[name].shape[2:]) for _, name in group]
            if (layer_at, kind) in group:
                while links.running(move):
                    links.advance([move])
                if "held" in move:
                    links.pair(move)
                own, other, first = move["pair"]
                return own, other, first + sum(widths[: group.index((layer_at, kind))])

    saved = []
    hidden_low = hidden
    masters = (proj_weight, out_weight, up_weight, down_weight)
    for layer_at in range(layers):
        projected = project(
            turns[layer_at, "proj"], hidden_low, gathered(layer_at, "proj"), value_bias[layer_at]
        )
        if layer_at == 0:
            (projected,) = links.advance([four], (projected,))
        chain = [projected] + [earlier["projected"] for earlier in reversed(saved)]
        context, log_norm = attend_forward(core, lengths, chain, seq_len)
        if layer_at > 0:
            (context,) = links.pair(four, (context,))
        if layer_at == 0:
            late_masters, context = lax.optimization_barrier((masters, context))
            squares = [jnp.sum(one * one, axis=tuple(range(1, one.ndim))) for one in late_masters]
            squares = jnp.pad(jnp.stack(squares, axis=1), ((0, 0), (0, 124)))
            squares, context = links.advance([four], (squares, context))
            (context,) = links.advance([four], (context,))
            if not links.running(four):
                (context,) = links.swap_early(four, (context,))
        kept = {
            "input_turned": hidden_turned, "projected": projected, "log_norm": log_norm, "context": context,
        }
        (
            kept["first_in"], kept["first_turned"], kept["active"], kept["slope"], hidden, *rest,
        ) = feed_forward(
            turns[layer_at, "ff"], hidden, context, gathered(layer_at, "out"), gathered(layer_at, "up"),
            gathered(layer_at, "down"), up_bias[layer_at], vectors[layer_at],
            grad_rows if layer_at == layers - 1 else None,
        )
        if layer_at == layers - 1:
            turned_grad = rest
        else:
            kept["second_in"], hidden_low, hidden_turned = rest
        saved.append(kept)

    smalls = [None] * layers
    later_total = None
    before = []
    for layer_at in reversed(range(layers)):
        kept = saved[layer_at]
        places_ff = turns[layer_at, "ff"]
        first_grad, down_low, down_turned, second_small = turned_grad
        own, other, bias_sum, first_grad = feed_backward(
            places_ff, first_grad, down_low, down_turned,
            [kept[name] for name in ("first_turned", "active", "slope")],
            gathered(layer_at, "up"), gathered(layer_at, "down"), parts,
        )
        ff_sum = links.scatter(own, other)
        (first_grad,) = links.advance(before + [ff_sum], (first_grad,))
        first_in_grad, out_in_turned, context_grad, first_small = context_backward(
            places_ff, first_grad, kept["first_in"], gathered(layer_at, "out"), vectors[layer_at]
        )
        (context_grad,) = links.advance([ff_sum] + before[1:], (context_grad,))
        chain = [kept["projected"]] + [earlier["projected"] for earlier in reversed(saved[:layer_at])]
        results = attend_backward(
            core, lengths, chain, kept["log_norm"], context_grad, later_total, layer_at > 0, seq_len
        )
        head_grads, value_sum = results[:2]
        later_total = results[2] if layer_at > 0 else None
        smalls[layer_at] = (value_sum, first_small, second_small, [bias_sum])
        if layer_at == 0:
            (head_grads,) = links.advance(before, (head_grads,))
            packed = pack(core, smalls, squares)
            packed, head_grads = links.advance([ff_sum], (packed, head_grads))
            packed = links.total(packed)
        attention_sum = links.scatter(
            *projection_grads(
                exchanged, out_in_turned, kept["context"], kept["input_turned"], head_grads, parts
            )
        )
        if layer_at > 0:
            (head_grads,) = links.advance([ff_sum, attention_sum], (head_grads,))
            turned_grad = project_backward(
                turns[layer_at, "proj"], head_grads, first_in_grad, gathered(layer_at, "proj"),
                (saved[layer_at - 1]["second_in"], vectors[layer_at - 1]),
            )
            turned_grad = links.advance([attention_sum], turned_grad)
        else:
            links.advance([attention_sum, packed])
            (head_grads,) = links.advance([attention_sum, before[1]], (head_grads,))
            (grad_rows,) = project_backward(
                turns[layer_at, "proj"], head_grads, first_in_grad, gathered(layer_at, "proj")
            )
        before += [ff_sum, attention_sum]

    width = small_params.shape[1]
    (grad_rows,) = links.advance([ff_sum, attention_sum], (grad_rows,))
    later_sums, grad_rows = links.settle(before[:2], grad_rows)
    sent = (links.sibling(grad_rows), links.sibling(hidden))
    links.advance([packed])
    links.advance([attention_sum])
    links.advance([ff_sum])
    hidden, grad_rows = join(core, ((hidden, sent[1]), (grad_rows, sent[0])))
    hidden, grad_rows = links.advance([packed], (hidden, grad_rows))
    links.advance([attention_sum])
    packed = links.finish([packed])[0]
    small_grad = packed[:, :width]
    weight_square = packed[:, width : width + 4].T

    ff_sums, attention_sums = (
        jnp.stack([earlier, later]) for earlier, later in zip(links.finish([ff_sum, attention_sum]), later_sums)
    )
    grads = (
        attention_sums[:, 1:].transpose(0, 2, 1, 3), attention_sums[:, 0], ff_sums[:, 1], ff_sums[:, 0],
    )
    firsts = (proj_first, out_first, up_first, down_first)
    seconds = (proj_second, out_second, up_second, down_second)
    square_part = sum(jnp.sum(grad * grad) for grad in grads)
    square_big = links.finish([links.total(jnp.broadcast_to(square_part, (8, 128)))])[0][0, 0]
    grad_norm = jnp.sqrt(square_big + jnp.sum(small_grad * small_grad))
    factor = clip_norm / jnp.maximum(grad_norm, clip_norm)
    moments = []
    updates = []
    for kind_at in range(4):
        first_new, second_new, direction = adam_parts(
            grads[kind_at], firsts[kind_at], seconds[kind_at], factor
        )
        moments.append((first_new, second_new))
        updates.append(direction + decay_rate * masters[kind_at])
    update_square = jnp.stack(
        [jnp.sum(update * update, axis=tuple(range(1, update.ndim))) for update in updates]
    )
    update_square = jnp.pad(update_square.reshape(1, -1), ((0, 7), (0, 128 - 4 * layers)))
    update_square = links.finish([links.total(update_square)])[0]
    update_square = update_square[0, : 4 * layers].reshape(4, layers)
    ratio = jnp.sqrt(weight_square) / jnp.sqrt(update_square)

    outputs = [hidden, grad_rows, grad_norm]
    for kind_at in range(4):
        master = masters[kind_at]
        scaled = ratio[kind_at].reshape((-1,) + (1,) * (master.ndim - 1))
        outputs += [
            moments[kind_at][0],
            moments[kind_at][1],
            master - matrix_rate * scaled * updates[kind_at],
        ]
    small_first_new, small_second_new, small_direction = adam_parts(
        small_grad, small_first, small_second, factor
    )
    outputs += [small_first_new, small_second_new, small_params - vector_rate * small_direction]
    return tuple(outputs)


def solution(mesh):
    proj = P(None, "dp", None, "tensor")
    matrix = P(None, "dp", "tensor")
    rows = P("dp", None)
    return jax.shard_map(
        local,
        mesh=mesh,
        in_specs=(rows, rows, P("dp"), proj, matrix, matrix, matrix, P())
        + (proj, proj)
        + (matrix,) * 6
        + (P(), P()),
        out_specs=(rows, rows, P()) + (proj,) * 3 + (matrix,) * 9 + (P(),) * 3,
        check_vma=False,
    )
```
